32 devices in a mesh: groups: 2 (over x), dp: 2 (over core), tensor: 8 (over z, y).
Axes of the slice: x: 2, y: 2, z: 4, core: 2. Of those that a mesh axis runs over, the one named last changes fastest.
Arguments:
- hidden: bfloat16 [4, 1024, 8192], P(('groups', 'dp'), 'tensor'), parts along dimension 0, may hold values from -24 to 24
- query_weight: bfloat16 [8192, 4096], P(None, 'tensor'), may hold values from -0.0625 to 0.0625
- key_weight: bfloat16 [8, 4096, 128], P('tensor'), may hold values from -0.0625 to 0.0625
- value_weight: bfloat16 [8, 4096, 128], P('tensor'), may hold values from -0.0625 to 0.0625
- head_grad: bfloat16 [4, 1024, 4096], P(('groups', 'dp'), None, 'tensor'), parts along dimension 0, may hold values from -6 to 6
- lengths: int32 [4], P(('groups', 'dp')), parts along dimension 0, may hold values from 256 to 1024, as said below
Outputs:
- fisher_key: float32 [16, 4096, 128], P(('groups', 'tensor'), 'dp'), parts along dimension 0
- fisher_value: float32 [16, 4096, 128], P(('groups', 'tensor'), 'dp'), parts along dimension 0
The draws below stay inside these ranges and needn't reach their ends.
There are 2 independent parts, one for each index of `groups`. The reference program is written for one: setup_inputs(seed, part) draws one part's arguments, and reference() takes and returns one part's arrays. A program takes and returns all parts, laid end to end along the dimension named above; an argument that names none is the same for every part. Nothing has to cross between parts.
Inputs may be any that keep to these rules, and one draw needn't show every extreme that they name: `lengths`: some sequence of each part has length 1024.
All inputs are finite; a program needn't handle non-finite values.
Results may differ from the reference program's by a relative error of at most 0.013.
The reference program's roundings to bfloat16 on the way count: a program that leaves them out, or rounds other values in their place, can miss the bound.
Values may be sent and summed in bfloat16 or wider, within the bound.
A program may use at most 256 MiB of HBM per device.

```python
import math
import jax
import jax.numpy as jnp
from jax import lax

D = 8192
HD = 128
QH = 32
KVH = 4
SEQ_LEN = 1024
NSEQ = 2


def draw_hidden(key, part):
    base_key = jax.random.fold_in(jax.random.fold_in(key, 11), 0)
    values = jax.random.normal(base_key, (NSEQ, SEQ_LEN, D), jnp.float32)
    return jnp.clip(values, -24.0, 24.0).astype(jnp.bfloat16)


def draw_lengths(key, part):
    value_key, pick_key = jax.random.split(jax.random.fold_in(key, 23))
    drawn = jax.random.randint(value_key, (NSEQ,), SEQ_LEN // 4, SEQ_LEN + 1)
    chosen = jax.random.randint(pick_key, (), 0, NSEQ)
    return jnp.where(jnp.arange(NSEQ) == chosen, SEQ_LEN, drawn).astype(jnp.int32)


def shard_levels(rng, extent, cuts, least, top_value):
    factor_of, own = 1.0, jax.random.fold_in(rng, 6)
    for dim, shards_of in cuts:
        steps = jnp.exp(jax.random.uniform(jax.random.fold_in(own, dim), (shards_of,), jnp.float32, least / len(cuts), top_value / len(cuts)))
        factor_of = factor_of * jnp.repeat(steps, extent[dim] // shards_of).reshape([-1 if axis == dim else 1 for axis in range(len(extent))])
    return factor_of


def gaussian(own_key, dims, scale, most, shards=(), kind=jnp.bfloat16):
    array = jax.random.normal(own_key, dims, jnp.float32) * scale
    if len(shards) > 0:
        array = shard_levels(own_key, dims, shards, -0.22, 0.18) * array
    return jnp.clip(array, min=-most, max=most).astype(kind)


def setup_inputs(seed: int = 0, part: int = 0) -> dict:
    splits = jax.random.split(jax.random.key(seed), 7)
    own_keys = jax.random.split(jax.random.fold_in(splits[6], part), 7)
    return {
        "hidden": draw_hidden(jax.random.fold_in(jax.random.fold_in(splits[6], part), 71), part),
        "query_weight": gaussian(splits[1], (D, QH * HD), D ** -0.5, 0.0625, ((1, 8),)),
        "key_weight": gaussian(splits[2], (2 * KVH, D // 2, HD), D ** -0.5, 0.0625, ((0, 8),)),
        "value_weight": gaussian(splits[3], (2 * KVH, D // 2, HD), D ** -0.5, 0.0625, ((0, 8),)),
        "head_grad": gaussian(own_keys[4], (NSEQ, SEQ_LEN, QH * HD), 1.0, 6.0, ((0, 2), (2, 8))),
        "lengths": draw_lengths(jax.random.fold_in(jax.random.fold_in(splits[6], part), 71), part),
    }


rope_base = 1000000.0
far_below = -1e+30

def angle_table(length, head_width):
    position = jnp.arange(length, dtype=jnp.float32)[:, None]
    frequency = rope_base ** (-2.0 * jnp.arange(head_width // 2, dtype=jnp.float32) / head_width)
    return (position * frequency)[:, None, :]

def rotate(vectors, angles):
    half_dim = vectors.shape[-1] // 2
    lead_half = vectors[..., :half_dim]
    tail_half = vectors[..., half_dim:]
    cosine = jnp.cos(angles)
    sines = jnp.sin(angles)
    return jnp.concatenate([lead_half * cosine - tail_half * sines, tail_half * cosine + lead_half * sines], axis=-1)

def unrotate(vectors, angles):
    half_dim = vectors.shape[-1] // 2
    lead_half = vectors[..., :half_dim]
    tail_half = vectors[..., half_dim:]
    cosine = jnp.cos(angles)
    sines = jnp.sin(angles)
    return jnp.concatenate([lead_half * cosine + tail_half * sines, tail_half * cosine - lead_half * sines], axis=-1)

def full_rows(weight):
    return weight.reshape(KVH, 2, D // 2, HD).transpose(1, 2, 0, 3).reshape(D, KVH * HD)

def split_rows(matrix):
    return matrix.reshape(2, D // 2, KVH, HD).transpose(2, 0, 1, 3).reshape(2 * KVH, D // 2, HD)

def reference(hidden, query_weight, key_weight, value_weight, head_grad, lengths):
    score_scale = 1.0 / math.sqrt(HD)
    group_size = QH // KVH
    angles = angle_table(SEQ_LEN, HD)
    key_full = full_rows(key_weight)
    value_full = full_rows(value_weight)
    positions = jnp.arange(SEQ_LEN, dtype=jnp.int32)
    causal_ok = positions[:, None] >= positions[None, :]
    fisher_key = jnp.zeros((D, KVH * HD), jnp.float32)
    fisher_value = jnp.zeros((D, KVH * HD), jnp.float32)
    for seq_idx in range(NSEQ):
        seq_rows = hidden[seq_idx]
        queries = rotate(jnp.dot(seq_rows, query_weight, preferred_element_type=jnp.float32).reshape(SEQ_LEN, QH, HD), angles).astype(jnp.bfloat16)
        keys = rotate(jnp.dot(seq_rows, key_full, preferred_element_type=jnp.float32).reshape(SEQ_LEN, KVH, HD), angles).astype(jnp.bfloat16)
        values = jnp.dot(seq_rows, value_full, preferred_element_type=jnp.float32).astype(jnp.bfloat16).reshape(SEQ_LEN, KVH, HD)
        live_rows = (positions < lengths[seq_idx])[:, None]
        upstream = jnp.where(live_rows, head_grad[seq_idx], jnp.zeros_like(head_grad[seq_idx])).reshape(SEQ_LEN, QH, HD)
        query_groups = queries.reshape(SEQ_LEN, KVH, group_size, HD).transpose(1, 2, 0, 3)
        up_groups = upstream.reshape(SEQ_LEN, KVH, group_size, HD).transpose(1, 2, 0, 3)

        def one_group(operands):
            group_queries, group_up, head_keys, head_values = operands
            key_acc = jnp.zeros((SEQ_LEN, HD), jnp.float32)
            value_acc = jnp.zeros((SEQ_LEN, HD), jnp.float32)
            for member in range(group_size):
                query_head = group_queries[member]
                up_head = group_up[member]
                scores = jnp.dot(query_head, head_keys.T, preferred_element_type=jnp.float32) * score_scale
                scores = jnp.where(causal_ok, scores, far_below)
                exp_scores = jnp.exp(scores - lax.optimization_barrier(jnp.max(scores, axis=-1, keepdims=True)))
                prob_rows = exp_scores / lax.optimization_barrier(jnp.sum(exp_scores, axis=-1, keepdims=True))
                dprob = jnp.dot(up_head, head_values.T, preferred_element_type=jnp.float32)
                row_dot = lax.optimization_barrier(jnp.sum(prob_rows * dprob, axis=-1, keepdims=True))
                dscore = (prob_rows * (dprob - row_dot) * score_scale).astype(jnp.bfloat16)
                key_acc = key_acc + jnp.dot(dscore.T, query_head, preferred_element_type=jnp.float32)
                value_acc = value_acc + jnp.dot(prob_rows.astype(jnp.bfloat16).T, up_head, preferred_element_type=jnp.float32)
            return (key_acc, value_acc)
        key_rot, value_acc = lax.map(one_group, (query_groups, up_groups, keys.transpose(1, 0, 2), values.transpose(1, 0, 2)))
        key_gradient = unrotate(key_rot.transpose(1, 0, 2), angles).astype(jnp.bfloat16).reshape(SEQ_LEN, KVH * HD)
        value_grad = value_acc.transpose(1, 0, 2).astype(jnp.bfloat16).reshape(SEQ_LEN, KVH * HD)
        key_sample = jnp.dot(seq_rows.T, key_gradient, preferred_element_type=jnp.float32)
        value_sample = jnp.dot(seq_rows.T, value_grad, preferred_element_type=jnp.float32)
        fisher_key = fisher_key + key_sample * key_sample
        fisher_value = fisher_value + value_sample * value_sample
    return (split_rows(fisher_key), split_rows(fisher_value))
```

```python
import functools
import math

import jax
import jax.numpy as jnp
import numpy as np
from jax import lax
from jax.experimental import pallas as pl
from jax.experimental.pallas import tpu as pltpu
from jax.sharding import PartitionSpec as P

MESH = pl.DeviceIdType.MESH

rope_base = 1000000.0
far_below = -1e30


def turn_table(length, head_width):
    position = np.arange(length, dtype=np.float64)[:, None]
    frequency = rope_base ** (-2.0 * np.arange(head_width // 2, dtype=np.float64) / head_width)
    angles = position * frequency
    return np.concatenate([np.cos(angles), np.sin(angles)], axis=-1).astype(np.float32)


def swap_halves(vectors):
    return pltpu.roll(vectors, vectors.shape[-1] // 2, axis=1)


def cosine_sine(table):
    other = swap_halves(table)
    lead = lax.broadcasted_iota(jnp.int32, table.shape, 1) < table.shape[1] // 2
    return jnp.where(lead, table, other), jnp.where(lead, -other, table)


def gather_project_kernel(
    count, dp_count, lengths_ref, gradient_ref, table_ref,
    hidden_ref, query_ref, key_ref, value_ref,
    rows_out, queries_out, pairs_out, upstream_out,
    held, weights, partial, other, queries, pairs, upstream,
    rows_recv, up_send, down_send, mate_send, load_sem, weight_send, weight_recv,
    share_send, share_recv, partial_send, partial_recv, rows_store, queries_store, pairs_store,
    upstream_store,
):
    me = lax.axis_index("tensor")
    core = lax.axis_index("dp")
    side = lax.rem(me, 2)
    place = lax.div(me, 2)
    mate = me + 1 - 2 * side
    chain = count // 2
    half = held.shape[2]
    query_cols = query_ref.shape[1]
    head_width = key_ref.shape[1]
    own_cols = query_cols + 2 * head_width
    has_up = place < chain - 1
    has_down = place > 0
    share = half // dp_count

    barrier = pltpu.get_barrier_semaphore()
    pl.semaphore_signal(barrier, inc=1, device_id={"tensor": mate}, device_id_type=MESH)
    for step in range(1, dp_count):
        peer = lax.rem(core + step, dp_count)
        pl.semaphore_signal(barrier, inc=1, device_id={"dp": peer}, device_id_type=MESH)

    @pl.when(has_up)
    def _():
        pl.semaphore_signal(barrier, inc=1, device_id={"tensor": me + 2}, device_id_type=MESH)

    @pl.when(has_down)
    def _():
        pl.semaphore_signal(barrier, inc=1, device_id={"tensor": me - 2}, device_id_type=MESH)

    edges = jnp.where(has_up, 1, 0) + jnp.where(has_down, 1, 0)
    pl.semaphore_wait(barrier, dp_count + edges)

    own_half = hidden_ref.at[:, pl.ds(pl.multiple_of(side * half, half), half)]
    mate_half = hidden_ref.at[:, pl.ds(pl.multiple_of((1 - side) * half, half), half)]

    def up_copy(slot, source):
        return pltpu.make_async_remote_copy(
            src_ref=source, dst_ref=held.at[slot], send_sem=up_send.at[slot],
            recv_sem=rows_recv.at[slot], device_id={"tensor": me + 2}, device_id_type=MESH)

    def down_copy(slot, source):
        return pltpu.make_async_remote_copy(
            src_ref=source, dst_ref=held.at[slot], send_sem=down_send.at[slot],
            recv_sem=rows_recv.at[slot], device_id={"tensor": me - 2}, device_id_type=MESH)

    def wait_rows(slot):
        pltpu.make_async_remote_copy(
            src_ref=held.at[slot], dst_ref=held.at[slot], send_sem=mate_send,
            recv_sem=rows_recv.at[slot], device_id={"tensor": mate}, device_id_type=MESH).wait_recv()

    def store_rows(slot):
        return pltpu.make_async_copy(held.at[slot], rows_out.at[slot], rows_store.at[slot])

    def store_queries(slot):
        return pltpu.make_async_copy(queries.at[slot], queries_out.at[slot], queries_store.at[slot])

    def store_pairs(slot):
        return pltpu.make_async_copy(pairs.at[slot], pairs_out.at[slot], pairs_store.at[slot])

    tile = 256
    pieces = own_cols // tile

    def partial_copy(slot, piece):
        source = pl.ds(pl.multiple_of(query_cols + piece * tile, tile), tile)
        target = pl.ds(pl.multiple_of(piece * tile, tile), tile)
        return pltpu.make_async_remote_copy(
            src_ref=partial.at[slot, :, source], dst_ref=other.at[slot, :, target],
            send_sem=partial_send.at[slot, piece], recv_sem=partial_recv.at[slot, piece],
            device_id={"tensor": mate}, device_id_type=MESH)

    to_mate = pltpu.make_async_remote_copy(
        src_ref=mate_half, dst_ref=held.at[me], send_sem=mate_send,
        recv_sem=rows_recv.at[me], device_id={"tensor": mate}, device_id_type=MESH)
    to_mate.start()

    @pl.when(has_up)
    def _():
        up_copy(me, own_half).start()

    @pl.when(has_down)
    def _():
        down_copy(me, own_half).start()

    half_rows = pl.ds(pl.multiple_of(side * half, half), half)
    loads = [
        pltpu.make_async_copy(own_half, held.at[me], load_sem.at[0]),
        pltpu.make_async_copy(
            query_ref.at[half_rows], weights.at[:, pl.ds(0, query_cols)], load_sem.at[1]),
        pltpu.make_async_copy(
            key_ref, weights.at[:, pl.ds(query_cols, head_width)], load_sem.at[2]),
        pltpu.make_async_copy(
            value_ref, weights.at[:, pl.ds(query_cols + head_width, head_width)], load_sem.at[3]),
    ]
    for load in loads:
        load.start()

    share_rows = pl.ds(pl.multiple_of(core * share, share), share)
    mate_cols = pl.ds(own_cols, query_cols)
    weight_copy = pltpu.make_async_remote_copy(
        src_ref=query_ref.at[pl.ds(pl.multiple_of((1 - side) * half + core * share, share), share)],
        dst_ref=weights.at[share_rows, mate_cols], send_sem=weight_send, recv_sem=weight_recv,
        device_id={"tensor": mate}, device_id_type=MESH)

    live = lengths_ref[0]
    rows = held.shape[1]
    heads = query_cols // head_width

    @pl.loop(0, count)
    def _(slot):
        here = pl.ds(pl.multiple_of(slot * rows, rows), rows)
        position = slot * rows + lax.broadcasted_iota(jnp.int32, (rows, head_width), 0)
        for head in range(heads):
            gradient = gradient_ref[here, head * head_width:(head + 1) * head_width]
            upstream[slot, head * rows:(head + 1) * rows, :] = jnp.where(
                position < live, gradient.astype(jnp.float32), 0.0).astype(jnp.bfloat16)

    store_upstream = pltpu.make_async_copy(upstream, upstream_out, upstream_store)
    store_upstream.start()
    wait_rows(mate)

    @pl.when(has_up)
    def _():
        up_copy(mate, held.at[mate]).start()

    @pl.when(has_down)
    def _():
        down_copy(mate, held.at[mate]).start()

    weight_copy.start()

    def slot_at(step, which):
        return 2 * step + jnp.where(which == 0, side, 1 - side)

    def receive(distance, which):
        below = place - distance
        above = place + distance

        @pl.when(below >= 0)
        def _():
            slot = slot_at(below, which)
            wait_rows(slot)

            @pl.when(has_up)
            def _():
                up_copy(slot, held.at[slot]).start()

        @pl.when(above < chain)
        def _():
            slot = slot_at(above, which)
            wait_rows(slot)

            @pl.when(has_down)
            def _():
                down_copy(slot, held.at[slot]).start()

    def multiply(slot, start):
        columns = pl.ds(pl.multiple_of(start, tile), tile)
        partial[slot, :, columns] = jnp.dot(
            held[slot], weights[:, columns], preferred_element_type=jnp.float32)

    def project_pair(slot):
        store_rows(slot).start()
        multiply(slot, query_cols)

    def send_pair(slot):
        partial_copy(slot, 0).start()

    def project_queries(slot):
        @pl.loop(1, pieces)
        def _(piece):
            multiply(slot, query_cols + piece * tile)
            partial_copy(slot, piece).start()

        @pl.loop(0, query_cols // tile)
        def _(piece):
            multiply(slot, piece * tile)

    def project(slot):
        project_pair(slot)
        send_pair(slot)
        project_queries(slot)

    def project_at(distance, which, action):
        below = place - distance
        above = place + distance

        @pl.when(below >= 0)
        def _():
            action(slot_at(below, which))

        @pl.when(above < chain)
        def _():
            action(slot_at(above, which))

    receive(1, 0)
    receive(1, 1)
    for load in loads:
        load.wait()

    def early(action):
        @pl.loop(0, 2)
        def _(which):
            action(slot_at(place, which))

        @pl.loop(0, 2)
        def _(which):
            project_at(1, which, action)

    early(project_pair)
    weight_copy.wait_recv()
    shares = []
    for step in range(1, dp_count):
        peer = lax.rem(core + step, dp_count)
        shares.append(pltpu.make_async_remote_copy(
            src_ref=weights.at[share_rows, mate_cols], dst_ref=weights.at[share_rows, mate_cols],
            send_sem=share_send.at[step - 1], recv_sem=share_recv.at[step - 1],
            device_id={"dp": peer}, device_id_type=MESH))
    for copy in shares:
        copy.start()
    early(send_pair)
    for copy in shares:
        copy.wait_recv()
    early(project_queries)

    @pl.loop(4, 2 * chain)
    def _(step):
        distance = lax.div(step, 2)
        which = lax.rem(step, 2)
        receive(distance, which)
        project_at(distance, which, project)

    def finish(slot):
        for piece in range(pieces):
            partial_copy(slot, piece).wait_recv()
        cosine, sine = cosine_sine(table_ref[pl.ds(pl.multiple_of(slot * rows, rows), rows), :])

        def turn(mixed):
            return (mixed * cosine + swap_halves(mixed) * sine).astype(jnp.bfloat16)

        for head in range(heads):
            columns = slice(head * head_width, (head + 1) * head_width)
            shifted = slice((head + 2) * head_width, (head + 3) * head_width)
            queries[slot, head * rows:(head + 1) * rows, :] = turn(
                partial[slot, :, columns] + other[slot, :, shifted])
        pairs[slot, :, :head_width] = turn(
            partial[slot, :, query_cols:query_cols + head_width] + other[slot, :, :head_width])
        pairs[slot, :, head_width:] = (
            partial[slot, :, query_cols + head_width:own_cols]
            + other[slot, :, head_width:2 * head_width]
        ).astype(jnp.bfloat16)
        store_queries(slot).start()
        store_pairs(slot).start()

    @pl.loop(0, 2 * chain)
    def _(step):
        distance = lax.div(step, 2)
        which = lax.rem(step, 2)
        below = place - distance
        above = place + distance

        @pl.when(below >= 0)
        def _():
            finish(slot_at(below, which))

        @pl.when((above < chain) & (distance > 0))
        def _():
            finish(slot_at(above, which))

    store_upstream.wait()
    to_mate.wait_send()
    weight_copy.wait_send()
    for copy in shares:
        copy.wait_send()

    @pl.loop(0, count)
    def _(slot):
        for piece in range(pieces):
            partial_copy(slot, piece).wait_send()
        store_rows(slot).wait()
        store_queries(slot).wait()
        store_pairs(slot).wait()
        origin = lax.div(slot, 2)

        @pl.when(has_up & (origin <= place))
        def _():
            up_copy(slot, held.at[slot]).wait_send()

        @pl.when(has_down & (origin >= place))
        def _():
            down_copy(slot, held.at[slot]).wait_send()


def gather_project(lengths, head_grad, table, hidden, query_weight, key_weight, value_weight):
    count = lax.axis_size("tensor")
    dp_count = lax.axis_size("dp")
    rows, model_width = hidden.shape
    half = model_width // 2
    query_cols = query_weight.shape[1]
    head_width = key_weight.shape[1]
    own_cols = query_cols + 2 * head_width
    all_cols = own_cols + query_cols
    heads = query_cols // head_width
    stack_shape = jax.ShapeDtypeStruct((count, heads * rows, head_width), jnp.bfloat16)
    pair_shape = jax.ShapeDtypeStruct((count, rows, 2 * head_width), jnp.bfloat16)
    dma = pltpu.SemaphoreType.DMA
    anywhere = pl.BlockSpec(memory_space=pl.ANY)
    return pl.pallas_call(
        functools.partial(gather_project_kernel, count, dp_count),
        out_shape=(
            jax.ShapeDtypeStruct((count, rows, half), jnp.bfloat16),
            stack_shape,
            pair_shape,
            stack_shape,
        ),
        in_specs=[pl.BlockSpec(memory_space=pltpu.SMEM)]
        + [pl.BlockSpec(memory_space=pltpu.VMEM)] * 2 + [anywhere] * 4,
        out_specs=(anywhere,) * 4,
        scratch_shapes=[
            pltpu.VMEM((count, rows, half), jnp.bfloat16),
            pltpu.VMEM((half, all_cols), jnp.bfloat16),
            pltpu.VMEM((count, rows, all_cols), jnp.float32),
            pltpu.VMEM((count, rows, own_cols), jnp.float32),
            pltpu.VMEM(stack_shape.shape, jnp.bfloat16),
            pltpu.VMEM(pair_shape.shape, jnp.bfloat16),
            pltpu.VMEM(stack_shape.shape, jnp.bfloat16),
            dma((count,)), dma((count,)), dma((count,)), dma, dma((4,)), dma, dma,
            dma((dp_count - 1,)), dma((dp_count - 1,)),
            dma((count, own_cols // 256)), dma((count, own_cols // 256)),
            dma((count,)), dma((count,)), dma((count,)), dma,
        ],
        compiler_params=pltpu.CompilerParams(
            collective_id=0, has_side_effects=True, vmem_limit_bytes=58 * 2**20),
    )(lengths, head_grad, table, hidden, query_weight, key_weight, value_weight)

def attend_kernel(
    dp_count, head_width, queries, upstream, pairs, table_ref, rows_ref,
    squares_out, peer_out,
    rows, grads, mate_grads, rounded, peer_squares,
    rows_load, grad_send, grad_recv, final_send, final_recv, peer_send, peer_recv,
):
    me = lax.axis_index("tensor")
    core = lax.axis_index("dp")
    side = lax.rem(me, 2)
    mate = me + 1 - 2 * side
    blocks, stacked, _ = queries.shape
    step_rows = head_width
    scale = 1.0 / math.sqrt(head_width)
    share = squares_out.shape[1]
    tile = 256
    tiles = share // tile

    barrier = pltpu.get_barrier_semaphore()
    pl.semaphore_signal(barrier, inc=1, device_id={"tensor": mate}, device_id_type=MESH)
    for step in range(1, dp_count):
        peer = lax.rem(core + step, dp_count)
        pl.semaphore_signal(barrier, inc=1, device_id={"dp": peer}, device_id_type=MESH)

    load = pltpu.make_async_copy(rows_ref, rows, rows_load)
    load.start()
    pl.semaphore_wait(barrier, dp_count)

    def grad_copy(block):
        return pltpu.make_async_remote_copy(
            src_ref=grads.at[block], dst_ref=mate_grads.at[block],
            send_sem=grad_send.at[block], recv_sem=grad_recv.at[block],
            device_id={"tensor": mate}, device_id_type=MESH)

    def rows_of(block):
        return slice(block * step_rows, (block + 1) * step_rows)

    def final_copy(block):
        here = rows_of(block)
        return pltpu.make_async_remote_copy(
            src_ref=rounded.at[here], dst_ref=rounded.at[here],
            send_sem=final_send.at[block], recv_sem=final_recv.at[block],
            device_id={"tensor": mate}, device_id_type=MESH)

    def finish(block):
        @pl.when(side == block % 2)
        def _():
            grad_copy(block).wait_recv()
            here = rows_of(block)
            cosine, sine = cosine_sine(table_ref[here, :])
            key_grad = grads[block, :, :head_width] + mate_grads[block, :, :head_width]
            key_grad = key_grad * cosine - swap_halves(key_grad) * sine
            rounded[here, :head_width] = key_grad.astype(jnp.bfloat16)
            rounded[here, head_width:] = (
                grads[block, :, head_width:] + mate_grads[block, :, head_width:]
            ).astype(jnp.bfloat16)
            final_copy(block).start()

    wide = 2 * head_width
    contract_last = (((1,), (1,)), ((), ()))
    for block in reversed(range(blocks)):
        extent = (block + 1) * step_rows
        for chunk in range(stacked // wide):
            chunk_rows = slice(chunk * wide, (chunk + 1) * wide)
            query = queries[block, chunk_rows, :]
            above = upstream[block, chunk_rows, :]
            scores = lax.dot_general(
                pairs[:extent, :head_width], query, contract_last, preferred_element_type=jnp.float32)
            key_at = lax.broadcasted_iota(jnp.int32, (step_rows, wide), 0)
            query_at = lax.rem(lax.broadcasted_iota(jnp.int32, (step_rows, wide), 1), step_rows)
            corner = jnp.where(key_at <= query_at, scores[extent - step_rows:], far_below)
            if block > 0:
                scores = jnp.concatenate([scores[:extent - step_rows], corner], axis=0)
            else:
                scores = corner
            peak = jnp.max(scores, axis=0, keepdims=True)
            powers = jnp.exp2((scores - peak) * (scale * math.log2(math.e)))
            prob = powers * (1.0 / jnp.sum(powers, axis=0, keepdims=True))
            dprob = lax.dot_general(
                pairs[:extent, head_width:], above, contract_last, preferred_element_type=jnp.float32)
            row_dot = jnp.sum(prob * dprob, axis=0, keepdims=True)
            dscore = (prob * (dprob - row_dot) * scale).astype(jnp.bfloat16)
            key_part = jnp.dot(dscore, query, preferred_element_type=jnp.float32)
            value_part = jnp.dot(
                prob.astype(jnp.bfloat16), above, preferred_element_type=jnp.float32)
            key_part = key_part.reshape(block + 1, step_rows, head_width)
            value_part = value_part.reshape(block + 1, step_rows, head_width)
            if block == blocks - 1 and chunk == 0:
                grads[:, :, :head_width] = key_part
                grads[:, :, head_width:] = value_part
            else:
                grads[:block + 1, :, :head_width] += key_part
                grads[:block + 1, :, head_width:] += value_part
        @pl.when(side != block % 2)
        def _():
            grad_copy(block).start()

        if block + 3 < blocks:
            finish(block + 3)

    for block in reversed(range(min(3, blocks))):
        finish(block)
    for block in reversed(range(blocks)):
        @pl.when(side != block % 2)
        def _():
            final_copy(block).wait_recv()

    load.wait()

    def squares_of(start):
        columns = pl.ds(pl.multiple_of(start, tile), tile)
        sample = lax.dot_general(
            rows[:, columns], rounded[...], (((0,), (0,)), ((), ())),
            preferred_element_type=jnp.float32)
        return sample * sample

    def peer_copy(step, index):
        here = pl.ds(pl.multiple_of(index * tile, tile), tile)
        return pltpu.make_async_remote_copy(
            src_ref=peer_squares.at[step - 1, :, here], dst_ref=peer_out.at[step - 1, :, here],
            send_sem=peer_send.at[step - 1, index], recv_sem=peer_recv.at[step - 1, index],
            device_id={"dp": lax.rem(core + step, dp_count)}, device_id_type=MESH)

    for step in range(1, dp_count):
        @pl.loop(0, tiles)
        def _(index):
            here = pl.ds(pl.multiple_of(index * tile, tile), tile)
            start = lax.rem(core + step, dp_count) * share + index * tile
            squares = squares_of(start)
            peer_squares[step - 1, 0, here, :] = squares[:, :head_width]
            peer_squares[step - 1, 1, here, :] = squares[:, head_width:]
            peer_copy(step, index).start()

    @pl.loop(0, tiles)
    def _(index):
        here = pl.ds(pl.multiple_of(index * tile, tile), tile)
        squares = squares_of(core * share + index * tile)
        squares_out[0, here, :] = squares[:, :head_width]
        squares_out[1, here, :] = squares[:, head_width:]

    for block in range(blocks):
        @pl.when(side != block % 2)
        def _():
            grad_copy(block).wait_send()

        @pl.when(side == block % 2)
        def _():
            final_copy(block).wait_send()
    for step in range(1, dp_count):
        @pl.loop(0, tiles)
        def _(index):
            peer_copy(step, index).wait()


def attend(queries, upstream, pairs, table, half_rows, head_width):
    dp_count = lax.axis_size("dp")
    length, half = half_rows.shape
    blocks = length // head_width
    share = half // dp_count
    wide = 2 * head_width
    dma = pltpu.SemaphoreType.DMA
    here = pl.BlockSpec(memory_space=pltpu.VMEM)
    anywhere = pl.BlockSpec(memory_space=pl.ANY)
    return pl.pallas_call(
        functools.partial(attend_kernel, dp_count, head_width),
        out_shape=(
            jax.ShapeDtypeStruct((2, share, head_width), jnp.float32),
            jax.ShapeDtypeStruct((dp_count - 1, 2, share, head_width), jnp.float32),
        ),
        in_specs=[here] * 4 + [anywhere],
        out_specs=(here, anywhere),
        scratch_shapes=[
            pltpu.VMEM((length, half), jnp.bfloat16),
            pltpu.VMEM((blocks, head_width, wide), jnp.float32),
            pltpu.VMEM((blocks, head_width, wide), jnp.float32),
            pltpu.VMEM((length, wide), jnp.bfloat16),
            pltpu.VMEM((dp_count - 1, 2, share, head_width), jnp.float32),
            dma, dma((blocks,)), dma((blocks,)), dma((blocks,)), dma((blocks,)),
            dma((dp_count - 1, share // 256)), dma((dp_count - 1, share // 256)),
        ],
        compiler_params=pltpu.CompilerParams(
            collective_id=1, has_side_effects=True, vmem_limit_bytes=56 * 2**20),
    )(queries, upstream, pairs, table, half_rows)


def fused_kernel(
    count, lengths_ref, gradient_ref, table_ref, hidden_ref, query_ref, key_ref, value_ref,
    key_out, value_out,
    held, weights, partial, other, queries, pairs, upstream,
    grads, mate_grads, rounded, send_squares, peer_squares,
    rows_recv, rows_send, mate_send, load_sem,
    wide_send, wide_recv, core_send, core_recv, cross_send, cross_recv, hand_send, hand_recv,
    partial_send, partial_recv, grad_send, grad_recv, final_send, final_recv,
    square_send, square_recv,
):
    me = lax.axis_index("tensor")
    core = lax.axis_index("dp")
    group = lax.axis_index("groups")
    side = lax.rem(me, 2)
    place = lax.div(me, 2)
    mate = me + 1 - 2 * side
    chain = count // 2
    length, half = held.shape
    rows = length // count
    piece_rows = rows // PIECES
    query_cols = query_ref.shape[1]
    head_width = key_ref.shape[1]
    pair_cols = 2 * head_width
    heads = query_cols // head_width
    sent_cols = query_cols + pair_cols
    has_up = place < chain - 1
    has_down = place > 0

    barrier = pltpu.get_barrier_semaphore()
    pl.semaphore_signal(barrier, inc=1, device_id={"tensor": mate}, device_id_type=MESH)
    pl.semaphore_signal(barrier, inc=1, device_id={"dp": 1 - core}, device_id_type=MESH)
    pl.semaphore_signal(barrier, inc=1, device_id={"groups": 1 - group}, device_id_type=MESH)

    @pl.when(has_up)
    def _():
        pl.semaphore_signal(barrier, inc=1, device_id={"tensor": me + 2}, device_id_type=MESH)

    @pl.when(has_down)
    def _():
        pl.semaphore_signal(barrier, inc=1, device_id={"tensor": me - 2}, device_id_type=MESH)

    edges = jnp.where(has_up, 1, 0) + jnp.where(has_down, 1, 0)
    pl.semaphore_wait(barrier, 3 + edges)

    def piece_at(slot, piece):
        return pl.ds(pl.multiple_of(slot * rows + piece * piece_rows, piece_rows), piece_rows)

    def rows_copy(way, slot, piece, source):
        return pltpu.make_async_remote_copy(
            src_ref=source, dst_ref=held.at[piece_at(slot, piece)],
            send_sem=rows_send.at[way, slot, piece], recv_sem=rows_recv.at[slot, piece],
            device_id={"tensor": me + 2 - 4 * way}, device_id_type=MESH)

    def pass_on(way, slot, piece):
        rows_copy(way, slot, piece, held.at[piece_at(slot, piece)]).start()

    def wait_rows(slot, piece):
        here = held.at[piece_at(slot, piece)]
        pltpu.make_async_remote_copy(
            src_ref=here, dst_ref=here, send_sem=mate_send.at[piece],
            recv_sem=rows_recv.at[slot, piece], device_id={"tensor": mate},
            device_id_type=MESH).wait_recv()

    own_cols = pl.ds(pl.multiple_of(side * half, half), half)
    mate_half = pl.ds(pl.multiple_of((1 - side) * half, half), half)

    def own_piece(piece):
        return hidden_ref.at[piece * piece_rows:(piece + 1) * piece_rows, own_cols]

    to_mate = [
        pltpu.make_async_remote_copy(
            src_ref=hidden_ref.at[piece * piece_rows:(piece + 1) * piece_rows, mate_half],
            dst_ref=held.at[piece_at(me, piece)], send_sem=mate_send.at[piece],
            recv_sem=rows_recv.at[me, piece], device_id={"tensor": mate}, device_id_type=MESH)
        for piece in range(PIECES)
    ]
    for piece in range(PIECES):
        to_mate[piece].start()

        @pl.when(has_up)
        def _():
            rows_copy(0, me, piece, own_piece(piece)).start()

        @pl.when(has_down)
        def _():
            rows_copy(1, me, piece, own_piece(piece)).start()

    quarter = half // 4
    strip = quarter // STRIPS
    half_rows = pl.ds(pl.multiple_of(side * half, half), half)
    loads = [
        pltpu.make_async_copy(
            hidden_ref.at[:, own_cols], held.at[pl.ds(pl.multiple_of(me * rows, rows), rows)],
            load_sem.at[0]),
        pltpu.make_async_copy(
            key_ref, weights.at[:, pl.ds(query_cols, head_width)], load_sem.at[1]),
        pltpu.make_async_copy(
            value_ref, weights.at[:, pl.ds(query_cols + head_width, head_width)], load_sem.at[2]),
        pltpu.make_async_copy(
            query_ref.at[half_rows], weights.at[:, pl.ds(sent_cols, query_cols)], load_sem.at[3]),
    ]
    for load in loads:
        load.start()

    def strip_at(quarter_of, index):
        start = quarter_of * quarter + index * strip
        return pl.ds(pl.multiple_of(start, strip), strip)

    here_quarter = group * 2 + core
    cross_quarter = (1 - group) * 2 + core

    def wide_copy(index):
        start = (1 - side) * half + here_quarter * quarter + index * strip
        return pltpu.make_async_remote_copy(
            src_ref=query_ref.at[pl.ds(pl.multiple_of(start, strip), strip)],
            dst_ref=weights.at[strip_at(here_quarter, index), pl.ds(0, query_cols)],
            send_sem=wide_send.at[index], recv_sem=wide_recv.at[index],
            device_id={"tensor": mate}, device_id_type=MESH)

    def weight_copy(quarter_of, index, send, recv, device):
        here = weights.at[strip_at(quarter_of, index), pl.ds(0, query_cols)]
        return pltpu.make_async_remote_copy(
            src_ref=here, dst_ref=here, send_sem=send.at[index], recv_sem=recv.at[index],
            device_id=device, device_id_type=MESH)

    def core_copy(index):
        return weight_copy(here_quarter, index, core_send, core_recv, {"dp": 1 - core})

    def cross_copy(index):
        return weight_copy(here_quarter, index, cross_send, cross_recv, {"groups": 1 - group})

    def hand_copy(index):
        return weight_copy(cross_quarter, index, hand_send, hand_recv, {"dp": 1 - core})

    for index in range(STRIPS):
        wide_copy(index).start()

    live = lengths_ref[0]

    @pl.loop(0, count)
    def _(slot):
        here = pl.ds(pl.multiple_of(slot * rows, rows), rows)
        position = slot * rows + lax.broadcasted_iota(jnp.int32, (rows, head_width), 0)
        for head in range(heads):
            gradient = gradient_ref[here, head * head_width:(head + 1) * head_width]
            upstream[slot, head * rows:(head + 1) * rows, :] = jnp.where(
                position < live, gradient.astype(jnp.float32), 0.0).astype(jnp.bfloat16)

    for piece in range(PIECES):
        wait_rows(mate, piece)

        @pl.when(has_up)
        def _():
            pass_on(0, mate, piece)

        @pl.when(has_down)
        def _():
            pass_on(1, mate, piece)

    def slot_of(distance, which, way):
        plane = place - distance + 2 * distance * way
        turned = side + which - 2 * side * which
        return plane, 2 * plane + turned

    def receive(distance, which):
        @pl.loop(0, 2 * PIECES)
        def _(step):
            piece = lax.div(step, 2)
            way = lax.rem(step, 2)
            plane, slot = slot_of(distance, which, way)

            @pl.when((plane >= 0) & (plane < chain))
            def _():
                wait_rows(slot, piece)

                @pl.when((place + 1 - 2 * way >= 0) & (place + 1 - 2 * way < chain))
                def _():
                    pass_on(way, slot, piece)

    def partial_copy(slot, piece):
        here = piece_at(slot, piece)
        return pltpu.make_async_remote_copy(
            src_ref=partial.at[here, pl.ds(0, sent_cols)], dst_ref=other.at[here],
            send_sem=partial_send.at[slot, piece], recv_sem=partial_recv.at[slot, piece],
            device_id={"tensor": mate}, device_id_type=MESH)

    def project(slot, piece):
        here = piece_at(slot, piece)
        partial[here, :sent_cols] = jnp.dot(
            held[here], weights[:, :sent_cols], preferred_element_type=jnp.float32)
        partial_copy(slot, piece).start()
        partial[here, sent_cols:] = jnp.dot(
            held[here], weights[:, sent_cols:], preferred_element_type=jnp.float32)

    def project_step(distance, which):
        @pl.loop(0, 2 * PIECES)
        def _(step):
            piece = lax.div(step, 2)
            way = lax.rem(step, 2)
            plane, slot = slot_of(distance, which, way)

            @pl.when((plane >= 0) & (plane < chain))
            def _():
                project(slot, piece)

    def finish(slot):
        for piece in range(PIECES):
            partial_copy(slot, piece).wait_recv()
        here = pl.ds(pl.multiple_of(slot * rows, rows), rows)
        cosine, sine = cosine_sine(table_ref[here, :])

        def turn(mixed):
            return (mixed * cosine + swap_halves(mixed) * sine).astype(jnp.bfloat16)

        for head in range(heads):
            columns = slice(head * head_width, (head + 1) * head_width)
            mine = slice(sent_cols + head * head_width, sent_cols + (head + 1) * head_width)
            queries[slot, head * rows:(head + 1) * rows, :] = turn(
                partial[here, mine] + other[here, columns])
        key_at = slice(query_cols, query_cols + head_width)
        value_at = slice(query_cols + head_width, sent_cols)
        pairs[here, :head_width] = turn(partial[here, key_at] + other[here, key_at])
        pairs[here, head_width:] = (
            partial[here, value_at] + other[here, value_at]).astype(jnp.bfloat16)

    def finish_step(distance, which):
        @pl.loop(0, 2)
        def _(way):
            plane, slot = slot_of(distance, which, way)

            @pl.when((plane >= 0) & (plane < chain))
            def _():
                finish(slot)

    receive(1, 0)
    for index in range(STRIPS):
        wide_copy(index).wait_recv()
        core_copy(index).start()
        cross_copy(index).start()
    receive(1, 1)
    for index in range(STRIPS):
        cross_copy(index).wait_recv()
        hand_copy(index).start()
    for load in loads:
        load.wait()
    for index in range(STRIPS):
        core_copy(index).wait_recv()
    for index in range(STRIPS):
        hand_copy(index).wait_recv()

    @pl.loop(0, 2 * PIECES)
    def _(step):
        project(2 * place + lax.rem(step, 2), lax.div(step, 2))

    @pl.loop(0, 2)
    def _(which):
        project_step(1, which)

    @pl.loop(0, 2)
    def _(which):
        finish(2 * place + which)

    @pl.loop(4, 2 * chain)
    def _(step):
        receive(lax.div(step, 2), lax.rem(step, 2))
        project_step(lax.div(step, 2), lax.rem(step, 2))
        finish_step(lax.div(step - 2, 2), lax.rem(step, 2))

    @pl.loop(2 * chain - 2, 2 * chain)
    def _(step):
        finish_step(lax.div(step, 2), lax.rem(step, 2))

    scale = 1.0 / math.sqrt(head_width)
    blocks = count

    def grad_copy(block):
        return pltpu.make_async_remote_copy(
            src_ref=grads.at[block], dst_ref=mate_grads.at[block],
            send_sem=grad_send.at[block], recv_sem=grad_recv.at[block],
            device_id={"tensor": mate}, device_id_type=MESH)

    def rows_of(block):
        return slice(block * rows, (block + 1) * rows)

    def final_copy(block):
        here = rows_of(block)
        return pltpu.make_async_remote_copy(
            src_ref=rounded.at[here], dst_ref=rounded.at[here],
            send_sem=final_send.at[block], recv_sem=final_recv.at[block],
            device_id={"tensor": mate}, device_id_type=MESH)

    def sum_up(block):
        @pl.when(side == block % 2)
        def _():
            grad_copy(block).wait_recv()
            here = rows_of(block)
            cosine, sine = cosine_sine(table_ref[here, :])
            key_grad = grads[block, :, :head_width] + mate_grads[block, :, :head_width]
            key_grad = key_grad * cosine - swap_halves(key_grad) * sine
            rounded[here, :head_width] = key_grad.astype(jnp.bfloat16)
            rounded[here, head_width:] = (
                grads[block, :, head_width:] + mate_grads[block, :, head_width:]
            ).astype(jnp.bfloat16)
            final_copy(block).start()

    wide = heads * rows
    contract_last = (((1,), (1,)), ((), ()))
    for block in reversed(range(blocks)):
        extent = (block + 1) * rows
        query = queries[block]
        above = upstream[block]
        scores = lax.dot_general(
            pairs[:extent, :head_width], query, contract_last, preferred_element_type=jnp.float32)
        key_at = lax.broadcasted_iota(jnp.int32, (rows, wide), 0)
        query_at = lax.rem(lax.broadcasted_iota(jnp.int32, (rows, wide), 1), rows)
        corner = jnp.where(key_at <= query_at, scores[extent - rows:], far_below)
        if block > 0:
            scores = jnp.concatenate([scores[:extent - rows], corner], axis=0)
        else:
            scores = corner
        peak = jnp.max(scores, axis=0, keepdims=True)
        powers = jnp.exp2((scores - peak) * (scale * math.log2(math.e)))
        prob = powers * (1.0 / jnp.sum(powers, axis=0, keepdims=True))
        dprob = lax.dot_general(
            pairs[:extent, head_width:], above, contract_last, preferred_element_type=jnp.float32)
        row_dot = jnp.sum(prob * dprob, axis=0, keepdims=True)
        dscore = (prob * (dprob - row_dot) * scale).astype(jnp.bfloat16)
        key_part = jnp.dot(dscore, query, preferred_element_type=jnp.float32)
        value_part = jnp.dot(prob.astype(jnp.bfloat16), above, preferred_element_type=jnp.float32)
        key_part = key_part.reshape(block + 1, rows, head_width)
        value_part = value_part.reshape(block + 1, rows, head_width)
        if block == blocks - 1:
            grads[:, :, :head_width] = key_part
            grads[:, :, head_width:] = value_part
        else:
            grads[:block + 1, :, :head_width] += key_part
            grads[:block + 1, :, head_width:] += value_part

        @pl.when(side != block % 2)
        def _():
            grad_copy(block).start()

        if block + 3 < blocks:
            sum_up(block + 3)

    for block in reversed(range(min(3, blocks))):
        sum_up(block)
    for block in reversed(range(blocks)):
        @pl.when(side != block % 2)
        def _():
            final_copy(block).wait_recv()

    share = half // 2
    tiles = share // TILE

    def squares_of(start):
        columns = pl.ds(pl.multiple_of(start, TILE), TILE)
        sample = lax.dot_general(
            held[:, columns], rounded[...], (((0,), (0,)), ((), ())),
            preferred_element_type=jnp.float32)
        return sample * sample

    def square_copy(index):
        here = pl.ds(pl.multiple_of(index * TILE, TILE), TILE)
        return pltpu.make_async_remote_copy(
            src_ref=send_squares.at[here], dst_ref=peer_squares.at[here],
            send_sem=square_send.at[index], recv_sem=square_recv.at[index],
            device_id={"dp": 1 - core}, device_id_type=MESH)

    @pl.loop(0, tiles)
    def _(index):
        here = pl.ds(pl.multiple_of(index * TILE, TILE), TILE)
        send_squares[here, :] = squares_of((1 - core) * share + index * TILE)
        square_copy(index).start()

    @pl.loop(0, tiles)
    def _(index):
        here = pl.ds(pl.multiple_of(index * TILE, TILE), TILE)
        squares = squares_of(core * share + index * TILE)
        square_copy(index).wait_recv()
        squares = squares + peer_squares[here, :]
        key_out[here, :] = squares[:, :head_width]
        value_out[here, :] = squares[:, head_width:]

    for copy in to_mate:
        copy.wait_send()
    for index in range(STRIPS):
        wide_copy(index).wait_send()
        core_copy(index).wait_send()
        cross_copy(index).wait_send()
        hand_copy(index).wait_send()

    @pl.loop(0, count * PIECES)
    def _(step):
        slot = lax.div(step, PIECES)
        piece = lax.rem(step, PIECES)
        partial_copy(slot, piece).wait_send()
        origin = lax.div(slot, 2)

        @pl.when(has_up & (origin <= place))
        def _():
            rows_copy(0, slot, piece, held.at[piece_at(slot, piece)]).wait_send()

        @pl.when(has_down & (origin >= place))
        def _():
            rows_copy(1, slot, piece, held.at[piece_at(slot, piece)]).wait_send()

    for block in range(blocks):
        @pl.when(side != block % 2)
        def _():
            grad_copy(block).wait_send()

        @pl.when(side == block % 2)
        def _():
            final_copy(block).wait_send()

    @pl.loop(0, tiles)
    def _(index):
        square_copy(index).wait_send()


PIECES = 2
STRIPS = 4
TILE = 512


def fused(lengths, head_grad, table, hidden, query_weight, key_weight, value_weight):
    count = lax.axis_size("tensor")
    rows, model_width = hidden.shape
    length = rows * count
    half = model_width // 2
    query_cols = query_weight.shape[1]
    head_width = key_weight.shape[1]
    pair_cols = 2 * head_width
    sent_cols = query_cols + pair_cols
    all_cols = sent_cols + query_cols
    heads = query_cols // head_width
    share = half // 2
    dma = pltpu.SemaphoreType.DMA
    anywhere = pl.BlockSpec(memory_space=pl.ANY)
    here = pl.BlockSpec(memory_space=pltpu.VMEM)
    out = jax.ShapeDtypeStruct((share, head_width), jnp.float32)
    return pl.pallas_call(
        functools.partial(fused_kernel, count),
        out_shape=(out, out),
        in_specs=[pl.BlockSpec(memory_space=pltpu.SMEM)] + [here] * 2 + [anywhere] * 4,
        out_specs=(here, here),
        scratch_shapes=[
            pltpu.VMEM((length, half), jnp.bfloat16),
            pltpu.VMEM((half, all_cols), jnp.bfloat16),
            pltpu.VMEM((length, all_cols), jnp.float32),
            pltpu.VMEM((length, sent_cols), jnp.float32),
            pltpu.VMEM((count, heads * rows, head_width), jnp.bfloat16),
            pltpu.VMEM((length, pair_cols), jnp.bfloat16),
            pltpu.VMEM((count, heads * rows, head_width), jnp.bfloat16),
            pltpu.VMEM((count, rows, pair_cols), jnp.float32),
            pltpu.VMEM((count, rows, pair_cols), jnp.float32),
            pltpu.VMEM((length, pair_cols), jnp.bfloat16),
            pltpu.VMEM((share, pair_cols), jnp.float32),
            pltpu.VMEM((share, pair_cols), jnp.float32),
            dma((count, PIECES)), dma((2, count, PIECES)), dma((PIECES,)), dma((4,)),
            dma((STRIPS,)), dma((STRIPS,)), dma((STRIPS,)), dma((STRIPS,)),
            dma((STRIPS,)), dma((STRIPS,)), dma((STRIPS,)), dma((STRIPS,)),
            dma((count, PIECES)), dma((count, PIECES)),
            dma((count,)), dma((count,)), dma((count,)), dma((count,)),
            dma((share // TILE,)), dma((share // TILE,)),
        ],
        compiler_params=pltpu.CompilerParams(
            collective_id=2, has_side_effects=True, vmem_limit_bytes=58 * 2**20),
    )(lengths, head_grad, table, hidden, query_weight, key_weight, value_weight)


def local(hidden, query_weight, key_weight, value_weight, head_grad, lengths):
    head_width = key_weight.shape[2]
    length = head_grad.shape[1]
    table = jnp.asarray(turn_table(length, head_width))
    if lax.axis_size("groups") == 2 and lax.axis_size("dp") == 2 and lax.axis_size("tensor") == 8:
        fisher_key, fisher_value = fused(
            lengths, head_grad[0], table, hidden[0], query_weight, key_weight[0], value_weight[0])
        return (fisher_key[None], fisher_value[None])
    half_rows, queries, pairs, upstream = gather_project(
        lengths, head_grad[0], table, hidden[0], query_weight, key_weight[0], value_weight[0]
    )
    own, peer = attend(
        queries, upstream, pairs.reshape(length, -1), table, half_rows.reshape(length, -1),
        head_width,
    )
    fisher_key = own[:1] + jnp.sum(peer[:, :1], axis=0)
    fisher_value = own[1:] + jnp.sum(peer[:, 1:], axis=0)
    return (fisher_key, fisher_value)


def solution(mesh):
    in_specs = (
        P(("groups", "dp"), "tensor", None),
        P(None, "tensor"),
        P("tensor", None, None),
        P("tensor", None, None),
        P(("groups", "dp"), None, "tensor"),
        P(("groups", "dp")),
    )
    out_specs = (P(("groups", "tensor"), "dp", None), P(("groups", "tensor"), "dp", None))
    return jax.shard_map(local, mesh=mesh, in_specs=in_specs, out_specs=out_specs, check_vma=False)
```

```python
import functools
import math

import jax
import jax.numpy as jnp
import numpy as np
from jax import lax
from jax.experimental import pallas as pl
from jax.experimental.pallas import tpu as pltpu
from jax.sharding import PartitionSpec as P

MESH = pl.DeviceIdType.MESH

rope_base = 1000000.0
far_below = -1e30


def turn_table(length, head_width):
    position = np.arange(length, dtype=np.float64)[:, None]
    frequency = rope_base ** (-2.0 * np.arange(head_width // 2, dtype=np.float64) / head_width)
    angles = position * frequency
    return np.concatenate([np.cos(angles), np.sin(angles)], axis=-1).astype(np.float32)


def swap_halves(vectors):
    return pltpu.roll(vectors, vectors.shape[-1] // 2, axis=1)


def cosine_sine(table):
    other = swap_halves(table)
    lead = lax.broadcasted_iota(jnp.int32, table.shape, 1) < table.shape[1] // 2
    return jnp.where(lead, table, other), jnp.where(lead, -other, table)


def gather_project_kernel(
    count, dp_count, lengths_ref, gradient_ref, table_ref,
    hidden_ref, query_ref, key_ref, value_ref,
    rows_out, queries_out, pairs_out, upstream_out,
    held, weights, partial, other, queries, pairs, upstream,
    rows_recv, up_send, down_send, mate_send, load_sem, weight_send, weight_recv,
    share_send, share_recv, partial_send, partial_recv, rows_store, queries_store, pairs_store,
    upstream_store,
):
    me = lax.axis_index("tensor")
    core = lax.axis_index("dp")
    side = lax.rem(me, 2)
    place = lax.div(me, 2)
    mate = me + 1 - 2 * side
    chain = count // 2
    half = held.shape[2]
    query_cols = query_ref.shape[1]
    head_width = key_ref.shape[1]
    own_cols = query_cols + 2 * head_width
    has_up = place < chain - 1
    has_down = place > 0
    share = half // dp_count

    barrier = pltpu.get_barrier_semaphore()
    pl.semaphore_signal(barrier, inc=1, device_id={"tensor": mate}, device_id_type=MESH)
    for step in range(1, dp_count):
        peer = lax.rem(core + step, dp_count)
        pl.semaphore_signal(barrier, inc=1, device_id={"dp": peer}, device_id_type=MESH)

    @pl.when(has_up)
    def _():
        pl.semaphore_signal(barrier, inc=1, device_id={"tensor": me + 2}, device_id_type=MESH)

    @pl.when(has_down)
    def _():
        pl.semaphore_signal(barrier, inc=1, device_id={"tensor": me - 2}, device_id_type=MESH)

    edges = jnp.where(has_up, 1, 0) + jnp.where(has_down, 1, 0)
    pl.semaphore_wait(barrier, dp_count + edges)

    own_half = hidden_ref.at[:, pl.ds(pl.multiple_of(side * half, half), half)]
    mate_half = hidden_ref.at[:, pl.ds(pl.multiple_of((1 - side) * half, half), half)]

    def up_copy(slot, source):
        return pltpu.make_async_remote_copy(
            src_ref=source, dst_ref=held.at[slot], send_sem=up_send.at[slot],
            recv_sem=rows_recv.at[slot], device_id={"tensor": me + 2}, device_id_type=MESH)

    def down_copy(slot, source):
        return pltpu.make_async_remote_copy(
            src_ref=source, dst_ref=held.at[slot], send_sem=down_send.at[slot],
            recv_sem=rows_recv.at[slot], device_id={"tensor": me - 2}, device_id_type=MESH)

    def wait_rows(slot):
        pltpu.make_async_remote_copy(
            src_ref=held.at[slot], dst_ref=held.at[slot], send_sem=mate_send,
            recv_sem=rows_recv.at[slot], device_id={"tensor": mate}, device_id_type=MESH).wait_recv()

    def store_rows(slot):
        return pltpu.make_async_copy(held.at[slot], rows_out.at[slot], rows_store.at[slot])

    def store_queries(slot):
        return pltpu.make_async_copy(queries.at[slot], queries_out.at[slot], queries_store.at[slot])

    def store_pairs(slot):
        return pltpu.make_async_copy(pairs.at[slot], pairs_out.at[slot], pairs_store.at[slot])

    tile = 256
    pieces = own_cols // tile

    def partial_copy(slot, piece):
        source = pl.ds(pl.multiple_of(query_cols + piece * tile, tile), tile)
        target = pl.ds(pl.multiple_of(piece * tile, tile), tile)
        return pltpu.make_async_remote_copy(
            src_ref=partial.at[slot, :, source], dst_ref=other.at[slot, :, target],
            send_sem=partial_send.at[slot, piece], recv_sem=partial_recv.at[slot, piece],
            device_id={"tensor": mate}, device_id_type=MESH)

    to_mate = pltpu.make_async_remote_copy(
        src_ref=mate_half, dst_ref=held.at[me], send_sem=mate_send,
        recv_sem=rows_recv.at[me], device_id={"tensor": mate}, device_id_type=MESH)
    to_mate.start()

    @pl.when(has_up)
    def _():
        up_copy(me, own_half).start()

    @pl.when(has_down)
    def _():
        down_copy(me, own_half).start()

    half_rows = pl.ds(pl.multiple_of(side * half, half), half)
    loads = [
        pltpu.make_async_copy(own_half, held.at[me], load_sem.at[0]),
        pltpu.make_async_copy(
            query_ref.at[half_rows], weights.at[:, pl.ds(0, query_cols)], load_sem.at[1]),
        pltpu.make_async_copy(
            key_ref, weights.at[:, pl.ds(query_cols, head_width)], load_sem.at[2]),
        pltpu.make_async_copy(
            value_ref, weights.at[:, pl.ds(query_cols + head_width, head_width)], load_sem.at[3]),
    ]
    for load in loads:
        load.start()

    share_rows = pl.ds(pl.multiple_of(core * share, share), share)
    mate_cols = pl.ds(own_cols, query_cols)
    weight_copy = pltpu.make_async_remote_copy(
        src_ref=query_ref.at[pl.ds(pl.multiple_of((1 - side) * half + core * share, share), share)],
        dst_ref=weights.at[share_rows, mate_cols], send_sem=weight_send, recv_sem=weight_recv,
        device_id={"tensor": mate}, device_id_type=MESH)

    live = lengths_ref[0]
    rows = held.shape[1]
    heads = query_cols // head_width

    @pl.loop(0, count)
    def _(slot):
        here = pl.ds(pl.multiple_of(slot * rows, rows), rows)
        position = slot * rows + lax.broadcasted_iota(jnp.int32, (rows, head_width), 0)
        for head in range(heads):
            gradient = gradient_ref[here, head * head_width:(head + 1) * head_width]
            upstream[slot, head * rows:(head + 1) * rows, :] = jnp.where(
                position < live, gradient.astype(jnp.float32), 0.0).astype(jnp.bfloat16)

    store_upstream = pltpu.make_async_copy(upstream, upstream_out, upstream_store)
    store_upstream.start()
    wait_rows(mate)

    @pl.when(has_up)
    def _():
        up_copy(mate, held.at[mate]).start()

    @pl.when(has_down)
    def _():
        down_copy(mate, held.at[mate]).start()

    weight_copy.start()

    def slot_at(step, which):
        return 2 * step + jnp.where(which == 0, side, 1 - side)

    def receive(distance, which):
        below = place - distance
        above = place + distance

        @pl.when(below >= 0)
        def _():
            slot = slot_at(below, which)
            wait_rows(slot)

            @pl.when(has_up)
            def _():
                up_copy(slot, held.at[slot]).start()

        @pl.when(above < chain)
        def _():
            slot = slot_at(above, which)
            wait_rows(slot)

            @pl.when(has_down)
            def _():
                down_copy(slot, held.at[slot]).start()

    def multiply(slot, start):
        columns = pl.ds(pl.multiple_of(start, tile), tile)
        partial[slot, :, columns] = jnp.dot(
            held[slot], weights[:, columns], preferred_element_type=jnp.float32)

    def project_pair(slot):
        store_rows(slot).start()
        multiply(slot, query_cols)

    def send_pair(slot):
        partial_copy(slot, 0).start()

    def project_queries(slot):
        @pl.loop(1, pieces)
        def _(piece):
            multiply(slot, query_cols + piece * tile)
            partial_copy(slot, piece).start()

        @pl.loop(0, query_cols // tile)
        def _(piece):
            multiply(slot, piece * tile)

    def project(slot):
        project_pair(slot)
        send_pair(slot)
        project_queries(slot)

    def project_at(distance, which, action):
        below = place - distance
        above = place + distance

        @pl.when(below >= 0)
        def _():
            action(slot_at(below, which))

        @pl.when(above < chain)
        def _():
            action(slot_at(above, which))

    receive(1, 0)
    receive(1, 1)
    for load in loads:
        load.wait()

    def early(action):
        @pl.loop(0, 2)
        def _(which):
            action(slot_at(place, which))

        @pl.loop(0, 2)
        def _(which):
            project_at(1, which, action)

    early(project_pair)
    weight_copy.wait_recv()
    shares = []
    for step in range(1, dp_count):
        peer = lax.rem(core + step, dp_count)
        shares.append(pltpu.make_async_remote_copy(
            src_ref=weights.at[share_rows, mate_cols], dst_ref=weights.at[share_rows, mate_cols],
            send_sem=share_send.at[step - 1], recv_sem=share_recv.at[step - 1],
            device_id={"dp": peer}, device_id_type=MESH))
    for copy in shares:
        copy.start()
    early(send_pair)
    for copy in shares:
        copy.wait_recv()
    early(project_queries)

    @pl.loop(4, 2 * chain)
    def _(step):
        distance = lax.div(step, 2)
        which = lax.rem(step, 2)
        receive(distance, which)
        project_at(distance, which, project)

    def finish(slot):
        for piece in range(pieces):
            partial_copy(slot, piece).wait_recv()
        cosine, sine = cosine_sine(table_ref[pl.ds(pl.multiple_of(slot * rows, rows), rows), :])

        def turn(mixed):
            return (mixed * cosine + swap_halves(mixed) * sine).astype(jnp.bfloat16)

        for head in range(heads):
            columns = slice(head * head_width, (head + 1) * head_width)
            shifted = slice((head + 2) * head_width, (head + 3) * head_width)
            queries[slot, head * rows:(head + 1) * rows, :] = turn(
                partial[slot, :, columns] + other[slot, :, shifted])
        pairs[slot, :, :head_width] = turn(
            partial[slot, :, query_cols:query_cols + head_width] + other[slot, :, :head_width])
        pairs[slot, :, head_width:] = (
            partial[slot, :, query_cols + head_width:own_cols]
            + other[slot, :, head_width:2 * head_width]
        ).astype(jnp.bfloat16)
        store_queries(slot).start()
        store_pairs(slot).start()

    @pl.loop(0, 2 * chain)
    def _(step):
        distance = lax.div(step, 2)
        which = lax.rem(step, 2)
        below = place - distance
        above = place + distance

        @pl.when(below >= 0)
        def _():
            finish(slot_at(below, which))

        @pl.when((above < chain) & (distance > 0))
        def _():
            finish(slot_at(above, which))

    store_upstream.wait()
    to_mate.wait_send()
    weight_copy.wait_send()
    for copy in shares:
        copy.wait_send()

    @pl.loop(0, count)
    def _(slot):
        for piece in range(pieces):
            partial_copy(slot, piece).wait_send()
        store_rows(slot).wait()
        store_queries(slot).wait()
        store_pairs(slot).wait()
        origin = lax.div(slot, 2)

        @pl.when(has_up & (origin <= place))
        def _():
            up_copy(slot, held.at[slot]).wait_send()

        @pl.when(has_down & (origin >= place))
        def _():
            down_copy(slot, held.at[slot]).wait_send()


def gather_project(lengths, head_grad, table, hidden, query_weight, key_weight, value_weight):
    count = lax.axis_size("tensor")
    dp_count = lax.axis_size("dp")
    rows, model_width = hidden.shape
    half = model_width // 2
    query_cols = query_weight.shape[1]
    head_width = key_weight.shape[1]
    own_cols = query_cols + 2 * head_width
    all_cols = own_cols + query_cols
    heads = query_cols // head_width
    stack_shape = jax.ShapeDtypeStruct((count, heads * rows, head_width), jnp.bfloat16)
    pair_shape = jax.ShapeDtypeStruct((count, rows, 2 * head_width), jnp.bfloat16)
    dma = pltpu.SemaphoreType.DMA
    anywhere = pl.BlockSpec(memory_space=pl.ANY)
    return pl.pallas_call(
        functools.partial(gather_project_kernel, count, dp_count),
        out_shape=(
            jax.ShapeDtypeStruct((count, rows, half), jnp.bfloat16),
            stack_shape,
            pair_shape,
            stack_shape,
        ),
        in_specs=[pl.BlockSpec(memory_space=pltpu.SMEM)]
        + [pl.BlockSpec(memory_space=pltpu.VMEM)] * 2 + [anywhere] * 4,
        out_specs=(anywhere,) * 4,
        scratch_shapes=[
            pltpu.VMEM((count, rows, half), jnp.bfloat16),
            pltpu.VMEM((half, all_cols), jnp.bfloat16),
            pltpu.VMEM((count, rows, all_cols), jnp.float32),
            pltpu.VMEM((count, rows, own_cols), jnp.float32),
            pltpu.VMEM(stack_shape.shape, jnp.bfloat16),
            pltpu.VMEM(pair_shape.shape, jnp.bfloat16),
            pltpu.VMEM(stack_shape.shape, jnp.bfloat16),
            dma((count,)), dma((count,)), dma((count,)), dma, dma((4,)), dma, dma,
            dma((dp_count - 1,)), dma((dp_count - 1,)),
            dma((count, own_cols // 256)), dma((count, own_cols // 256)),
            dma((count,)), dma((count,)), dma((count,)), dma,
        ],
        compiler_params=pltpu.CompilerParams(
            collective_id=0, has_side_effects=True, vmem_limit_bytes=58 * 2**20),
    )(lengths, head_grad, table, hidden, query_weight, key_weight, value_weight)

def attend_kernel(
    dp_count, head_width, queries, upstream, pairs, table_ref, rows_ref,
    squares_out, peer_out,
    rows, grads, mate_grads, rounded, peer_squares,
    rows_load, grad_send, grad_recv, final_send, final_recv, peer_send, peer_recv,
):
    me = lax.axis_index("tensor")
    core = lax.axis_index("dp")
    side = lax.rem(me, 2)
    mate = me + 1 - 2 * side
    blocks, stacked, _ = queries.shape
    step_rows = head_width
    scale = 1.0 / math.sqrt(head_width)
    share = squares_out.shape[1]
    tile = 256
    tiles = share // tile

    barrier = pltpu.get_barrier_semaphore()
    pl.semaphore_signal(barrier, inc=1, device_id={"tensor": mate}, device_id_type=MESH)
    for step in range(1, dp_count):
        peer = lax.rem(core + step, dp_count)
        pl.semaphore_signal(barrier, inc=1, device_id={"dp": peer}, device_id_type=MESH)

    load = pltpu.make_async_copy(rows_ref, rows, rows_load)
    load.start()
    pl.semaphore_wait(barrier, dp_count)

    def grad_copy(block):
        return pltpu.make_async_remote_copy(
            src_ref=grads.at[block], dst_ref=mate_grads.at[block],
            send_sem=grad_send.at[block], recv_sem=grad_recv.at[block],
            device_id={"tensor": mate}, device_id_type=MESH)

    def rows_of(block):
        return slice(block * step_rows, (block + 1) * step_rows)

    def final_copy(block):
        here = rows_of(block)
        return pltpu.make_async_remote_copy(
            src_ref=rounded.at[here], dst_ref=rounded.at[here],
            send_sem=final_send.at[block], recv_sem=final_recv.at[block],
            device_id={"tensor": mate}, device_id_type=MESH)

    def finish(block):
        @pl.when(side == block % 2)
        def _():
            grad_copy(block).wait_recv()
            here = rows_of(block)
            cosine, sine = cosine_sine(table_ref[here, :])
            key_grad = grads[block, :, :head_width] + mate_grads[block, :, :head_width]
            key_grad = key_grad * cosine - swap_halves(key_grad) * sine
            rounded[here, :head_width] = key_grad.astype(jnp.bfloat16)
            rounded[here, head_width:] = (
                grads[block, :, head_width:] + mate_grads[block, :, head_width:]
            ).astype(jnp.bfloat16)
            final_copy(block).start()

    wide = 2 * head_width
    contract_last = (((1,), (1,)), ((), ()))
    for block in reversed(range(blocks)):
        extent = (block + 1) * step_rows
        for chunk in range(stacked // wide):
            chunk_rows = slice(chunk * wide, (chunk + 1) * wide)
            query = queries[block, chunk_rows, :]
            above = upstream[block, chunk_rows, :]
            scores = lax.dot_general(
                pairs[:extent, :head_width], query, contract_last, preferred_element_type=jnp.float32)
            key_at = lax.broadcasted_iota(jnp.int32, (step_rows, wide), 0)
            query_at = lax.rem(lax.broadcasted_iota(jnp.int32, (step_rows, wide), 1), step_rows)
            corner = jnp.where(key_at <= query_at, scores[extent - step_rows:], far_below)
            if block > 0:
                scores = jnp.concatenate([scores[:extent - step_rows], corner], axis=0)
            else:
                scores = corner
            peak = jnp.max(scores, axis=0, keepdims=True)
            powers = jnp.exp2((scores - peak) * (scale * math.log2(math.e)))
            prob = powers * (1.0 / jnp.sum(powers, axis=0, keepdims=True))
            dprob = lax.dot_general(
                pairs[:extent, head_width:], above, contract_last, preferred_element_type=jnp.float32)
            row_dot = jnp.sum(prob * dprob, axis=0, keepdims=True)
            dscore = (prob * (dprob - row_dot) * scale).astype(jnp.bfloat16)
            key_part = jnp.dot(dscore, query, preferred_element_type=jnp.float32)
            value_part = jnp.dot(
                prob.astype(jnp.bfloat16), above, preferred_element_type=jnp.float32)
            key_part = key_part.reshape(block + 1, step_rows, head_width)
            value_part = value_part.reshape(block + 1, step_rows, head_width)
            if block == blocks - 1 and chunk == 0:
                grads[:, :, :head_width] = key_part
                grads[:, :, head_width:] = value_part
            else:
                grads[:block + 1, :, :head_width] += key_part
                grads[:block + 1, :, head_width:] += value_part
        @pl.when(side != block % 2)
        def _():
            grad_copy(block).start()

        if block + 3 < blocks:
            finish(block + 3)

    for block in reversed(range(min(3, blocks))):
        finish(block)
    for block in reversed(range(blocks)):
        @pl.when(side != block % 2)
        def _():
            final_copy(block).wait_recv()

    load.wait()

    def squares_of(start):
        columns = pl.ds(pl.multiple_of(start, tile), tile)
        sample = lax.dot_general(
            rows[:, columns], rounded[...], (((0,), (0,)), ((), ())),
            preferred_element_type=jnp.float32)
        return sample * sample

    def peer_copy(step, index):
        here = pl.ds(pl.multiple_of(index * tile, tile), tile)
        return pltpu.make_async_remote_copy(
            src_ref=peer_squares.at[step - 1, :, here], dst_ref=peer_out.at[step - 1, :, here],
            send_sem=peer_send.at[step - 1, index], recv_sem=peer_recv.at[step - 1, index],
            device_id={"dp": lax.rem(core + step, dp_count)}, device_id_type=MESH)

    for step in range(1, dp_count):
        @pl.loop(0, tiles)
        def _(index):
            here = pl.ds(pl.multiple_of(index * tile, tile), tile)
            start = lax.rem(core + step, dp_count) * share + index * tile
            squares = squares_of(start)
            peer_squares[step - 1, 0, here, :] = squares[:, :head_width]
            peer_squares[step - 1, 1, here, :] = squares[:, head_width:]
            peer_copy(step, index).start()

    @pl.loop(0, tiles)
    def _(index):
        here = pl.ds(pl.multiple_of(index * tile, tile), tile)
        squares = squares_of(core * share + index * tile)
        squares_out[0, here, :] = squares[:, :head_width]
        squares_out[1, here, :] = squares[:, head_width:]

    for block in range(blocks):
        @pl.when(side != block % 2)
        def _():
            grad_copy(block).wait_send()

        @pl.when(side == block % 2)
        def _():
            final_copy(block).wait_send()
    for step in range(1, dp_count):
        @pl.loop(0, tiles)
        def _(index):
            peer_copy(step, index).wait()


def attend(queries, upstream, pairs, table, half_rows, head_width):
    dp_count = lax.axis_size("dp")
    length, half = half_rows.shape
    blocks = length // head_width
    share = half // dp_count
    wide = 2 * head_width
    dma = pltpu.SemaphoreType.DMA
    here = pl.BlockSpec(memory_space=pltpu.VMEM)
    anywhere = pl.BlockSpec(memory_space=pl.ANY)
    return pl.pallas_call(
        functools.partial(attend_kernel, dp_count, head_width),
        out_shape=(
            jax.ShapeDtypeStruct((2, share, head_width), jnp.float32),
            jax.ShapeDtypeStruct((dp_count - 1, 2, share, head_width), jnp.float32),
        ),
        in_specs=[here] * 4 + [anywhere],
        out_specs=(here, anywhere),
        scratch_shapes=[
            pltpu.VMEM((length, half), jnp.bfloat16),
            pltpu.VMEM((blocks, head_width, wide), jnp.float32),
            pltpu.VMEM((blocks, head_width, wide), jnp.float32),
            pltpu.VMEM((length, wide), jnp.bfloat16),
            pltpu.VMEM((dp_count - 1, 2, share, head_width), jnp.float32),
            dma, dma((blocks,)), dma((blocks,)), dma((blocks,)), dma((blocks,)),
            dma((dp_count - 1, share // 256)), dma((dp_count - 1, share // 256)),
        ],
        compiler_params=pltpu.CompilerParams(
            collective_id=1, has_side_effects=True, vmem_limit_bytes=56 * 2**20),
    )(queries, upstream, pairs, table, half_rows)


def fused_kernel(
    count, lengths_ref, gradient_ref, table_ref, hidden_ref, query_ref, key_ref, value_ref,
    key_out, value_out,
    held, weights, partial, other, queries, pairs, staged, upstream,
    grads, peer_grads, made, rounded, send_squares, peer_squares,
    aid_weights, guest, aid_partial, guest_partial, aid_cross, aid_other, gift, gift_pairs,
    rows_recv, rows_send, mate_send, load_sem,
    wide_send, wide_recv, core_send, core_recv, cross_send, cross_recv, hand_send, hand_recv,
    partial_send, partial_recv, share_send, share_recv, pair_send, pair_recv,
    above_keep, above_send, above_recv, grad_send, grad_recv,
    near_send, far_send, final_recv, square_send, square_recv,
    aid_send, aid_recv, aid_core_send, aid_core_recv, guest_send, guest_recv,
    return_send, return_recv, aid_sum_send, aid_sum_recv, gift_send, gift_recv,
):
    me = lax.axis_index("tensor")
    core = lax.axis_index("dp")
    group = lax.axis_index("groups")
    side = lax.rem(me, 2)
    place = lax.div(me, 2)
    mate = me + 1 - 2 * side
    chain = count // 2
    length, half = held.shape
    rows = length // count
    piece_rows = rows // PIECES
    query_cols = query_ref.shape[1]
    head_width = key_ref.shape[1]
    heads = query_cols // head_width
    cut = query_cols + head_width
    sums = core == side
    has_up = place < chain - 1
    has_down = place > 0

    helper = has_up & has_down
    end = jnp.logical_not(helper)
    end_way = 2 - place
    near = 1 + lax.div(place, chain - 1)
    last = PIECES - 1

    def helped(slot, piece):
        return end & (lax.div(slot, 2) == near) & (piece == last)

    barrier = pltpu.get_barrier_semaphore()
    pl.semaphore_signal(barrier, inc=1, device_id={"tensor": mate}, device_id_type=MESH)
    pl.semaphore_signal(barrier, inc=1, device_id={"dp": 1 - core}, device_id_type=MESH)
    pl.semaphore_signal(
        barrier, inc=1, device_id={"tensor": mate, "dp": 1 - core}, device_id_type=MESH)
    pl.semaphore_signal(barrier, inc=1, device_id={"groups": 1 - group}, device_id_type=MESH)

    @pl.when(has_up)
    def _():
        pl.semaphore_signal(barrier, inc=1, device_id={"tensor": me + 2}, device_id_type=MESH)

    @pl.when(has_down)
    def _():
        pl.semaphore_signal(barrier, inc=1, device_id={"tensor": me - 2}, device_id_type=MESH)

    edges = jnp.where(has_up, 1, 0) + jnp.where(has_down, 1, 0)
    pl.semaphore_wait(barrier, 4 + edges)

    def piece_at(slot, piece):
        return pl.ds(pl.multiple_of(slot * rows + piece * piece_rows, piece_rows), piece_rows)

    def rows_copy(way, slot, piece, source):
        return pltpu.make_async_remote_copy(
            src_ref=source, dst_ref=held.at[piece_at(slot, piece)],
            send_sem=rows_send.at[way, slot, piece], recv_sem=rows_recv.at[slot, piece],
            device_id={"tensor": me + 2 - 4 * way}, device_id_type=MESH)

    def pass_on(way, slot, piece):
        rows_copy(way, slot, piece, held.at[piece_at(slot, piece)]).start()

    def wait_rows(slot, piece):
        here = held.at[piece_at(slot, piece)]
        pltpu.make_async_remote_copy(
            src_ref=here, dst_ref=here, send_sem=mate_send.at[piece],
            recv_sem=rows_recv.at[slot, piece], device_id={"tensor": mate},
            device_id_type=MESH).wait_recv()

    own_cols = pl.ds(pl.multiple_of(side * half, half), half)
    mate_half = pl.ds(pl.multiple_of((1 - side) * half, half), half)

    def own_piece(piece):
        return hidden_ref.at[piece * piece_rows:(piece + 1) * piece_rows, own_cols]

    to_mate = [
        pltpu.make_async_remote_copy(
            src_ref=hidden_ref.at[piece * piece_rows:(piece + 1) * piece_rows, mate_half],
            dst_ref=held.at[piece_at(me, piece)], send_sem=mate_send.at[piece],
            recv_sem=rows_recv.at[me, piece], device_id={"tensor": mate}, device_id_type=MESH)
        for piece in range(PIECES)
    ]
    to_mate[0].start()
    for piece in range(PIECES):
        @pl.when(has_up & jnp.logical_not(helper & (end_way == 0) & (piece == last)))
        def _():
            rows_copy(0, me, piece, own_piece(piece)).start()

        @pl.when(has_down & jnp.logical_not(helper & (end_way == 1) & (piece == last)))
        def _():
            rows_copy(1, me, piece, own_piece(piece)).start()

    own_at = pl.ds(pl.multiple_of(side * cut, head_width), query_cols)
    mate_at = pl.ds(pl.multiple_of((1 - side) * cut, head_width), query_cols)
    quarter = half // 4
    strip = quarter // STRIPS
    half_rows = pl.ds(pl.multiple_of(side * half, half), half)
    loads = [
        pltpu.make_async_copy(
            hidden_ref.at[:, own_cols], held.at[pl.ds(pl.multiple_of(me * rows, rows), rows)],
            load_sem.at[0]),
        pltpu.make_async_copy(
            key_ref, weights.at[:, pl.ds(query_cols, head_width)], load_sem.at[1]),
        pltpu.make_async_copy(
            value_ref, weights.at[:, pl.ds(cut + query_cols, head_width)], load_sem.at[2]),
        pltpu.make_async_copy(
            query_ref.at[half_rows], weights.at[:, own_at], load_sem.at[3]),
    ]
    for load in loads:
        load.start()

    def strip_at(quarter_of, index):
        start = quarter_of * quarter + index * strip
        return pl.ds(pl.multiple_of(start, strip), strip)

    here_quarter = group * 2 + core
    cross_quarter = (1 - group) * 2 + core

    def wide_copy(index):
        start = (1 - side) * half + here_quarter * quarter + index * strip
        return pltpu.make_async_remote_copy(
            src_ref=query_ref.at[pl.ds(pl.multiple_of(start, strip), strip)],
            dst_ref=weights.at[strip_at(here_quarter, index), own_at],
            send_sem=wide_send.at[index], recv_sem=wide_recv.at[index],
            device_id={"tensor": mate}, device_id_type=MESH)

    def weight_copy(quarter_of, index, send, recv, device):
        here = weights.at[strip_at(quarter_of, index), mate_at]
        return pltpu.make_async_remote_copy(
            src_ref=here, dst_ref=here, send_sem=send.at[index], recv_sem=recv.at[index],
            device_id=device, device_id_type=MESH)

    def core_copy(index):
        return weight_copy(here_quarter, index, core_send, core_recv, {"dp": 1 - core})

    def cross_copy(index):
        return weight_copy(here_quarter, index, cross_send, cross_recv, {"groups": 1 - group})

    def hand_copy(index):
        return weight_copy(cross_quarter, index, hand_send, hand_recv, {"dp": 1 - core})

    live = lengths_ref[0]

    @pl.loop(0, count)
    def _(slot):
        here = pl.ds(pl.multiple_of(slot * rows, rows), rows)
        position = slot * rows + lax.broadcasted_iota(jnp.int32, (rows, head_width), 0)
        for head in range(heads):
            gradient = gradient_ref[here, head * head_width:(head + 1) * head_width]
            staged[slot, head * rows:(head + 1) * rows, :] = jnp.where(
                position < live, gradient.astype(jnp.float32), 0.0).astype(jnp.bfloat16)

    for piece in range(PIECES):
        if piece < last:
            to_mate[piece].wait_send()
            to_mate[piece + 1].start()
        wait_rows(mate, piece)

        @pl.when(has_up & jnp.logical_not(helper & (end_way == 0) & (piece == last)))
        def _():
            pass_on(0, mate, piece)

        @pl.when(has_down & jnp.logical_not(helper & (end_way == 1) & (piece == last)))
        def _():
            pass_on(1, mate, piece)

    for index in range(STRIPS):
        wide_copy(index).start()
    for load in loads:
        load.wait()

    quarter_cols = 2 * quarter
    near_cols = pl.ds(pl.multiple_of(group * quarter_cols, quarter_cols), quarter_cols)
    cross_cols = pl.ds(pl.multiple_of((1 - group) * quarter_cols, quarter_cols), quarter_cols)
    aided = (2 * place, 2 * place + 1)

    def part_at(part):
        return pl.ds(pl.multiple_of(part * cut, head_width), cut)

    def aid_rows(of_core, index):
        start = of_core * quarter + index * strip
        return pl.ds(pl.multiple_of(start, strip), strip)

    def aid_copy(turn, part, index):
        return pltpu.make_async_remote_copy(
            src_ref=weights.at[strip_at(here_quarter, index), part_at(part)],
            dst_ref=aid_weights.at[aid_rows(core, index), part_at(part)],
            send_sem=aid_send.at[turn, index], recv_sem=aid_recv.at[turn, index],
            device_id={"tensor": 2 * near + side}, device_id_type=MESH)

    def aid_core_copy(turn, part, index):
        here = aid_weights.at[aid_rows(core, index), part_at(part)]
        return pltpu.make_async_remote_copy(
            src_ref=here, dst_ref=here, send_sem=aid_core_send.at[turn, index],
            recv_sem=aid_core_recv.at[turn, index], device_id={"dp": 1 - core},
            device_id_type=MESH)

    def guest_copy(which):
        return pltpu.make_async_remote_copy(
            src_ref=held.at[piece_at(aided[which], last), cross_cols], dst_ref=guest.at[which],
            send_sem=guest_send.at[which], recv_sem=guest_recv.at[which],
            device_id={"groups": 1 - group}, device_id_type=MESH)

    def return_copy(turn, part, which):
        return pltpu.make_async_remote_copy(
            src_ref=guest_partial.at[which, :, part_at(part)],
            dst_ref=aid_cross.at[which, :, part_at(part)],
            send_sem=return_send.at[turn, which], recv_sem=return_recv.at[turn, which],
            device_id={"groups": 1 - group}, device_id_type=MESH)

    def aid_sum_copy(part, which):
        return pltpu.make_async_remote_copy(
            src_ref=aid_partial.at[which, :, part_at(part)],
            dst_ref=aid_other.at[which, :, part_at(part)],
            send_sem=aid_sum_send.at[part, which], recv_sem=aid_sum_recv.at[part, which],
            device_id={"tensor": mate}, device_id_type=MESH)

    def gift_copies(which):
        slot = aided[which]
        to_end = {"tensor": me + 2 - 4 * end_way}
        rows_there = pl.ds(last * piece_rows, piece_rows)
        return [
            pltpu.make_async_remote_copy(
                src_ref=gift.at[which, part], dst_ref=queries.at[part, slot, :, rows_there],
                send_sem=gift_send.at[which, part], recv_sem=gift_recv.at[which, part],
                device_id=to_end, device_id_type=MESH)
            for part in range(2)
        ] + [
            pltpu.make_async_remote_copy(
                src_ref=gift_pairs.at[which], dst_ref=pairs.at[piece_at(slot, last)],
                send_sem=gift_send.at[which, 2], recv_sem=gift_recv.at[which, 2],
                device_id=to_end, device_id_type=MESH),
        ]

    @pl.when(helper)
    def _():
        for which in range(2):
            guest_copy(which).start()

    def slot_of(distance, which, way):
        plane = place - distance + 2 * distance * way
        turned = side + which - 2 * side * which
        return plane, 2 * plane + turned

    def receive(distance, which):
        @pl.loop(0, 2 * PIECES)
        def _(step):
            piece = lax.div(step, 2)
            way = lax.rem(step, 2)
            plane, slot = slot_of(distance, which, way)

            @pl.when((plane >= 0) & (plane < chain) & jnp.logical_not(helped(slot, piece)))
            def _():
                wait_rows(slot, piece)

                @pl.when((place + 1 - 2 * way >= 0) & (place + 1 - 2 * way < chain))
                def _():
                    pass_on(way, slot, piece)

    def partial_copy(slot, piece, part):
        here = piece_at(slot, piece)
        columns = pl.ds(part * cut, cut)
        return pltpu.make_async_remote_copy(
            src_ref=partial.at[here, columns], dst_ref=other.at[here, columns],
            send_sem=partial_send.at[slot, piece, part],
            recv_sem=partial_recv.at[slot, piece, part],
            device_id={"tensor": mate}, device_id_type=MESH)

    def project(slot, piece):
        here = piece_at(slot, piece)
        for part in range(2):
            columns = slice(part * cut, (part + 1) * cut)
            partial[here, columns] = jnp.dot(
                held[here], weights[:, columns], preferred_element_type=jnp.float32)

            @pl.when(jnp.logical_not(sums))
            def _():
                partial_copy(slot, piece, part).start()

    def project_whole(slot):
        here = pl.ds(pl.multiple_of(slot * rows, rows), rows)
        for part in range(2):
            columns = slice(part * cut, (part + 1) * cut)
            partial[here, columns] = jnp.dot(
                held[here], weights[:, columns], preferred_element_type=jnp.float32)

            @pl.when(jnp.logical_not(sums))
            def _():
                for piece in range(PIECES):
                    partial_copy(slot, piece, part).start()

    def project_step(distance, which):
        @pl.loop(0, 2)
        def _(way):
            plane, slot = slot_of(distance, which, way)
            inside = (plane >= 0) & (plane < chain)

            @pl.when(inside & jnp.logical_not(end & (plane == near)))
            def _():
                project_whole(slot)

            @pl.when(inside & end & (plane == near))
            def _():
                for piece in range(last):
                    project(slot, piece)

    def share_copy(slot, piece):
        here = queries.at[
            1 - core, slot, :, pl.ds(pl.multiple_of(piece * piece_rows, piece_rows), piece_rows)]
        return pltpu.make_async_remote_copy(
            src_ref=here, dst_ref=here, send_sem=share_send.at[slot, piece],
            recv_sem=share_recv.at[slot, piece], device_id={"dp": 1 - core}, device_id_type=MESH)

    def pair_copy(slot, piece):
        here = pairs.at[piece_at(slot, piece)]
        return pltpu.make_async_remote_copy(
            src_ref=here, dst_ref=here, send_sem=pair_send.at[slot, piece],
            recv_sem=pair_recv.at[slot, piece], device_id={"dp": 1 - core}, device_id_type=MESH)

    key_at = slice(query_cols, cut)
    value_at = slice(cut + query_cols, 2 * cut)

    def turner(here):
        cosine, sine = cosine_sine(table_ref[here, :])

        def turn(mixed):
            return (mixed * cosine + swap_halves(mixed) * sine).astype(jnp.bfloat16)

        return turn

    def head_at(part, head):
        start = part * cut + head * head_width
        return slice(start, start + head_width)

    def finish(slot, piece):
        for part in range(2):
            partial_copy(slot, piece, part).wait_recv()
        here = piece_at(slot, piece)
        there = pl.ds(pl.multiple_of(piece * piece_rows, piece_rows), piece_rows)
        turn = turner(here)
        for part in range(2):
            for head in range(heads):
                columns = head_at(part, head)
                queries[part, slot, head, there, :] = turn(
                    partial[here, columns] + other[here, columns])
        pairs[here, :head_width] = turn(partial[here, key_at] + other[here, key_at])
        pairs[here, head_width:] = (
            partial[here, value_at] + other[here, value_at]).astype(jnp.bfloat16)
        share_copy(slot, piece).start()
        pair_copy(slot, piece).start()

    def finish_step(distance, which):
        @pl.loop(0, 2 * PIECES)
        def _(step):
            piece = lax.div(step, 2)
            way = lax.rem(step, 2)
            plane, slot = slot_of(distance, which, way)
            inside = (plane >= 0) & (plane < chain)

            @pl.when(sums & inside & jnp.logical_not(helped(slot, piece)))
            def _():
                finish(slot, piece)

    def aid(turn):
        part = side + turn - 2 * side * turn
        for index in range(STRIPS):
            aid_copy(turn, part, index).wait_recv()
            aid_core_copy(turn, part, index).start()
        for index in range(STRIPS):
            aid_core_copy(turn, part, index).wait_recv()
        for which in range(2):
            guest_partial[which, :, part_at(part)] = jnp.dot(
                guest[which], aid_weights[:, part_at(part)], preferred_element_type=jnp.float32)
            return_copy(turn, part, which).start()
        for which in range(2):
            aid_partial[which, :, part_at(part)] = jnp.dot(
                held[piece_at(aided[which], last), near_cols], aid_weights[:, part_at(part)],
                preferred_element_type=jnp.float32)

    def aid_sum(turn):
        part = side + turn - 2 * side * turn
        for which in range(2):
            return_copy(turn, part, which).wait_recv()
            aid_partial[which, :, part_at(part)] += aid_cross[which, :, part_at(part)]

            @pl.when(jnp.logical_not(sums))
            def _():
                aid_sum_copy(part, which).start()

    def aid_finish(which):
        for part in range(2):
            aid_sum_copy(part, which).wait_recv()
        turn = turner(piece_at(aided[which], last))
        for part in range(2):
            for head in range(heads):
                columns = head_at(part, head)
                gift[which, part, head] = turn(
                    aid_partial[which, :, columns] + aid_other[which, :, columns])
        gift_pairs[which, :, :head_width] = turn(
            aid_partial[which, :, key_at] + aid_other[which, :, key_at])
        gift_pairs[which, :, head_width:] = (
            aid_partial[which, :, value_at] + aid_other[which, :, value_at]).astype(jnp.bfloat16)
        for copy in gift_copies(which):
            copy.start()

    receive(1, 0)
    for index in range(STRIPS):
        wide_copy(index).wait_recv()
        core_copy(index).start()
        cross_copy(index).start()
    keep_above = pltpu.make_async_copy(staged, upstream, above_keep)
    send_above = pltpu.make_async_remote_copy(
        src_ref=staged, dst_ref=upstream, send_sem=above_send, recv_sem=above_recv,
        device_id={"tensor": mate, "dp": 1 - core}, device_id_type=MESH)

    @pl.when(sums)
    def _():
        keep_above.start()

    @pl.when(jnp.logical_not(sums))
    def _():
        send_above.start()

    receive(1, 1)

    @pl.when(end)
    def _():
        for turn in range(2):
            part = side + turn - 2 * side * turn
            for index in range(STRIPS):
                aid_copy(turn, part, index).start()

    for index in range(STRIPS):
        cross_copy(index).wait_recv()
        hand_copy(index).start()
    for index in range(STRIPS):
        core_copy(index).wait_recv()
    for index in range(STRIPS):
        hand_copy(index).wait_recv()

    @pl.loop(0, 2)
    def _(which):
        project_whole(2 * place + which)

    receive(2, 0)

    @pl.loop(0, 2)
    def _(which):
        project_step(1, which)

    @pl.when(sums)
    def _():
        @pl.loop(0, 2 * PIECES)
        def _(step):
            finish(2 * place + lax.rem(step, 2), lax.div(step, 2))

    receive(2, 1)
    project_step(2, 0)

    @pl.when(helper)
    def _():
        for which in range(2):
            guest_copy(which).wait_recv()
        aid(0)

    project_step(2, 1)

    @pl.when(helper)
    def _():
        for slot in aided:
            pass_on(end_way, slot, last)

    @pl.when(helper)
    def _():
        aid_sum(0)
        aid(1)
        aid_sum(1)

    @pl.loop(2, 6)
    def _(step):
        finish_step(lax.div(step, 2), lax.rem(step, 2))

    @pl.when(helper & sums)
    def _():
        for which in range(2):
            aid_finish(which)

    @pl.loop(6, 2 * chain)
    def _(step):
        @pl.loop(0, PIECES)
        def _(piece):
            for way in range(2):
                plane, slot = slot_of(lax.div(step, 2), lax.rem(step, 2), way)

                @pl.when((plane >= 0) & (plane < chain))
                def _():
                    wait_rows(slot, piece)
                    project(slot, piece)

        @pl.when(step == 2 * chain - 1)
        def _():
            finish_step(chain - 1, 0)

    finish_step(chain - 1, 1)

    near_slots = (2 * near, 2 * near + 1)

    @pl.when(end & sums)
    def _():
        for which in range(2):
            rows_there = pl.ds(last * piece_rows, piece_rows)
            mine = [queries.at[part, near_slots[which], :, rows_there] for part in range(2)]
            pair = pairs.at[piece_at(near_slots[which], last)]
            for index, here in enumerate(mine + [pair]):
                pltpu.make_async_remote_copy(
                    src_ref=here, dst_ref=here, send_sem=gift_send.at[which, index],
                    recv_sem=gift_recv.at[which, index], device_id={"tensor": mate},
                    device_id_type=MESH).wait_recv()
            share_copy(near_slots[which], last).start()
            pair_copy(near_slots[which], last).start()

    scale = 1.0 / math.sqrt(head_width)
    blocks = count

    def grad_copy(block):
        return pltpu.make_async_remote_copy(
            src_ref=grads.at[block], dst_ref=peer_grads.at[block],
            send_sem=grad_send.at[block], recv_sem=grad_recv.at[block],
            device_id={"dp": 1 - core}, device_id_type=MESH)

    def rows_of(block):
        return slice(block * rows, (block + 1) * rows)

    def near_copy(block):
        here = rows_of(block)
        return pltpu.make_async_remote_copy(
            src_ref=made.at[here], dst_ref=rounded.at[here],
            send_sem=near_send.at[block], recv_sem=final_recv.at[block],
            device_id={"dp": 1 - core}, device_id_type=MESH)

    def far_copy(block):
        here = rows_of(block)
        return pltpu.make_async_remote_copy(
            src_ref=made.at[here], dst_ref=rounded.at[here],
            send_sem=far_send.at[block], recv_sem=final_recv.at[block],
            device_id={"tensor": mate, "dp": side}, device_id_type=MESH)

    def sum_up(block):
        @pl.when(core == block % 2)
        def _():
            grad_copy(block).wait_recv()
            here = rows_of(block)
            cosine, sine = cosine_sine(table_ref[here, :])
            key_grad = grads[block, :, :head_width] + peer_grads[block, :, :head_width]
            key_grad = key_grad * cosine - swap_halves(key_grad) * sine
            key_grad = key_grad.astype(jnp.bfloat16)
            value_grad = (
                grads[block, :, head_width:] + peer_grads[block, :, head_width:]
            ).astype(jnp.bfloat16)
            made[here, :head_width] = key_grad
            made[here, head_width:] = value_grad
            far_copy(block).start()

            @pl.when(sums)
            def _():
                rounded[here, :head_width] = key_grad
                rounded[here, head_width:] = value_grad

            @pl.when(jnp.logical_not(sums))
            def _():
                near_copy(block).start()

    wide = heads * rows
    contract_last = (((1,), (1,)), ((), ()))
    @pl.when(sums)
    def _():
        keep_above.wait()

    @pl.when(jnp.logical_not(sums))
    def _():
        send_above.wait_recv()

        @pl.loop(0, count * PIECES)
        def _(step):
            share_copy(lax.div(step, PIECES), lax.rem(step, PIECES)).wait_recv()
            pair_copy(lax.div(step, PIECES), lax.rem(step, PIECES)).wait_recv()

    for block in reversed(range(blocks)):
        extent = (block + 1) * rows
        query = queries[core, block].reshape(wide, head_width)
        above = upstream[block]
        scores = lax.dot_general(
            pairs[:extent, :head_width], query, contract_last, preferred_element_type=jnp.float32)
        key_at = lax.broadcasted_iota(jnp.int32, (rows, wide), 0)
        query_at = lax.rem(lax.broadcasted_iota(jnp.int32, (rows, wide), 1), rows)
        corner = jnp.where(key_at <= query_at, scores[extent - rows:], far_below)
        if block > 0:
            scores = jnp.concatenate([scores[:extent - rows], corner], axis=0)
        else:
            scores = corner
        peak = jnp.max(scores, axis=0, keepdims=True)
        powers = jnp.exp2((scores - peak) * (scale * math.log2(math.e)))
        prob = powers * (1.0 / jnp.sum(powers, axis=0, keepdims=True))
        dprob = lax.dot_general(
            pairs[:extent, head_width:], above, contract_last, preferred_element_type=jnp.float32)
        row_dot = jnp.sum(prob * dprob, axis=0, keepdims=True)
        dscore = (prob * (dprob - row_dot) * scale).astype(jnp.bfloat16)
        key_part = jnp.dot(dscore, query, preferred_element_type=jnp.float32)
        value_part = jnp.dot(prob.astype(jnp.bfloat16), above, preferred_element_type=jnp.float32)
        key_part = key_part.reshape(block + 1, rows, head_width)
        value_part = value_part.reshape(block + 1, rows, head_width)
        if block == blocks - 1:
            grads[:, :, :head_width] = key_part
            grads[:, :, head_width:] = value_part
        else:
            grads[:block + 1, :, :head_width] += key_part
            grads[:block + 1, :, head_width:] += value_part

        @pl.when(core != block % 2)
        def _():
            grad_copy(block).start()

        if block + 3 < blocks:
            sum_up(block + 3)

    for block in reversed(range(min(3, blocks))):
        sum_up(block)
    for block in reversed(range(blocks)):
        @pl.when(jnp.logical_not(sums & (core == block % 2)))
        def _():
            far_copy(block).wait_recv()

    @pl.when(end)
    def _():
        for slot in near_slots:
            wait_rows(slot, last)

    share = half // 2
    tiles = share // TILE

    def squares_of(start):
        columns = pl.ds(pl.multiple_of(start, TILE), TILE)
        sample = lax.dot_general(
            held[:, columns], rounded[...], (((0,), (0,)), ((), ())),
            preferred_element_type=jnp.float32)
        return sample * sample

    def square_copy(index):
        here = pl.ds(pl.multiple_of(index * TILE, TILE), TILE)
        return pltpu.make_async_remote_copy(
            src_ref=send_squares.at[here], dst_ref=peer_squares.at[here],
            send_sem=square_send.at[index], recv_sem=square_recv.at[index],
            device_id={"dp": 1 - core}, device_id_type=MESH)

    @pl.loop(0, tiles)
    def _(index):
        here = pl.ds(pl.multiple_of(index * TILE, TILE), TILE)
        send_squares[here, :] = squares_of((1 - core) * share + index * TILE)
        square_copy(index).start()

    @pl.loop(0, tiles)
    def _(index):
        here = pl.ds(pl.multiple_of(index * TILE, TILE), TILE)
        squares = squares_of(core * share + index * TILE)
        square_copy(index).wait_recv()
        squares = squares + peer_squares[here, :]
        key_out[here, :] = squares[:, :head_width]
        value_out[here, :] = squares[:, head_width:]

    to_mate[last].wait_send()
    for index in range(STRIPS):
        wide_copy(index).wait_send()
        core_copy(index).wait_send()
        cross_copy(index).wait_send()
        hand_copy(index).wait_send()

    @pl.loop(0, count * PIECES)
    def _(step):
        slot = lax.div(step, PIECES)
        piece = lax.rem(step, PIECES)

        @pl.when(jnp.logical_not(sums) & jnp.logical_not(helped(slot, piece)))
        def _():
            for part in range(2):
                partial_copy(slot, piece, part).wait_send()

        origin = lax.div(slot, 2)

        @pl.when(has_up & (origin <= place))
        def _():
            rows_copy(0, slot, piece, held.at[piece_at(slot, piece)]).wait_send()

        @pl.when(has_down & (origin >= place))
        def _():
            rows_copy(1, slot, piece, held.at[piece_at(slot, piece)]).wait_send()

    @pl.when(sums)
    def _():
        @pl.loop(0, count * PIECES)
        def _(step):
            share_copy(lax.div(step, PIECES), lax.rem(step, PIECES)).wait_send()
            pair_copy(lax.div(step, PIECES), lax.rem(step, PIECES)).wait_send()

        @pl.when(helper)
        def _():
            for which in range(2):
                for copy in gift_copies(which):
                    copy.wait_send()

    @pl.when(jnp.logical_not(sums))
    def _():
        send_above.wait_send()

        @pl.when(helper)
        def _():
            for which in range(2):
                for part in range(2):
                    aid_sum_copy(part, which).wait_send()

    @pl.when(helper)
    def _():
        for which in range(2):
            guest_copy(which).wait_send()
        for turn in range(2):
            part = side + turn - 2 * side * turn
            for which in range(2):
                return_copy(turn, part, which).wait_send()
            for index in range(STRIPS):
                aid_core_copy(turn, part, index).wait_send()

    @pl.when(end)
    def _():
        for turn in range(2):
            part = side + turn - 2 * side * turn
            for index in range(STRIPS):
                aid_copy(turn, part, index).wait_send()

    for block in range(blocks):
        @pl.when(core != block % 2)
        def _():
            grad_copy(block).wait_send()

        @pl.when(core == block % 2)
        def _():
            far_copy(block).wait_send()

            @pl.when(jnp.logical_not(sums))
            def _():
                near_copy(block).wait_send()

    @pl.loop(0, tiles)
    def _(index):
        square_copy(index).wait_send()


PIECES = 2
STRIPS = 4
TILE = 512


def fused(lengths, head_grad, table, hidden, query_weight, key_weight, value_weight):
    count = lax.axis_size("tensor")
    rows, model_width = hidden.shape
    length = rows * count
    half = model_width // 2
    query_cols = query_weight.shape[1]
    head_width = key_weight.shape[1]
    pair_cols = 2 * head_width
    all_cols = 2 * (query_cols + head_width)
    heads = query_cols // head_width
    share = half // 2
    dma = pltpu.SemaphoreType.DMA
    anywhere = pl.BlockSpec(memory_space=pl.ANY)
    here = pl.BlockSpec(memory_space=pltpu.VMEM)
    out = jax.ShapeDtypeStruct((share, head_width), jnp.float32)
    return pl.pallas_call(
        functools.partial(fused_kernel, count),
        out_shape=(out, out),
        in_specs=[pl.BlockSpec(memory_space=pltpu.SMEM)] + [here] * 2 + [anywhere] * 4,
        out_specs=(here, here),
        scratch_shapes=[
            pltpu.VMEM((length, half), jnp.bfloat16),
            pltpu.VMEM((half, all_cols), jnp.bfloat16),
            pltpu.VMEM((length, all_cols), jnp.float32),
            pltpu.VMEM((length, all_cols), jnp.float32),
            pltpu.VMEM((2, count, heads, rows, head_width), jnp.bfloat16),
            pltpu.VMEM((length, pair_cols), jnp.bfloat16),
            pltpu.VMEM((count, heads * rows, head_width), jnp.bfloat16),
            pltpu.VMEM((count, heads * rows, head_width), jnp.bfloat16),
            pltpu.VMEM((count, rows, pair_cols), jnp.float32),
            pltpu.VMEM((count, rows, pair_cols), jnp.float32),
            pltpu.VMEM((length, pair_cols), jnp.bfloat16),
            pltpu.VMEM((length, pair_cols), jnp.bfloat16),
            pltpu.VMEM((share, pair_cols), jnp.float32),
            pltpu.VMEM((share, pair_cols), jnp.float32),
            pltpu.VMEM((half // 2, all_cols), jnp.bfloat16),
            pltpu.VMEM((2, rows // PIECES, half // 2), jnp.bfloat16),
            pltpu.VMEM((2, rows // PIECES, all_cols), jnp.float32),
            pltpu.VMEM((2, rows // PIECES, all_cols), jnp.float32),
            pltpu.VMEM((2, rows // PIECES, all_cols), jnp.float32),
            pltpu.VMEM((2, rows // PIECES, all_cols), jnp.float32),
            pltpu.VMEM((2, 2, heads, rows // PIECES, head_width), jnp.bfloat16),
            pltpu.VMEM((2, rows // PIECES, pair_cols), jnp.bfloat16),
            dma((count, PIECES)), dma((2, count, PIECES)), dma((PIECES,)), dma((4,)),
            dma((STRIPS,)), dma((STRIPS,)), dma((STRIPS,)), dma((STRIPS,)),
            dma((STRIPS,)), dma((STRIPS,)), dma((STRIPS,)), dma((STRIPS,)),
            dma((count, PIECES, 2)), dma((count, PIECES, 2)),
            dma((count, PIECES)), dma((count, PIECES)), dma((count, PIECES)), dma((count, PIECES)),
            dma, dma, dma,
            dma((count,)), dma((count,)), dma((count,)), dma((count,)), dma((count,)),
            dma((share // TILE,)), dma((share // TILE,)),
            dma((2, STRIPS)), dma((2, STRIPS)), dma((2, STRIPS)), dma((2, STRIPS)),
            dma((2,)), dma((2,)), dma((2, 2)), dma((2, 2)), dma((2, 2)), dma((2, 2)),
            dma((2, 3)), dma((2, 3)),
        ],
        compiler_params=pltpu.CompilerParams(
            collective_id=2, has_side_effects=True, vmem_limit_bytes=58 * 2**20),
    )(lengths, head_grad, table, hidden, query_weight, key_weight, value_weight)


def local(hidden, query_weight, key_weight, value_weight, head_grad, lengths):
    head_width = key_weight.shape[2]
    length = head_grad.shape[1]
    table = jnp.asarray(turn_table(length, head_width))
    if lax.axis_size("groups") == 2 and lax.axis_size("dp") == 2 and lax.axis_size("tensor") == 8:
        fisher_key, fisher_value = fused(
            lengths, head_grad[0], table, hidden[0], query_weight, key_weight[0], value_weight[0])
        return (fisher_key[None], fisher_value[None])
    half_rows, queries, pairs, upstream = gather_project(
        lengths, head_grad[0], table, hidden[0], query_weight, key_weight[0], value_weight[0]
    )
    own, peer = attend(
        queries, upstream, pairs.reshape(length, -1), table, half_rows.reshape(length, -1),
        head_width,
    )
    fisher_key = own[:1] + jnp.sum(peer[:, :1], axis=0)
    fisher_value = own[1:] + jnp.sum(peer[:, 1:], axis=0)
    return (fisher_key, fisher_value)


def solution(mesh):
    in_specs = (
        P(("groups", "dp"), "tensor", None),
        P(None, "tensor"),
        P("tensor", None, None),
        P("tensor", None, None),
        P(("groups", "dp"), None, "tensor"),
        P(("groups", "dp")),
    )
    out_specs = (P(("groups", "tensor"), "dp", None), P(("groups", "tensor"), "dp", None))
    return jax.shard_map(local, mesh=mesh, in_specs=in_specs, out_specs=out_specs, check_vma=False)
```

```python
import functools
import math

import jax
import jax.numpy as jnp
import numpy as np
from jax import lax
from jax.experimental import pallas as pl
from jax.experimental.pallas import tpu as pltpu
from jax.sharding import PartitionSpec as P

MESH = pl.DeviceIdType.MESH

rope_base = 1000000.0
far_below = -1e30


def turn_table(length, head_width):
    position = np.arange(length, dtype=np.float64)[:, None]
    frequency = rope_base ** (-2.0 * np.arange(head_width // 2, dtype=np.float64) / head_width)
    angles = position * frequency
    return np.concatenate([np.cos(angles), np.sin(angles)], axis=-1).astype(np.float32)


def swap_halves(vectors):
    return pltpu.roll(vectors, vectors.shape[-1] // 2, axis=1)


def cosine_sine(table):
    other = swap_halves(table)
    lead = lax.broadcasted_iota(jnp.int32, table.shape, 1) < table.shape[1] // 2
    return jnp.where(lead, table, other), jnp.where(lead, -other, table)


def gather_project_kernel(
    count, dp_count, lengths_ref, gradient_ref, table_ref,
    hidden_ref, query_ref, key_ref, value_ref,
    rows_out, queries_out, pairs_out, upstream_out,
    held, weights, partial, other, queries, pairs, upstream,
    rows_recv, up_send, down_send, mate_send, load_sem, weight_send, weight_recv,
    share_send, share_recv, partial_send, partial_recv, rows_store, queries_store, pairs_store,
    upstream_store,
):
    me = lax.axis_index("tensor")
    core = lax.axis_index("dp")
    side = lax.rem(me, 2)
    place = lax.div(me, 2)
    mate = me + 1 - 2 * side
    chain = count // 2
    half = held.shape[2]
    query_cols = query_ref.shape[1]
    head_width = key_ref.shape[1]
    own_cols = query_cols + 2 * head_width
    has_up = place < chain - 1
    has_down = place > 0
    share = half // dp_count

    barrier = pltpu.get_barrier_semaphore()
    pl.semaphore_signal(barrier, inc=1, device_id={"tensor": mate}, device_id_type=MESH)
    for step in range(1, dp_count):
        peer = lax.rem(core + step, dp_count)
        pl.semaphore_signal(barrier, inc=1, device_id={"dp": peer}, device_id_type=MESH)

    @pl.when(has_up)
    def _():
        pl.semaphore_signal(barrier, inc=1, device_id={"tensor": me + 2}, device_id_type=MESH)

    @pl.when(has_down)
    def _():
        pl.semaphore_signal(barrier, inc=1, device_id={"tensor": me - 2}, device_id_type=MESH)

    edges = jnp.where(has_up, 1, 0) + jnp.where(has_down, 1, 0)
    pl.semaphore_wait(barrier, dp_count + edges)

    own_half = hidden_ref.at[:, pl.ds(pl.multiple_of(side * half, half), half)]
    mate_half = hidden_ref.at[:, pl.ds(pl.multiple_of((1 - side) * half, half), half)]

    def up_copy(slot, source):
        return pltpu.make_async_remote_copy(
            src_ref=source, dst_ref=held.at[slot], send_sem=up_send.at[slot],
            recv_sem=rows_recv.at[slot], device_id={"tensor": me + 2}, device_id_type=MESH)

    def down_copy(slot, source):
        return pltpu.make_async_remote_copy(
            src_ref=source, dst_ref=held.at[slot], send_sem=down_send.at[slot],
            recv_sem=rows_recv.at[slot], device_id={"tensor": me - 2}, device_id_type=MESH)

    def wait_rows(slot):
        pltpu.make_async_remote_copy(
            src_ref=held.at[slot], dst_ref=held.at[slot], send_sem=mate_send,
            recv_sem=rows_recv.at[slot], device_id={"tensor": mate}, device_id_type=MESH).wait_recv()

    def store_rows(slot):
        return pltpu.make_async_copy(held.at[slot], rows_out.at[slot], rows_store.at[slot])

    def store_queries(slot):
        return pltpu.make_async_copy(queries.at[slot], queries_out.at[slot], queries_store.at[slot])

    def store_pairs(slot):
        return pltpu.make_async_copy(pairs.at[slot], pairs_out.at[slot], pairs_store.at[slot])

    tile = 256
    pieces = own_cols // tile

    def partial_copy(slot, piece):
        source = pl.ds(pl.multiple_of(query_cols + piece * tile, tile), tile)
        target = pl.ds(pl.multiple_of(piece * tile, tile), tile)
        return pltpu.make_async_remote_copy(
            src_ref=partial.at[slot, :, source], dst_ref=other.at[slot, :, target],
            send_sem=partial_send.at[slot, piece], recv_sem=partial_recv.at[slot, piece],
            device_id={"tensor": mate}, device_id_type=MESH)

    to_mate = pltpu.make_async_remote_copy(
        src_ref=mate_half, dst_ref=held.at[me], send_sem=mate_send,
        recv_sem=rows_recv.at[me], device_id={"tensor": mate}, device_id_type=MESH)
    to_mate.start()

    @pl.when(has_up)
    def _():
        up_copy(me, own_half).start()

    @pl.when(has_down)
    def _():
        down_copy(me, own_half).start()

    half_rows = pl.ds(pl.multiple_of(side * half, half), half)
    loads = [
        pltpu.make_async_copy(own_half, held.at[me], load_sem.at[0]),
        pltpu.make_async_copy(
            query_ref.at[half_rows], weights.at[:, pl.ds(0, query_cols)], load_sem.at[1]),
        pltpu.make_async_copy(
            key_ref, weights.at[:, pl.ds(query_cols, head_width)], load_sem.at[2]),
        pltpu.make_async_copy(
            value_ref, weights.at[:, pl.ds(query_cols + head_width, head_width)], load_sem.at[3]),
    ]
    for load in loads:
        load.start()

    share_rows = pl.ds(pl.multiple_of(core * share, share), share)
    mate_cols = pl.ds(own_cols, query_cols)
    weight_copy = pltpu.make_async_remote_copy(
        src_ref=query_ref.at[pl.ds(pl.multiple_of((1 - side) * half + core * share, share), share)],
        dst_ref=weights.at[share_rows, mate_cols], send_sem=weight_send, recv_sem=weight_recv,
        device_id={"tensor": mate}, device_id_type=MESH)

    live = lengths_ref[0]
    rows = held.shape[1]
    heads = query_cols // head_width

    @pl.loop(0, count)
    def _(slot):
        here = pl.ds(pl.multiple_of(slot * rows, rows), rows)
        position = slot * rows + lax.broadcasted_iota(jnp.int32, (rows, head_width), 0)
        for head in range(heads):
            gradient = gradient_ref[here, head * head_width:(head + 1) * head_width]
            upstream[slot, head * rows:(head + 1) * rows, :] = jnp.where(
                position < live, gradient.astype(jnp.float32), 0.0).astype(jnp.bfloat16)

    store_upstream = pltpu.make_async_copy(upstream, upstream_out, upstream_store)
    store_upstream.start()
    wait_rows(mate)

    @pl.when(has_up)
    def _():
        up_copy(mate, held.at[mate]).start()

    @pl.when(has_down)
    def _():
        down_copy(mate, held.at[mate]).start()

    weight_copy.start()

    def slot_at(step, which):
        return 2 * step + jnp.where(which == 0, side, 1 - side)

    def receive(distance, which):
        below = place - distance
        above = place + distance

        @pl.when(below >= 0)
        def _():
            slot = slot_at(below, which)
            wait_rows(slot)

            @pl.when(has_up)
            def _():
                up_copy(slot, held.at[slot]).start()

        @pl.when(above < chain)
        def _():
            slot = slot_at(above, which)
            wait_rows(slot)

            @pl.when(has_down)
            def _():
                down_copy(slot, held.at[slot]).start()

    def multiply(slot, start):
        columns = pl.ds(pl.multiple_of(start, tile), tile)
        partial[slot, :, columns] = jnp.dot(
            held[slot], weights[:, columns], preferred_element_type=jnp.float32)

    def project_pair(slot):
        store_rows(slot).start()
        multiply(slot, query_cols)

    def send_pair(slot):
        partial_copy(slot, 0).start()

    def project_queries(slot):
        @pl.loop(1, pieces)
        def _(piece):
            multiply(slot, query_cols + piece * tile)
            partial_copy(slot, piece).start()

        @pl.loop(0, query_cols // tile)
        def _(piece):
            multiply(slot, piece * tile)

    def project(slot):
        project_pair(slot)
        send_pair(slot)
        project_queries(slot)

    def project_at(distance, which, action):
        below = place - distance
        above = place + distance

        @pl.when(below >= 0)
        def _():
            action(slot_at(below, which))

        @pl.when(above < chain)
        def _():
            action(slot_at(above, which))

    receive(1, 0)
    receive(1, 1)
    for load in loads:
        load.wait()

    def early(action):
        @pl.loop(0, 2)
        def _(which):
            action(slot_at(place, which))

        @pl.loop(0, 2)
        def _(which):
            project_at(1, which, action)

    early(project_pair)
    weight_copy.wait_recv()
    shares = []
    for step in range(1, dp_count):
        peer = lax.rem(core + step, dp_count)
        shares.append(pltpu.make_async_remote_copy(
            src_ref=weights.at[share_rows, mate_cols], dst_ref=weights.at[share_rows, mate_cols],
            send_sem=share_send.at[step - 1], recv_sem=share_recv.at[step - 1],
            device_id={"dp": peer}, device_id_type=MESH))
    for copy in shares:
        copy.start()
    early(send_pair)
    for copy in shares:
        copy.wait_recv()
    early(project_queries)

    @pl.loop(4, 2 * chain)
    def _(step):
        distance = lax.div(step, 2)
        which = lax.rem(step, 2)
        receive(distance, which)
        project_at(distance, which, project)

    def finish(slot):
        for piece in range(pieces):
            partial_copy(slot, piece).wait_recv()
        cosine, sine = cosine_sine(table_ref[pl.ds(pl.multiple_of(slot * rows, rows), rows), :])

        def turn(mixed):
            return (mixed * cosine + swap_halves(mixed) * sine).astype(jnp.bfloat16)

        for head in range(heads):
            columns = slice(head * head_width, (head + 1) * head_width)
            shifted = slice((head + 2) * head_width, (head + 3) * head_width)
            queries[slot, head * rows:(head + 1) * rows, :] = turn(
                partial[slot, :, columns] + other[slot, :, shifted])
        pairs[slot, :, :head_width] = turn(
            partial[slot, :, query_cols:query_cols + head_width] + other[slot, :, :head_width])
        pairs[slot, :, head_width:] = (
            partial[slot, :, query_cols + head_width:own_cols]
            + other[slot, :, head_width:2 * head_width]
        ).astype(jnp.bfloat16)
        store_queries(slot).start()
        store_pairs(slot).start()

    @pl.loop(0, 2 * chain)
    def _(step):
        distance = lax.div(step, 2)
        which = lax.rem(step, 2)
        below = place - distance
        above = place + distance

        @pl.when(below >= 0)
        def _():
            finish(slot_at(below, which))

        @pl.when((above < chain) & (distance > 0))
        def _():
            finish(slot_at(above, which))

    store_upstream.wait()
    to_mate.wait_send()
    weight_copy.wait_send()
    for copy in shares:
        copy.wait_send()

    @pl.loop(0, count)
    def _(slot):
        for piece in range(pieces):
            partial_copy(slot, piece).wait_send()
        store_rows(slot).wait()
        store_queries(slot).wait()
        store_pairs(slot).wait()
        origin = lax.div(slot, 2)

        @pl.when(has_up & (origin <= place))
        def _():
            up_copy(slot, held.at[slot]).wait_send()

        @pl.when(has_down & (origin >= place))
        def _():
            down_copy(slot, held.at[slot]).wait_send()


def gather_project(lengths, head_grad, table, hidden, query_weight, key_weight, value_weight):
    count = lax.axis_size("tensor")
    dp_count = lax.axis_size("dp")
    rows, model_width = hidden.shape
    half = model_width // 2
    query_cols = query_weight.shape[1]
    head_width = key_weight.shape[1]
    own_cols = query_cols + 2 * head_width
    all_cols = own_cols + query_cols
    heads = query_cols // head_width
    stack_shape = jax.ShapeDtypeStruct((count, heads * rows, head_width), jnp.bfloat16)
    pair_shape = jax.ShapeDtypeStruct((count, rows, 2 * head_width), jnp.bfloat16)
    dma = pltpu.SemaphoreType.DMA
    anywhere = pl.BlockSpec(memory_space=pl.ANY)
    return pl.pallas_call(
        functools.partial(gather_project_kernel, count, dp_count),
        out_shape=(
            jax.ShapeDtypeStruct((count, rows, half), jnp.bfloat16),
            stack_shape,
            pair_shape,
            stack_shape,
        ),
        in_specs=[pl.BlockSpec(memory_space=pltpu.SMEM)]
        + [pl.BlockSpec(memory_space=pltpu.VMEM)] * 2 + [anywhere] * 4,
        out_specs=(anywhere,) * 4,
        scratch_shapes=[
            pltpu.VMEM((count, rows, half), jnp.bfloat16),
            pltpu.VMEM((half, all_cols), jnp.bfloat16),
            pltpu.VMEM((count, rows, all_cols), jnp.float32),
            pltpu.VMEM((count, rows, own_cols), jnp.float32),
            pltpu.VMEM(stack_shape.shape, jnp.bfloat16),
            pltpu.VMEM(pair_shape.shape, jnp.bfloat16),
            pltpu.VMEM(stack_shape.shape, jnp.bfloat16),
            dma((count,)), dma((count,)), dma((count,)), dma, dma((4,)), dma, dma,
            dma((dp_count - 1,)), dma((dp_count - 1,)),
            dma((count, own_cols // 256)), dma((count, own_cols // 256)),
            dma((count,)), dma((count,)), dma((count,)), dma,
        ],
        compiler_params=pltpu.CompilerParams(
            collective_id=0, has_side_effects=True, vmem_limit_bytes=58 * 2**20),
    )(lengths, head_grad, table, hidden, query_weight, key_weight, value_weight)

def attend_kernel(
    dp_count, head_width, queries, upstream, pairs, table_ref, rows_ref,
    squares_out, peer_out,
    rows, grads, mate_grads, rounded, peer_squares,
    rows_load, grad_send, grad_recv, final_send, final_recv, peer_send, peer_recv,
):
    me = lax.axis_index("tensor")
    core = lax.axis_index("dp")
    side = lax.rem(me, 2)
    mate = me + 1 - 2 * side
    blocks, stacked, _ = queries.shape
    step_rows = head_width
    scale = 1.0 / math.sqrt(head_width)
    share = squares_out.shape[1]
    tile = 256
    tiles = share // tile

    barrier = pltpu.get_barrier_semaphore()
    pl.semaphore_signal(barrier, inc=1, device_id={"tensor": mate}, device_id_type=MESH)
    for step in range(1, dp_count):
        peer = lax.rem(core + step, dp_count)
        pl.semaphore_signal(barrier, inc=1, device_id={"dp": peer}, device_id_type=MESH)

    load = pltpu.make_async_copy(rows_ref, rows, rows_load)
    load.start()
    pl.semaphore_wait(barrier, dp_count)

    def grad_copy(block):
        return pltpu.make_async_remote_copy(
            src_ref=grads.at[block], dst_ref=mate_grads.at[block],
            send_sem=grad_send.at[block], recv_sem=grad_recv.at[block],
            device_id={"tensor": mate}, device_id_type=MESH)

    def rows_of(block):
        return slice(block * step_rows, (block + 1) * step_rows)

    def final_copy(block):
        here = rows_of(block)
        return pltpu.make_async_remote_copy(
            src_ref=rounded.at[here], dst_ref=rounded.at[here],
            send_sem=final_send.at[block], recv_sem=final_recv.at[block],
            device_id={"tensor": mate}, device_id_type=MESH)

    def finish(block):
        @pl.when(side == block % 2)
        def _():
            grad_copy(block).wait_recv()
            here = rows_of(block)
            cosine, sine = cosine_sine(table_ref[here, :])
            key_grad = grads[block, :, :head_width] + mate_grads[block, :, :head_width]
            key_grad = key_grad * cosine - swap_halves(key_grad) * sine
            rounded[here, :head_width] = key_grad.astype(jnp.bfloat16)
            rounded[here, head_width:] = (
                grads[block, :, head_width:] + mate_grads[block, :, head_width:]
            ).astype(jnp.bfloat16)
            final_copy(block).start()

    wide = 2 * head_width
    contract_last = (((1,), (1,)), ((), ()))
    for block in reversed(range(blocks)):
        extent = (block + 1) * step_rows
        for chunk in range(stacked // wide):
            chunk_rows = slice(chunk * wide, (chunk + 1) * wide)
            query = queries[block, chunk_rows, :]
            above = upstream[block, chunk_rows, :]
            scores = lax.dot_general(
                pairs[:extent, :head_width], query, contract_last, preferred_element_type=jnp.float32)
            key_at = lax.broadcasted_iota(jnp.int32, (step_rows, wide), 0)
            query_at = lax.rem(lax.broadcasted_iota(jnp.int32, (step_rows, wide), 1), step_rows)
            corner = jnp.where(key_at <= query_at, scores[extent - step_rows:], far_below)
            if block > 0:
                scores = jnp.concatenate([scores[:extent - step_rows], corner], axis=0)
            else:
                scores = corner
            peak = jnp.max(scores, axis=0, keepdims=True)
            powers = jnp.exp2((scores - peak) * (scale * math.log2(math.e)))
            prob = powers * (1.0 / jnp.sum(powers, axis=0, keepdims=True))
            dprob = lax.dot_general(
                pairs[:extent, head_width:], above, contract_last, preferred_element_type=jnp.float32)
            row_dot = jnp.sum(prob * dprob, axis=0, keepdims=True)
            dscore = (prob * (dprob - row_dot) * scale).astype(jnp.bfloat16)
            key_part = jnp.dot(dscore, query, preferred_element_type=jnp.float32)
            value_part = jnp.dot(
                prob.astype(jnp.bfloat16), above, preferred_element_type=jnp.float32)
            key_part = key_part.reshape(block + 1, step_rows, head_width)
            value_part = value_part.reshape(block + 1, step_rows, head_width)
            if block == blocks - 1 and chunk == 0:
                grads[:, :, :head_width] = key_part
                grads[:, :, head_width:] = value_part
            else:
                grads[:block + 1, :, :head_width] += key_part
                grads[:block + 1, :, head_width:] += value_part
        @pl.when(side != block % 2)
        def _():
            grad_copy(block).start()

        if block + 3 < blocks:
            finish(block + 3)

    for block in reversed(range(min(3, blocks))):
        finish(block)
    for block in reversed(range(blocks)):
        @pl.when(side != block % 2)
        def _():
            final_copy(block).wait_recv()

    load.wait()

    def squares_of(start):
        columns = pl.ds(pl.multiple_of(start, tile), tile)
        sample = lax.dot_general(
            rows[:, columns], rounded[...], (((0,), (0,)), ((), ())),
            preferred_element_type=jnp.float32)
        return sample * sample

    def peer_copy(step, index):
        here = pl.ds(pl.multiple_of(index * tile, tile), tile)
        return pltpu.make_async_remote_copy(
            src_ref=peer_squares.at[step - 1, :, here], dst_ref=peer_out.at[step - 1, :, here],
            send_sem=peer_send.at[step - 1, index], recv_sem=peer_recv.at[step - 1, index],
            device_id={"dp": lax.rem(core + step, dp_count)}, device_id_type=MESH)

    for step in range(1, dp_count):
        @pl.loop(0, tiles)
        def _(index):
            here = pl.ds(pl.multiple_of(index * tile, tile), tile)
            start = lax.rem(core + step, dp_count) * share + index * tile
            squares = squares_of(start)
            peer_squares[step - 1, 0, here, :] = squares[:, :head_width]
            peer_squares[step - 1, 1, here, :] = squares[:, head_width:]
            peer_copy(step, index).start()

    @pl.loop(0, tiles)
    def _(index):
        here = pl.ds(pl.multiple_of(index * tile, tile), tile)
        squares = squares_of(core * share + index * tile)
        squares_out[0, here, :] = squares[:, :head_width]
        squares_out[1, here, :] = squares[:, head_width:]

    for block in range(blocks):
        @pl.when(side != block % 2)
        def _():
            grad_copy(block).wait_send()

        @pl.when(side == block % 2)
        def _():
            final_copy(block).wait_send()
    for step in range(1, dp_count):
        @pl.loop(0, tiles)
        def _(index):
            peer_copy(step, index).wait()


def attend(queries, upstream, pairs, table, half_rows, head_width):
    dp_count = lax.axis_size("dp")
    length, half = half_rows.shape
    blocks = length // head_width
    share = half // dp_count
    wide = 2 * head_width
    dma = pltpu.SemaphoreType.DMA
    here = pl.BlockSpec(memory_space=pltpu.VMEM)
    anywhere = pl.BlockSpec(memory_space=pl.ANY)
    return pl.pallas_call(
        functools.partial(attend_kernel, dp_count, head_width),
        out_shape=(
            jax.ShapeDtypeStruct((2, share, head_width), jnp.float32),
            jax.ShapeDtypeStruct((dp_count - 1, 2, share, head_width), jnp.float32),
        ),
        in_specs=[here] * 4 + [anywhere],
        out_specs=(here, anywhere),
        scratch_shapes=[
            pltpu.VMEM((length, half), jnp.bfloat16),
            pltpu.VMEM((blocks, head_width, wide), jnp.float32),
            pltpu.VMEM((blocks, head_width, wide), jnp.float32),
            pltpu.VMEM((length, wide), jnp.bfloat16),
            pltpu.VMEM((dp_count - 1, 2, share, head_width), jnp.float32),
            dma, dma((blocks,)), dma((blocks,)), dma((blocks,)), dma((blocks,)),
            dma((dp_count - 1, share // 256)), dma((dp_count - 1, share // 256)),
        ],
        compiler_params=pltpu.CompilerParams(
            collective_id=1, has_side_effects=True, vmem_limit_bytes=56 * 2**20),
    )(queries, upstream, pairs, table, half_rows)


def fused_kernel(
    count, lengths_ref, gradient_ref, table_ref, hidden_ref, query_ref, key_ref, value_ref,
    key_out, value_out,
    held, weights, partial, other, queries, pairs, staged, upstream,
    grads, peer_grads, made, rounded, send_squares, peer_squares,
    aid_weights, guest, aid_partial, guest_partial, aid_cross, aid_other, gift, gift_pairs,
    rows_recv, rows_send, mate_send, load_sem,
    wide_send, wide_recv, core_send, core_recv, cross_send, cross_recv, hand_send, hand_recv,
    partial_send, partial_recv, share_send, share_recv, pair_send, pair_recv,
    above_keep, above_send, above_recv, grad_send, grad_recv,
    near_send, far_send, final_recv, square_send, square_recv,
    aid_send, aid_recv, aid_core_send, aid_core_recv, guest_send, guest_recv,
    return_send, return_recv, aid_sum_send, aid_sum_recv, gift_send, gift_recv,
):
    me = lax.axis_index("tensor")
    core = lax.axis_index("dp")
    group = lax.axis_index("groups")
    side = lax.rem(me, 2)
    place = lax.div(me, 2)
    mate = me + 1 - 2 * side
    chain = count // 2
    length, half = held.shape
    rows = length // count
    piece_rows = rows // PIECES
    query_cols = query_ref.shape[1]
    head_width = key_ref.shape[1]
    heads = query_cols // head_width
    cut = query_cols + head_width
    sums = core == side
    has_up = place < chain - 1
    has_down = place > 0

    helper = has_up & has_down
    end = jnp.logical_not(helper)
    end_way = 2 - place
    near = 1 + lax.div(place, chain - 1)
    last = PIECES - 1

    def helped(slot, piece):
        return end & (lax.div(slot, 2) == near) & (piece == last)

    barrier = pltpu.get_barrier_semaphore()
    pl.semaphore_signal(barrier, inc=1, device_id={"tensor": mate}, device_id_type=MESH)
    pl.semaphore_signal(barrier, inc=1, device_id={"dp": 1 - core}, device_id_type=MESH)
    pl.semaphore_signal(
        barrier, inc=1, device_id={"tensor": mate, "dp": 1 - core}, device_id_type=MESH)
    pl.semaphore_signal(barrier, inc=1, device_id={"groups": 1 - group}, device_id_type=MESH)

    @pl.when(has_up)
    def _():
        pl.semaphore_signal(barrier, inc=1, device_id={"tensor": me + 2}, device_id_type=MESH)

    @pl.when(has_down)
    def _():
        pl.semaphore_signal(barrier, inc=1, device_id={"tensor": me - 2}, device_id_type=MESH)

    edges = jnp.where(has_up, 1, 0) + jnp.where(has_down, 1, 0)
    pl.semaphore_wait(barrier, 4 + edges)

    def piece_at(slot, piece):
        return pl.ds(pl.multiple_of(slot * rows + piece * piece_rows, piece_rows), piece_rows)

    def rows_copy(way, slot, piece, source):
        return pltpu.make_async_remote_copy(
            src_ref=source, dst_ref=held.at[piece_at(slot, piece)],
            send_sem=rows_send.at[way, slot, piece], recv_sem=rows_recv.at[slot, piece],
            device_id={"tensor": me + 2 - 4 * way}, device_id_type=MESH)

    def pass_on(way, slot, piece):
        rows_copy(way, slot, piece, held.at[piece_at(slot, piece)]).start()

    def wait_rows(slot, piece):
        here = held.at[piece_at(slot, piece)]
        pltpu.make_async_remote_copy(
            src_ref=here, dst_ref=here, send_sem=mate_send.at[piece],
            recv_sem=rows_recv.at[slot, piece], device_id={"tensor": mate},
            device_id_type=MESH).wait_recv()

    own_cols = pl.ds(pl.multiple_of(side * half, half), half)
    mate_half = pl.ds(pl.multiple_of((1 - side) * half, half), half)

    def own_piece(piece):
        return hidden_ref.at[piece * piece_rows:(piece + 1) * piece_rows, own_cols]

    to_mate = [
        pltpu.make_async_remote_copy(
            src_ref=hidden_ref.at[piece * piece_rows:(piece + 1) * piece_rows, mate_half],
            dst_ref=held.at[piece_at(me, piece)], send_sem=mate_send.at[piece],
            recv_sem=rows_recv.at[me, piece], device_id={"tensor": mate}, device_id_type=MESH)
        for piece in range(PIECES)
    ]
    to_mate[0].start()
    for piece in range(PIECES):
        @pl.when(has_up & jnp.logical_not(helper & (end_way == 0) & (piece == last)))
        def _():
            rows_copy(0, me, piece, own_piece(piece)).start()

        @pl.when(has_down & jnp.logical_not(helper & (end_way == 1) & (piece == last)))
        def _():
            rows_copy(1, me, piece, own_piece(piece)).start()

    own_at = pl.ds(pl.multiple_of(side * cut, head_width), query_cols)
    mate_at = pl.ds(pl.multiple_of((1 - side) * cut, head_width), query_cols)
    quarter = half // 4
    strip = quarter // STRIPS
    half_rows = pl.ds(pl.multiple_of(side * half, half), half)
    loads = [
        pltpu.make_async_copy(
            hidden_ref.at[:, own_cols], held.at[pl.ds(pl.multiple_of(me * rows, rows), rows)],
            load_sem.at[0]),
        pltpu.make_async_copy(
            key_ref, weights.at[:, pl.ds(query_cols, head_width)], load_sem.at[1]),
        pltpu.make_async_copy(
            value_ref, weights.at[:, pl.ds(cut + query_cols, head_width)], load_sem.at[2]),
        pltpu.make_async_copy(
            query_ref.at[half_rows], weights.at[:, own_at], load_sem.at[3]),
    ]
    for load in loads:
        load.start()

    def strip_at(quarter_of, index):
        start = quarter_of * quarter + index * strip
        return pl.ds(pl.multiple_of(start, strip), strip)

    here_quarter = group * 2 + core
    cross_quarter = (1 - group) * 2 + core

    def wide_copy(index):
        start = (1 - side) * half + here_quarter * quarter + index * strip
        return pltpu.make_async_remote_copy(
            src_ref=query_ref.at[pl.ds(pl.multiple_of(start, strip), strip)],
            dst_ref=weights.at[strip_at(here_quarter, index), own_at],
            send_sem=wide_send.at[index], recv_sem=wide_recv.at[index],
            device_id={"tensor": mate}, device_id_type=MESH)

    def weight_copy(quarter_of, index, send, recv, device):
        here = weights.at[strip_at(quarter_of, index), mate_at]
        return pltpu.make_async_remote_copy(
            src_ref=here, dst_ref=here, send_sem=send.at[index], recv_sem=recv.at[index],
            device_id=device, device_id_type=MESH)

    def core_copy(index):
        return weight_copy(here_quarter, index, core_send, core_recv, {"dp": 1 - core})

    def cross_copy(index):
        return weight_copy(here_quarter, index, cross_send, cross_recv, {"groups": 1 - group})

    def hand_copy(index):
        return weight_copy(cross_quarter, index, hand_send, hand_recv, {"dp": 1 - core})

    live = lengths_ref[0]

    @pl.loop(0, count)
    def _(slot):
        here = pl.ds(pl.multiple_of(slot * rows, rows), rows)
        position = slot * rows + lax.broadcasted_iota(jnp.int32, (rows, head_width), 0)
        for head in range(heads):
            gradient = gradient_ref[here, head * head_width:(head + 1) * head_width]
            staged[slot, head * rows:(head + 1) * rows, :] = jnp.where(
                position < live, gradient.astype(jnp.float32), 0.0).astype(jnp.bfloat16)

    for piece in range(PIECES):
        if piece < last:
            to_mate[piece].wait_send()
            to_mate[piece + 1].start()
        wait_rows(mate, piece)

        @pl.when(has_up & jnp.logical_not(helper & (end_way == 0) & (piece == last)))
        def _():
            pass_on(0, mate, piece)

        @pl.when(has_down & jnp.logical_not(helper & (end_way == 1) & (piece == last)))
        def _():
            pass_on(1, mate, piece)

    for index in range(STRIPS):
        wide_copy(index).start()
    for load in loads:
        load.wait()

    quarter_cols = 2 * quarter
    near_cols = pl.ds(pl.multiple_of(group * quarter_cols, quarter_cols), quarter_cols)
    cross_cols = pl.ds(pl.multiple_of((1 - group) * quarter_cols, quarter_cols), quarter_cols)
    aided = (2 * place, 2 * place + 1)

    def part_at(part):
        return pl.ds(pl.multiple_of(part * cut, head_width), cut)

    def aid_rows(of_core, index):
        start = of_core * quarter + index * strip
        return pl.ds(pl.multiple_of(start, strip), strip)

    def aid_copy(turn, part, index):
        return pltpu.make_async_remote_copy(
            src_ref=weights.at[strip_at(here_quarter, index), part_at(part)],
            dst_ref=aid_weights.at[aid_rows(core, index), part_at(part)],
            send_sem=aid_send.at[turn, index], recv_sem=aid_recv.at[turn, index],
            device_id={"tensor": 2 * near + side}, device_id_type=MESH)

    def aid_core_copy(turn, part, index):
        here = aid_weights.at[aid_rows(core, index), part_at(part)]
        return pltpu.make_async_remote_copy(
            src_ref=here, dst_ref=here, send_sem=aid_core_send.at[turn, index],
            recv_sem=aid_core_recv.at[turn, index], device_id={"dp": 1 - core},
            device_id_type=MESH)

    def guest_copy(which):
        return pltpu.make_async_remote_copy(
            src_ref=held.at[piece_at(aided[which], last), cross_cols], dst_ref=guest.at[which],
            send_sem=guest_send.at[which], recv_sem=guest_recv.at[which],
            device_id={"groups": 1 - group}, device_id_type=MESH)

    def return_copy(turn, part, which):
        return pltpu.make_async_remote_copy(
            src_ref=guest_partial.at[which, :, part_at(part)],
            dst_ref=aid_cross.at[which, :, part_at(part)],
            send_sem=return_send.at[turn, which], recv_sem=return_recv.at[turn, which],
            device_id={"groups": 1 - group}, device_id_type=MESH)

    def aid_sum_copy(part, which):
        return pltpu.make_async_remote_copy(
            src_ref=aid_partial.at[which, :, part_at(part)],
            dst_ref=aid_other.at[which, :, part_at(part)],
            send_sem=aid_sum_send.at[part, which], recv_sem=aid_sum_recv.at[part, which],
            device_id={"tensor": mate}, device_id_type=MESH)

    def gift_copies(which):
        slot = aided[which]
        to_end = {"tensor": me + 2 - 4 * end_way}
        rows_there = pl.ds(last * piece_rows, piece_rows)
        return [
            pltpu.make_async_remote_copy(
                src_ref=gift.at[which, part], dst_ref=queries.at[part, slot, :, rows_there],
                send_sem=gift_send.at[which, part], recv_sem=gift_recv.at[which, part],
                device_id=to_end, device_id_type=MESH)
            for part in range(2)
        ] + [
            pltpu.make_async_remote_copy(
                src_ref=gift_pairs.at[which], dst_ref=pairs.at[piece_at(slot, last)],
                send_sem=gift_send.at[which, 2], recv_sem=gift_recv.at[which, 2],
                device_id=to_end, device_id_type=MESH),
        ]

    @pl.when(helper)
    def _():
        for which in range(2):
            guest_copy(which).start()

    def slot_of(distance, which, way):
        plane = place - distance + 2 * distance * way
        turned = side + which - 2 * side * which
        return plane, 2 * plane + turned

    def receive(distance, which):
        @pl.loop(0, 2 * PIECES)
        def _(step):
            piece = lax.div(step, 2)
            way = lax.rem(step, 2)
            plane, slot = slot_of(distance, which, way)

            @pl.when((plane >= 0) & (plane < chain) & jnp.logical_not(helped(slot, piece)))
            def _():
                wait_rows(slot, piece)

                @pl.when((place + 1 - 2 * way >= 0) & (place + 1 - 2 * way < chain))
                def _():
                    pass_on(way, slot, piece)

    def partial_copy(slot, piece, part):
        here = piece_at(slot, piece)
        columns = pl.ds(part * cut, cut)
        return pltpu.make_async_remote_copy(
            src_ref=partial.at[here, columns], dst_ref=other.at[here, columns],
            send_sem=partial_send.at[slot, piece, part],
            recv_sem=partial_recv.at[slot, piece, part],
            device_id={"tensor": mate}, device_id_type=MESH)

    def project(slot, piece):
        here = piece_at(slot, piece)
        for part in range(2):
            columns = slice(part * cut, (part + 1) * cut)
            partial[here, columns] = jnp.dot(
                held[here], weights[:, columns], preferred_element_type=jnp.float32)

            @pl.when(jnp.logical_not(sums))
            def _():
                partial_copy(slot, piece, part).start()

    def project_whole(slot):
        here = pl.ds(pl.multiple_of(slot * rows, rows), rows)
        for part in range(2):
            columns = slice(part * cut, (part + 1) * cut)
            partial[here, columns] = jnp.dot(
                held[here], weights[:, columns], preferred_element_type=jnp.float32)

            @pl.when(jnp.logical_not(sums))
            def _():
                for piece in range(PIECES):
                    partial_copy(slot, piece, part).start()

    def project_step(distance, which):
        @pl.loop(0, 2)
        def _(way):
            plane, slot = slot_of(distance, which, way)
            inside = (plane >= 0) & (plane < chain)

            @pl.when(inside & jnp.logical_not(end & (plane == near)))
            def _():
                project_whole(slot)

            @pl.when(inside & end & (plane == near))
            def _():
                for piece in range(last):
                    project(slot, piece)

    def share_copy(slot, piece):
        here = queries.at[
            1 - core, slot, :, pl.ds(pl.multiple_of(piece * piece_rows, piece_rows), piece_rows)]
        return pltpu.make_async_remote_copy(
            src_ref=here, dst_ref=here, send_sem=share_send.at[slot, piece],
            recv_sem=share_recv.at[slot, piece], device_id={"dp": 1 - core}, device_id_type=MESH)

    def pair_copy(slot, piece):
        here = pairs.at[piece_at(slot, piece)]
        return pltpu.make_async_remote_copy(
            src_ref=here, dst_ref=here, send_sem=pair_send.at[slot, piece],
            recv_sem=pair_recv.at[slot, piece], device_id={"dp": 1 - core}, device_id_type=MESH)

    key_at = slice(query_cols, cut)
    value_at = slice(cut + query_cols, 2 * cut)

    def turner(here):
        cosine, sine = cosine_sine(table_ref[here, :])

        def turn(mixed):
            return (mixed * cosine + swap_halves(mixed) * sine).astype(jnp.bfloat16)

        return turn

    def head_at(part, head):
        start = part * cut + head * head_width
        return slice(start, start + head_width)

    def finish(slot, piece):
        for part in range(2):
            partial_copy(slot, piece, part).wait_recv()
        here = piece_at(slot, piece)
        there = pl.ds(pl.multiple_of(piece * piece_rows, piece_rows), piece_rows)
        turn = turner(here)
        for part in range(2):
            for head in range(heads):
                columns = head_at(part, head)
                queries[part, slot, head, there, :] = turn(
                    partial[here, columns] + other[here, columns])
        pairs[here, :head_width] = turn(partial[here, key_at] + other[here, key_at])
        pairs[here, head_width:] = (
            partial[here, value_at] + other[here, value_at]).astype(jnp.bfloat16)
        share_copy(slot, piece).start()
        pair_copy(slot, piece).start()

    def finish_step(distance, which):
        @pl.loop(0, 2 * PIECES)
        def _(step):
            piece = lax.div(step, 2)
            way = lax.rem(step, 2)
            plane, slot = slot_of(distance, which, way)
            inside = (plane >= 0) & (plane < chain)

            @pl.when(sums & inside & jnp.logical_not(helped(slot, piece)))
            def _():
                finish(slot, piece)

    def aid(turn):
        part = side + turn - 2 * side * turn
        for index in range(STRIPS):
            aid_copy(turn, part, index).wait_recv()
            aid_core_copy(turn, part, index).start()
        for index in range(STRIPS):
            aid_core_copy(turn, part, index).wait_recv()
        for which in range(2):
            guest_partial[which, :, part_at(part)] = jnp.dot(
                guest[which], aid_weights[:, part_at(part)], preferred_element_type=jnp.float32)
            return_copy(turn, part, which).start()
        for which in range(2):
            aid_partial[which, :, part_at(part)] = jnp.dot(
                held[piece_at(aided[which], last), near_cols], aid_weights[:, part_at(part)],
                preferred_element_type=jnp.float32)

    def aid_sum(turn):
        part = side + turn - 2 * side * turn
        for which in range(2):
            return_copy(turn, part, which).wait_recv()
            aid_partial[which, :, part_at(part)] += aid_cross[which, :, part_at(part)]

            @pl.when(jnp.logical_not(sums))
            def _():
                aid_sum_copy(part, which).start()

    def aid_finish(which):
        for part in range(2):
            aid_sum_copy(part, which).wait_recv()
        turn = turner(piece_at(aided[which], last))
        for part in range(2):
            for head in range(heads):
                columns = head_at(part, head)
                gift[which, part, head] = turn(
                    aid_partial[which, :, columns] + aid_other[which, :, columns])
        gift_pairs[which, :, :head_width] = turn(
            aid_partial[which, :, key_at] + aid_other[which, :, key_at])
        gift_pairs[which, :, head_width:] = (
            aid_partial[which, :, value_at] + aid_other[which, :, value_at]).astype(jnp.bfloat16)
        for copy in gift_copies(which):
            copy.start()

    receive(1, 0)
    for index in range(STRIPS):
        wide_copy(index).wait_recv()
        core_copy(index).start()
        cross_copy(index).start()
    keep_above = pltpu.make_async_copy(staged, upstream, above_keep)
    send_above = pltpu.make_async_remote_copy(
        src_ref=staged, dst_ref=upstream, send_sem=above_send, recv_sem=above_recv,
        device_id={"tensor": mate, "dp": 1 - core}, device_id_type=MESH)

    @pl.when(sums)
    def _():
        keep_above.start()

    @pl.when(jnp.logical_not(sums))
    def _():
        send_above.start()

    receive(1, 1)

    @pl.when(end)
    def _():
        for turn in range(2):
            part = side + turn - 2 * side * turn
            for index in range(STRIPS):
                aid_copy(turn, part, index).start()

    for index in range(STRIPS):
        cross_copy(index).wait_recv()
        hand_copy(index).start()
    for index in range(STRIPS):
        core_copy(index).wait_recv()
    for index in range(STRIPS):
        hand_copy(index).wait_recv()

    @pl.loop(0, 2)
    def _(which):
        project_whole(2 * place + which)

    receive(2, 0)

    @pl.loop(0, 2)
    def _(which):
        project_step(1, which)

    @pl.when(sums)
    def _():
        @pl.loop(0, 2 * PIECES)
        def _(step):
            finish(2 * place + lax.rem(step, 2), lax.div(step, 2))

    receive(2, 1)
    project_step(2, 0)

    @pl.when(helper)
    def _():
        for which in range(2):
            guest_copy(which).wait_recv()
        aid(0)

    project_step(2, 1)

    @pl.when(helper)
    def _():
        pass_on(end_way, aided[0], last)

    @pl.when(helper)
    def _():
        aid_sum(0)
        aid(1)
        aid_sum(1)

    @pl.loop(2, 6)
    def _(step):
        finish_step(lax.div(step, 2), lax.rem(step, 2))

    @pl.when(helper & sums)
    def _():
        for which in range(2):
            aid_finish(which)

    @pl.when(helper)
    def _():
        pass_on(end_way, aided[1], last)

    @pl.loop(6, 2 * chain)
    def _(step):
        @pl.loop(0, PIECES)
        def _(piece):
            for way in range(2):
                plane, slot = slot_of(lax.div(step, 2), lax.rem(step, 2), way)

                @pl.when((plane >= 0) & (plane < chain))
                def _():
                    wait_rows(slot, piece)
                    project(slot, piece)

        @pl.when(step == 2 * chain - 1)
        def _():
            finish_step(chain - 1, 0)

    finish_step(chain - 1, 1)

    near_slots = (2 * near, 2 * near + 1)

    @pl.when(end & sums)
    def _():
        for which in range(2):
            rows_there = pl.ds(last * piece_rows, piece_rows)
            mine = [queries.at[part, near_slots[which], :, rows_there] for part in range(2)]
            pair = pairs.at[piece_at(near_slots[which], last)]
            for index, here in enumerate(mine + [pair]):
                pltpu.make_async_remote_copy(
                    src_ref=here, dst_ref=here, send_sem=gift_send.at[which, index],
                    recv_sem=gift_recv.at[which, index], device_id={"tensor": mate},
                    device_id_type=MESH).wait_recv()
            share_copy(near_slots[which], last).start()
            pair_copy(near_slots[which], last).start()

    scale = 1.0 / math.sqrt(head_width)
    blocks = count

    def grad_copy(block):
        return pltpu.make_async_remote_copy(
            src_ref=grads.at[block], dst_ref=peer_grads.at[block],
            send_sem=grad_send.at[block], recv_sem=grad_recv.at[block],
            device_id={"dp": 1 - core}, device_id_type=MESH)

    def rows_of(block):
        return slice(block * rows, (block + 1) * rows)

    def near_copy(block):
        here = rows_of(block)
        return pltpu.make_async_remote_copy(
            src_ref=made.at[here], dst_ref=rounded.at[here],
            send_sem=near_send.at[block], recv_sem=final_recv.at[block],
            device_id={"dp": 1 - core}, device_id_type=MESH)

    def far_copy(block):
        here = rows_of(block)
        return pltpu.make_async_remote_copy(
            src_ref=made.at[here], dst_ref=rounded.at[here],
            send_sem=far_send.at[block], recv_sem=final_recv.at[block],
            device_id={"tensor": mate, "dp": side}, device_id_type=MESH)

    def sum_up(block):
        @pl.when(core == block % 2)
        def _():
            grad_copy(block).wait_recv()
            here = rows_of(block)
            cosine, sine = cosine_sine(table_ref[here, :])
            key_grad = grads[block, :, :head_width] + peer_grads[block, :, :head_width]
            key_grad = key_grad * cosine - swap_halves(key_grad) * sine
            key_grad = key_grad.astype(jnp.bfloat16)
            value_grad = (
                grads[block, :, head_width:] + peer_grads[block, :, head_width:]
            ).astype(jnp.bfloat16)
            made[here, :head_width] = key_grad
            made[here, head_width:] = value_grad
            far_copy(block).start()

            @pl.when(sums)
            def _():
                rounded[here, :head_width] = key_grad
                rounded[here, head_width:] = value_grad

            @pl.when(jnp.logical_not(sums))
            def _():
                near_copy(block).start()

    wide = heads * rows
    contract_last = (((1,), (1,)), ((), ()))
    @pl.when(sums)
    def _():
        keep_above.wait()

    @pl.when(jnp.logical_not(sums))
    def _():
        send_above.wait_recv()

        @pl.loop(0, count * PIECES)
        def _(step):
            share_copy(lax.div(step, PIECES), lax.rem(step, PIECES)).wait_recv()
            pair_copy(lax.div(step, PIECES), lax.rem(step, PIECES)).wait_recv()

    for block in reversed(range(blocks)):
        extent = (block + 1) * rows
        query = queries[core, block].reshape(wide, head_width)
        above = upstream[block]
        scores = lax.dot_general(
            pairs[:extent, :head_width], query, contract_last, preferred_element_type=jnp.float32)
        key_at = lax.broadcasted_iota(jnp.int32, (rows, wide), 0)
        query_at = lax.rem(lax.broadcasted_iota(jnp.int32, (rows, wide), 1), rows)
        corner = jnp.where(key_at <= query_at, scores[extent - rows:], far_below)
        if block > 0:
            scores = jnp.concatenate([scores[:extent - rows], corner], axis=0)
        else:
            scores = corner
        peak = jnp.max(scores, axis=0, keepdims=True)
        powers = jnp.exp2((scores - peak) * (scale * math.log2(math.e)))
        prob = powers * (1.0 / jnp.sum(powers, axis=0, keepdims=True))
        dprob = lax.dot_general(
            pairs[:extent, head_width:], above, contract_last, preferred_element_type=jnp.float32)
        row_dot = jnp.sum(prob * dprob, axis=0, keepdims=True)
        dscore = (prob * (dprob - row_dot) * scale).astype(jnp.bfloat16)
        key_part = jnp.dot(dscore, query, preferred_element_type=jnp.float32)
        value_part = jnp.dot(prob.astype(jnp.bfloat16), above, preferred_element_type=jnp.float32)
        key_part = key_part.reshape(block + 1, rows, head_width)
        value_part = value_part.reshape(block + 1, rows, head_width)
        if block == blocks - 1:
            grads[:, :, :head_width] = key_part
            grads[:, :, head_width:] = value_part
        else:
            grads[:block + 1, :, :head_width] += key_part
            grads[:block + 1, :, head_width:] += value_part

        @pl.when(core != block % 2)
        def _():
            grad_copy(block).start()

        if block + 3 < blocks:
            sum_up(block + 3)

    for block in reversed(range(min(3, blocks))):
        sum_up(block)
    for block in reversed(range(blocks)):
        @pl.when(jnp.logical_not(sums & (core == block % 2)))
        def _():
            far_copy(block).wait_recv()

    @pl.when(end)
    def _():
        for slot in near_slots:
            wait_rows(slot, last)

    share = half // 2
    tiles = share // TILE

    def squares_of(start):
        columns = pl.ds(pl.multiple_of(start, TILE), TILE)
        sample = lax.dot_general(
            held[:, columns], rounded[...], (((0,), (0,)), ((), ())),
            preferred_element_type=jnp.float32)
        return sample * sample

    def square_copy(index):
        here = pl.ds(pl.multiple_of(index * TILE, TILE), TILE)
        return pltpu.make_async_remote_copy(
            src_ref=send_squares.at[here], dst_ref=peer_squares.at[here],
            send_sem=square_send.at[index], recv_sem=square_recv.at[index],
            device_id={"dp": 1 - core}, device_id_type=MESH)

    @pl.loop(0, tiles)
    def _(index):
        here = pl.ds(pl.multiple_of(index * TILE, TILE), TILE)
        send_squares[here, :] = squares_of((1 - core) * share + index * TILE)
        square_copy(index).start()

    @pl.loop(0, tiles)
    def _(index):
        here = pl.ds(pl.multiple_of(index * TILE, TILE), TILE)
        squares = squares_of(core * share + index * TILE)
        square_copy(index).wait_recv()
        squares = squares + peer_squares[here, :]
        key_out[here, :] = squares[:, :head_width]
        value_out[here, :] = squares[:, head_width:]

    to_mate[last].wait_send()
    for index in range(STRIPS):
        wide_copy(index).wait_send()
        core_copy(index).wait_send()
        cross_copy(index).wait_send()
        hand_copy(index).wait_send()

    @pl.loop(0, count * PIECES)
    def _(step):
        slot = lax.div(step, PIECES)
        piece = lax.rem(step, PIECES)

        @pl.when(jnp.logical_not(sums) & jnp.logical_not(helped(slot, piece)))
        def _():
            for part in range(2):
                partial_copy(slot, piece, part).wait_send()

        origin = lax.div(slot, 2)

        @pl.when(has_up & (origin <= place))
        def _():
            rows_copy(0, slot, piece, held.at[piece_at(slot, piece)]).wait_send()

        @pl.when(has_down & (origin >= place))
        def _():
            rows_copy(1, slot, piece, held.at[piece_at(slot, piece)]).wait_send()

    @pl.when(sums)
    def _():
        @pl.loop(0, count * PIECES)
        def _(step):
            share_copy(lax.div(step, PIECES), lax.rem(step, PIECES)).wait_send()
            pair_copy(lax.div(step, PIECES), lax.rem(step, PIECES)).wait_send()

        @pl.when(helper)
        def _():
            for which in range(2):
                for copy in gift_copies(which):
                    copy.wait_send()

    @pl.when(jnp.logical_not(sums))
    def _():
        send_above.wait_send()

        @pl.when(helper)
        def _():
            for which in range(2):
                for part in range(2):
                    aid_sum_copy(part, which).wait_send()

    @pl.when(helper)
    def _():
        for which in range(2):
            guest_copy(which).wait_send()
        for turn in range(2):
            part = side + turn - 2 * side * turn
            for which in range(2):
                return_copy(turn, part, which).wait_send()
            for index in range(STRIPS):
                aid_core_copy(turn, part, index).wait_send()

    @pl.when(end)
    def _():
        for turn in range(2):
            part = side + turn - 2 * side * turn
            for index in range(STRIPS):
                aid_copy(turn, part, index).wait_send()

    for block in range(blocks):
        @pl.when(core != block % 2)
        def _():
            grad_copy(block).wait_send()

        @pl.when(core == block % 2)
        def _():
            far_copy(block).wait_send()

            @pl.when(jnp.logical_not(sums))
            def _():
                near_copy(block).wait_send()

    @pl.loop(0, tiles)
    def _(index):
        square_copy(index).wait_send()


PIECES = 2
STRIPS = 4
TILE = 512


def fused(lengths, head_grad, table, hidden, query_weight, key_weight, value_weight):
    count = lax.axis_size("tensor")
    rows, model_width = hidden.shape
    length = rows * count
    half = model_width // 2
    query_cols = query_weight.shape[1]
    head_width = key_weight.shape[1]
    pair_cols = 2 * head_width
    all_cols = 2 * (query_cols + head_width)
    heads = query_cols // head_width
    share = half // 2
    dma = pltpu.SemaphoreType.DMA
    anywhere = pl.BlockSpec(memory_space=pl.ANY)
    here = pl.BlockSpec(memory_space=pltpu.VMEM)
    out = jax.ShapeDtypeStruct((share, head_width), jnp.float32)
    return pl.pallas_call(
        functools.partial(fused_kernel, count),
        out_shape=(out, out),
        in_specs=[pl.BlockSpec(memory_space=pltpu.SMEM)] + [here] * 2 + [anywhere] * 4,
        out_specs=(here, here),
        scratch_shapes=[
            pltpu.VMEM((length, half), jnp.bfloat16),
            pltpu.VMEM((half, all_cols), jnp.bfloat16),
            pltpu.VMEM((length, all_cols), jnp.float32),
            pltpu.VMEM((length, all_cols), jnp.float32),
            pltpu.VMEM((2, count, heads, rows, head_width), jnp.bfloat16),
            pltpu.VMEM((length, pair_cols), jnp.bfloat16),
            pltpu.VMEM((count, heads * rows, head_width), jnp.bfloat16),
            pltpu.VMEM((count, heads * rows, head_width), jnp.bfloat16),
            pltpu.VMEM((count, rows, pair_cols), jnp.float32),
            pltpu.VMEM((count, rows, pair_cols), jnp.float32),
            pltpu.VMEM((length, pair_cols), jnp.bfloat16),
            pltpu.VMEM((length, pair_cols), jnp.bfloat16),
            pltpu.VMEM((share, pair_cols), jnp.float32),
            pltpu.VMEM((share, pair_cols), jnp.float32),
            pltpu.VMEM((half // 2, all_cols), jnp.bfloat16),
            pltpu.VMEM((2, rows // PIECES, half // 2), jnp.bfloat16),
            pltpu.VMEM((2, rows // PIECES, all_cols), jnp.float32),
            pltpu.VMEM((2, rows // PIECES, all_cols), jnp.float32),
            pltpu.VMEM((2, rows // PIECES, all_cols), jnp.float32),
            pltpu.VMEM((2, rows // PIECES, all_cols), jnp.float32),
            pltpu.VMEM((2, 2, heads, rows // PIECES, head_width), jnp.bfloat16),
            pltpu.VMEM((2, rows // PIECES, pair_cols), jnp.bfloat16),
            dma((count, PIECES)), dma((2, count, PIECES)), dma((PIECES,)), dma((4,)),
            dma((STRIPS,)), dma((STRIPS,)), dma((STRIPS,)), dma((STRIPS,)),
            dma((STRIPS,)), dma((STRIPS,)), dma((STRIPS,)), dma((STRIPS,)),
            dma((count, PIECES, 2)), dma((count, PIECES, 2)),
            dma((count, PIECES)), dma((count, PIECES)), dma((count, PIECES)), dma((count, PIECES)),
            dma, dma, dma,
            dma((count,)), dma((count,)), dma((count,)), dma((count,)), dma((count,)),
            dma((share // TILE,)), dma((share // TILE,)),
            dma((2, STRIPS)), dma((2, STRIPS)), dma((2, STRIPS)), dma((2, STRIPS)),
            dma((2,)), dma((2,)), dma((2, 2)), dma((2, 2)), dma((2, 2)), dma((2, 2)),
            dma((2, 3)), dma((2, 3)),
        ],
        compiler_params=pltpu.CompilerParams(
            collective_id=2, has_side_effects=True, vmem_limit_bytes=58 * 2**20),
    )(lengths, head_grad, table, hidden, query_weight, key_weight, value_weight)


def local(hidden, query_weight, key_weight, value_weight, head_grad, lengths):
    head_width = key_weight.shape[2]
    length = head_grad.shape[1]
    table = jnp.asarray(turn_table(length, head_width))
    if lax.axis_size("groups") == 2 and lax.axis_size("dp") == 2 and lax.axis_size("tensor") == 8:
        fisher_key, fisher_value = fused(
            lengths, head_grad[0], table, hidden[0], query_weight, key_weight[0], value_weight[0])
        return (fisher_key[None], fisher_value[None])
    half_rows, queries, pairs, upstream = gather_project(
        lengths, head_grad[0], table, hidden[0], query_weight, key_weight[0], value_weight[0]
    )
    own, peer = attend(
        queries, upstream, pairs.reshape(length, -1), table, half_rows.reshape(length, -1),
        head_width,
    )
    fisher_key = own[:1] + jnp.sum(peer[:, :1], axis=0)
    fisher_value = own[1:] + jnp.sum(peer[:, 1:], axis=0)
    return (fisher_key, fisher_value)


def solution(mesh):
    in_specs = (
        P(("groups", "dp"), "tensor", None),
        P(None, "tensor"),
        P("tensor", None, None),
        P("tensor", None, None),
        P(("groups", "dp"), None, "tensor"),
        P(("groups", "dp")),
    )
    out_specs = (P(("groups", "tensor"), "dp", None), P(("groups", "tensor"), "dp", None))
    return jax.shard_map(local, mesh=mesh, in_specs=in_specs, out_specs=out_specs, check_vma=False)
```

```python
import functools
import math

import jax
import jax.numpy as jnp
import numpy as np
from jax import lax
from jax.experimental import pallas as pl
from jax.experimental.pallas import tpu as pltpu
from jax.sharding import PartitionSpec as P

MESH = pl.DeviceIdType.MESH

rope_base = 1000000.0
far_below = -1e30


def turn_table(length, head_width):
    position = np.arange(length, dtype=np.float64)[:, None]
    frequency = rope_base ** (-2.0 * np.arange(head_width // 2, dtype=np.float64) / head_width)
    angles = position * frequency
    return np.concatenate([np.cos(angles), np.sin(angles)], axis=-1).astype(np.float32)


def swap_halves(vectors):
    return pltpu.roll(vectors, vectors.shape[-1] // 2, axis=1)


def cosine_sine(table):
    other = swap_halves(table)
    lead = lax.broadcasted_iota(jnp.int32, table.shape, 1) < table.shape[1] // 2
    return jnp.where(lead, table, other), jnp.where(lead, -other, table)


def gather_project_kernel(
    count, dp_count, lengths_ref, gradient_ref, table_ref,
    hidden_ref, query_ref, key_ref, value_ref,
    rows_out, queries_out, pairs_out, upstream_out,
    held, weights, partial, other, queries, pairs, upstream,
    rows_recv, up_send, down_send, mate_send, load_sem, weight_send, weight_recv,
    share_send, share_recv, partial_send, partial_recv, rows_store, queries_store, pairs_store,
    upstream_store,
):
    me = lax.axis_index("tensor")
    core = lax.axis_index("dp")
    side = lax.rem(me, 2)
    place = lax.div(me, 2)
    mate = me + 1 - 2 * side
    chain = count // 2
    half = held.shape[2]
    query_cols = query_ref.shape[1]
    head_width = key_ref.shape[1]
    own_cols = query_cols + 2 * head_width
    has_up = place < chain - 1
    has_down = place > 0
    share = half // dp_count

    barrier = pltpu.get_barrier_semaphore()
    pl.semaphore_signal(barrier, inc=1, device_id={"tensor": mate}, device_id_type=MESH)
    for step in range(1, dp_count):
        peer = lax.rem(core + step, dp_count)
        pl.semaphore_signal(barrier, inc=1, device_id={"dp": peer}, device_id_type=MESH)

    @pl.when(has_up)
    def _():
        pl.semaphore_signal(barrier, inc=1, device_id={"tensor": me + 2}, device_id_type=MESH)

    @pl.when(has_down)
    def _():
        pl.semaphore_signal(barrier, inc=1, device_id={"tensor": me - 2}, device_id_type=MESH)

    edges = jnp.where(has_up, 1, 0) + jnp.where(has_down, 1, 0)
    pl.semaphore_wait(barrier, dp_count + edges)

    own_half = hidden_ref.at[:, pl.ds(pl.multiple_of(side * half, half), half)]
    mate_half = hidden_ref.at[:, pl.ds(pl.multiple_of((1 - side) * half, half), half)]

    def up_copy(slot, source):
        return pltpu.make_async_remote_copy(
            src_ref=source, dst_ref=held.at[slot], send_sem=up_send.at[slot],
            recv_sem=rows_recv.at[slot], device_id={"tensor": me + 2}, device_id_type=MESH)

    def down_copy(slot, source):
        return pltpu.make_async_remote_copy(
            src_ref=source, dst_ref=held.at[slot], send_sem=down_send.at[slot],
            recv_sem=rows_recv.at[slot], device_id={"tensor": me - 2}, device_id_type=MESH)

    def wait_rows(slot):
        pltpu.make_async_remote_copy(
            src_ref=held.at[slot], dst_ref=held.at[slot], send_sem=mate_send,
            recv_sem=rows_recv.at[slot], device_id={"tensor": mate}, device_id_type=MESH).wait_recv()

    def store_rows(slot):
        return pltpu.make_async_copy(held.at[slot], rows_out.at[slot], rows_store.at[slot])

    def store_queries(slot):
        return pltpu.make_async_copy(queries.at[slot], queries_out.at[slot], queries_store.at[slot])

    def store_pairs(slot):
        return pltpu.make_async_copy(pairs.at[slot], pairs_out.at[slot], pairs_store.at[slot])

    tile = 256
    pieces = own_cols // tile

    def partial_copy(slot, piece):
        source = pl.ds(pl.multiple_of(query_cols + piece * tile, tile), tile)
        target = pl.ds(pl.multiple_of(piece * tile, tile), tile)
        return pltpu.make_async_remote_copy(
            src_ref=partial.at[slot, :, source], dst_ref=other.at[slot, :, target],
            send_sem=partial_send.at[slot, piece], recv_sem=partial_recv.at[slot, piece],
            device_id={"tensor": mate}, device_id_type=MESH)

    to_mate = pltpu.make_async_remote_copy(
        src_ref=mate_half, dst_ref=held.at[me], send_sem=mate_send,
        recv_sem=rows_recv.at[me], device_id={"tensor": mate}, device_id_type=MESH)
    to_mate.start()

    @pl.when(has_up)
    def _():
        up_copy(me, own_half).start()

    @pl.when(has_down)
    def _():
        down_copy(me, own_half).start()

    half_rows = pl.ds(pl.multiple_of(side * half, half), half)
    loads = [
        pltpu.make_async_copy(own_half, held.at[me], load_sem.at[0]),
        pltpu.make_async_copy(
            query_ref.at[half_rows], weights.at[:, pl.ds(0, query_cols)], load_sem.at[1]),
        pltpu.make_async_copy(
            key_ref, weights.at[:, pl.ds(query_cols, head_width)], load_sem.at[2]),
        pltpu.make_async_copy(
            value_ref, weights.at[:, pl.ds(query_cols + head_width, head_width)], load_sem.at[3]),
    ]
    for load in loads:
        load.start()

    share_rows = pl.ds(pl.multiple_of(core * share, share), share)
    mate_cols = pl.ds(own_cols, query_cols)
    weight_copy = pltpu.make_async_remote_copy(
        src_ref=query_ref.at[pl.ds(pl.multiple_of((1 - side) * half + core * share, share), share)],
        dst_ref=weights.at[share_rows, mate_cols], send_sem=weight_send, recv_sem=weight_recv,
        device_id={"tensor": mate}, device_id_type=MESH)

    live = lengths_ref[0]
    rows = held.shape[1]
    heads = query_cols // head_width

    @pl.loop(0, count)
    def _(slot):
        here = pl.ds(pl.multiple_of(slot * rows, rows), rows)
        position = slot * rows + lax.broadcasted_iota(jnp.int32, (rows, head_width), 0)
        for head in range(heads):
            gradient = gradient_ref[here, head * head_width:(head + 1) * head_width]
            upstream[slot, head * rows:(head + 1) * rows, :] = jnp.where(
                position < live, gradient.astype(jnp.float32), 0.0).astype(jnp.bfloat16)

    store_upstream = pltpu.make_async_copy(upstream, upstream_out, upstream_store)
    store_upstream.start()
    wait_rows(mate)

    @pl.when(has_up)
    def _():
        up_copy(mate, held.at[mate]).start()

    @pl.when(has_down)
    def _():
        down_copy(mate, held.at[mate]).start()

    weight_copy.start()

    def slot_at(step, which):
        return 2 * step + jnp.where(which == 0, side, 1 - side)

    def receive(distance, which):
        below = place - distance
        above = place + distance

        @pl.when(below >= 0)
        def _():
            slot = slot_at(below, which)
            wait_rows(slot)

            @pl.when(has_up)
            def _():
                up_copy(slot, held.at[slot]).start()

        @pl.when(above < chain)
        def _():
            slot = slot_at(above, which)
            wait_rows(slot)

            @pl.when(has_down)
            def _():
                down_copy(slot, held.at[slot]).start()

    def multiply(slot, start):
        columns = pl.ds(pl.multiple_of(start, tile), tile)
        partial[slot, :, columns] = jnp.dot(
            held[slot], weights[:, columns], preferred_element_type=jnp.float32)

    def project_pair(slot):
        store_rows(slot).start()
        multiply(slot, query_cols)

    def send_pair(slot):
        partial_copy(slot, 0).start()

    def project_queries(slot):
        @pl.loop(1, pieces)
        def _(piece):
            multiply(slot, query_cols + piece * tile)
            partial_copy(slot, piece).start()

        @pl.loop(0, query_cols // tile)
        def _(piece):
            multiply(slot, piece * tile)

    def project(slot):
        project_pair(slot)
        send_pair(slot)
        project_queries(slot)

    def project_at(distance, which, action):
        below = place - distance
        above = place + distance

        @pl.when(below >= 0)
        def _():
            action(slot_at(below, which))

        @pl.when(above < chain)
        def _():
            action(slot_at(above, which))

    receive(1, 0)
    receive(1, 1)
    for load in loads:
        load.wait()

    def early(action):
        @pl.loop(0, 2)
        def _(which):
            action(slot_at(place, which))

        @pl.loop(0, 2)
        def _(which):
            project_at(1, which, action)

    early(project_pair)
    weight_copy.wait_recv()
    shares = []
    for step in range(1, dp_count):
        peer = lax.rem(core + step, dp_count)
        shares.append(pltpu.make_async_remote_copy(
            src_ref=weights.at[share_rows, mate_cols], dst_ref=weights.at[share_rows, mate_cols],
            send_sem=share_send.at[step - 1], recv_sem=share_recv.at[step - 1],
            device_id={"dp": peer}, device_id_type=MESH))
    for copy in shares:
        copy.start()
    early(send_pair)
    for copy in shares:
        copy.wait_recv()
    early(project_queries)

    @pl.loop(4, 2 * chain)
    def _(step):
        distance = lax.div(step, 2)
        which = lax.rem(step, 2)
        receive(distance, which)
        project_at(distance, which, project)

    def finish(slot):
        for piece in range(pieces):
            partial_copy(slot, piece).wait_recv()
        cosine, sine = cosine_sine(table_ref[pl.ds(pl.multiple_of(slot * rows, rows), rows), :])

        def turn(mixed):
            return (mixed * cosine + swap_halves(mixed) * sine).astype(jnp.bfloat16)

        for head in range(heads):
            columns = slice(head * head_width, (head + 1) * head_width)
            shifted = slice((head + 2) * head_width, (head + 3) * head_width)
            queries[slot, head * rows:(head + 1) * rows, :] = turn(
                partial[slot, :, columns] + other[slot, :, shifted])
        pairs[slot, :, :head_width] = turn(
            partial[slot, :, query_cols:query_cols + head_width] + other[slot, :, :head_width])
        pairs[slot, :, head_width:] = (
            partial[slot, :, query_cols + head_width:own_cols]
            + other[slot, :, head_width:2 * head_width]
        ).astype(jnp.bfloat16)
        store_queries(slot).start()
        store_pairs(slot).start()

    @pl.loop(0, 2 * chain)
    def _(step):
        distance = lax.div(step, 2)
        which = lax.rem(step, 2)
        below = place - distance
        above = place + distance

        @pl.when(below >= 0)
        def _():
            finish(slot_at(below, which))

        @pl.when((above < chain) & (distance > 0))
        def _():
            finish(slot_at(above, which))

    store_upstream.wait()
    to_mate.wait_send()
    weight_copy.wait_send()
    for copy in shares:
        copy.wait_send()

    @pl.loop(0, count)
    def _(slot):
        for piece in range(pieces):
            partial_copy(slot, piece).wait_send()
        store_rows(slot).wait()
        store_queries(slot).wait()
        store_pairs(slot).wait()
        origin = lax.div(slot, 2)

        @pl.when(has_up & (origin <= place))
        def _():
            up_copy(slot, held.at[slot]).wait_send()

        @pl.when(has_down & (origin >= place))
        def _():
            down_copy(slot, held.at[slot]).wait_send()


def gather_project(lengths, head_grad, table, hidden, query_weight, key_weight, value_weight):
    count = lax.axis_size("tensor")
    dp_count = lax.axis_size("dp")
    rows, model_width = hidden.shape
    half = model_width // 2
    query_cols = query_weight.shape[1]
    head_width = key_weight.shape[1]
    own_cols = query_cols + 2 * head_width
    all_cols = own_cols + query_cols
    heads = query_cols // head_width
    stack_shape = jax.ShapeDtypeStruct((count, heads * rows, head_width), jnp.bfloat16)
    pair_shape = jax.ShapeDtypeStruct((count, rows, 2 * head_width), jnp.bfloat16)
    dma = pltpu.SemaphoreType.DMA
    anywhere = pl.BlockSpec(memory_space=pl.ANY)
    return pl.pallas_call(
        functools.partial(gather_project_kernel, count, dp_count),
        out_shape=(
            jax.ShapeDtypeStruct((count, rows, half), jnp.bfloat16),
            stack_shape,
            pair_shape,
            stack_shape,
        ),
        in_specs=[pl.BlockSpec(memory_space=pltpu.SMEM)]
        + [pl.BlockSpec(memory_space=pltpu.VMEM)] * 2 + [anywhere] * 4,
        out_specs=(anywhere,) * 4,
        scratch_shapes=[
            pltpu.VMEM((count, rows, half), jnp.bfloat16),
            pltpu.VMEM((half, all_cols), jnp.bfloat16),
            pltpu.VMEM((count, rows, all_cols), jnp.float32),
            pltpu.VMEM((count, rows, own_cols), jnp.float32),
            pltpu.VMEM(stack_shape.shape, jnp.bfloat16),
            pltpu.VMEM(pair_shape.shape, jnp.bfloat16),
            pltpu.VMEM(stack_shape.shape, jnp.bfloat16),
            dma((count,)), dma((count,)), dma((count,)), dma, dma((4,)), dma, dma,
            dma((dp_count - 1,)), dma((dp_count - 1,)),
            dma((count, own_cols // 256)), dma((count, own_cols // 256)),
            dma((count,)), dma((count,)), dma((count,)), dma,
        ],
        compiler_params=pltpu.CompilerParams(
            collective_id=0, has_side_effects=True, vmem_limit_bytes=58 * 2**20),
    )(lengths, head_grad, table, hidden, query_weight, key_weight, value_weight)

def attend_kernel(
    dp_count, head_width, queries, upstream, pairs, table_ref, rows_ref,
    squares_out, peer_out,
    rows, grads, mate_grads, rounded, peer_squares,
    rows_load, grad_send, grad_recv, final_send, final_recv, peer_send, peer_recv,
):
    me = lax.axis_index("tensor")
    core = lax.axis_index("dp")
    side = lax.rem(me, 2)
    mate = me + 1 - 2 * side
    blocks, stacked, _ = queries.shape
    step_rows = head_width
    scale = 1.0 / math.sqrt(head_width)
    share = squares_out.shape[1]
    tile = 256
    tiles = share // tile

    barrier = pltpu.get_barrier_semaphore()
    pl.semaphore_signal(barrier, inc=1, device_id={"tensor": mate}, device_id_type=MESH)
    for step in range(1, dp_count):
        peer = lax.rem(core + step, dp_count)
        pl.semaphore_signal(barrier, inc=1, device_id={"dp": peer}, device_id_type=MESH)

    load = pltpu.make_async_copy(rows_ref, rows, rows_load)
    load.start()
    pl.semaphore_wait(barrier, dp_count)

    def grad_copy(block):
        return pltpu.make_async_remote_copy(
            src_ref=grads.at[block], dst_ref=mate_grads.at[block],
            send_sem=grad_send.at[block], recv_sem=grad_recv.at[block],
            device_id={"tensor": mate}, device_id_type=MESH)

    def rows_of(block):
        return slice(block * step_rows, (block + 1) * step_rows)

    def final_copy(block):
        here = rows_of(block)
        return pltpu.make_async_remote_copy(
            src_ref=rounded.at[here], dst_ref=rounded.at[here],
            send_sem=final_send.at[block], recv_sem=final_recv.at[block],
            device_id={"tensor": mate}, device_id_type=MESH)

    def finish(block):
        @pl.when(side == block % 2)
        def _():
            grad_copy(block).wait_recv()
            here = rows_of(block)
            cosine, sine = cosine_sine(table_ref[here, :])
            key_grad = grads[block, :, :head_width] + mate_grads[block, :, :head_width]
            key_grad = key_grad * cosine - swap_halves(key_grad) * sine
            rounded[here, :head_width] = key_grad.astype(jnp.bfloat16)
            rounded[here, head_width:] = (
                grads[block, :, head_width:] + mate_grads[block, :, head_width:]
            ).astype(jnp.bfloat16)
            final_copy(block).start()

    wide = 2 * head_width
    contract_last = (((1,), (1,)), ((), ()))
    for block in reversed(range(blocks)):
        extent = (block + 1) * step_rows
        for chunk in range(stacked // wide):
            chunk_rows = slice(chunk * wide, (chunk + 1) * wide)
            query = queries[block, chunk_rows, :]
            above = upstream[block, chunk_rows, :]
            scores = lax.dot_general(
                pairs[:extent, :head_width], query, contract_last, preferred_element_type=jnp.float32)
            key_at = lax.broadcasted_iota(jnp.int32, (step_rows, wide), 0)
            query_at = lax.rem(lax.broadcasted_iota(jnp.int32, (step_rows, wide), 1), step_rows)
            corner = jnp.where(key_at <= query_at, scores[extent - step_rows:], far_below)
            if block > 0:
                scores = jnp.concatenate([scores[:extent - step_rows], corner], axis=0)
            else:
                scores = corner
            peak = jnp.max(scores, axis=0, keepdims=True)
            powers = jnp.exp2((scores - peak) * (scale * math.log2(math.e)))
            prob = powers * (1.0 / jnp.sum(powers, axis=0, keepdims=True))
            dprob = lax.dot_general(
                pairs[:extent, head_width:], above, contract_last, preferred_element_type=jnp.float32)
            row_dot = jnp.sum(prob * dprob, axis=0, keepdims=True)
            dscore = (prob * (dprob - row_dot) * scale).astype(jnp.bfloat16)
            key_part = jnp.dot(dscore, query, preferred_element_type=jnp.float32)
            value_part = jnp.dot(
                prob.astype(jnp.bfloat16), above, preferred_element_type=jnp.float32)
            key_part = key_part.reshape(block + 1, step_rows, head_width)
            value_part = value_part.reshape(block + 1, step_rows, head_width)
            if block == blocks - 1 and chunk == 0:
                grads[:, :, :head_width] = key_part
                grads[:, :, head_width:] = value_part
            else:
                grads[:block + 1, :, :head_width] += key_part
                grads[:block + 1, :, head_width:] += value_part
        @pl.when(side != block % 2)
        def _():
            grad_copy(block).start()

        if block + 3 < blocks:
            finish(block + 3)

    for block in reversed(range(min(3, blocks))):
        finish(block)
    for block in reversed(range(blocks)):
        @pl.when(side != block % 2)
        def _():
            final_copy(block).wait_recv()

    load.wait()

    def squares_of(start):
        columns = pl.ds(pl.multiple_of(start, tile), tile)
        sample = lax.dot_general(
            rows[:, columns], rounded[...], (((0,), (0,)), ((), ())),
            preferred_element_type=jnp.float32)
        return sample * sample

    def peer_copy(step, index):
        here = pl.ds(pl.multiple_of(index * tile, tile), tile)
        return pltpu.make_async_remote_copy(
            src_ref=peer_squares.at[step - 1, :, here], dst_ref=peer_out.at[step - 1, :, here],
            send_sem=peer_send.at[step - 1, index], recv_sem=peer_recv.at[step - 1, index],
            device_id={"dp": lax.rem(core + step, dp_count)}, device_id_type=MESH)

    for step in range(1, dp_count):
        @pl.loop(0, tiles)
        def _(index):
            here = pl.ds(pl.multiple_of(index * tile, tile), tile)
            start = lax.rem(core + step, dp_count) * share + index * tile
            squares = squares_of(start)
            peer_squares[step - 1, 0, here, :] = squares[:, :head_width]
            peer_squares[step - 1, 1, here, :] = squares[:, head_width:]
            peer_copy(step, index).start()

    @pl.loop(0, tiles)
    def _(index):
        here = pl.ds(pl.multiple_of(index * tile, tile), tile)
        squares = squares_of(core * share + index * tile)
        squares_out[0, here, :] = squares[:, :head_width]
        squares_out[1, here, :] = squares[:, head_width:]

    for block in range(blocks):
        @pl.when(side != block % 2)
        def _():
            grad_copy(block).wait_send()

        @pl.when(side == block % 2)
        def _():
            final_copy(block).wait_send()
    for step in range(1, dp_count):
        @pl.loop(0, tiles)
        def _(index):
            peer_copy(step, index).wait()


def attend(queries, upstream, pairs, table, half_rows, head_width):
    dp_count = lax.axis_size("dp")
    length, half = half_rows.shape
    blocks = length // head_width
    share = half // dp_count
    wide = 2 * head_width
    dma = pltpu.SemaphoreType.DMA
    here = pl.BlockSpec(memory_space=pltpu.VMEM)
    anywhere = pl.BlockSpec(memory_space=pl.ANY)
    return pl.pallas_call(
        functools.partial(attend_kernel, dp_count, head_width),
        out_shape=(
            jax.ShapeDtypeStruct((2, share, head_width), jnp.float32),
            jax.ShapeDtypeStruct((dp_count - 1, 2, share, head_width), jnp.float32),
        ),
        in_specs=[here] * 4 + [anywhere],
        out_specs=(here, anywhere),
        scratch_shapes=[
            pltpu.VMEM((length, half), jnp.bfloat16),
            pltpu.VMEM((blocks, head_width, wide), jnp.float32),
            pltpu.VMEM((blocks, head_width, wide), jnp.float32),
            pltpu.VMEM((length, wide), jnp.bfloat16),
            pltpu.VMEM((dp_count - 1, 2, share, head_width), jnp.float32),
            dma, dma((blocks,)), dma((blocks,)), dma((blocks,)), dma((blocks,)),
            dma((dp_count - 1, share // 256)), dma((dp_count - 1, share // 256)),
        ],
        compiler_params=pltpu.CompilerParams(
            collective_id=1, has_side_effects=True, vmem_limit_bytes=56 * 2**20),
    )(queries, upstream, pairs, table, half_rows)


def fused_kernel(
    count, lengths_ref, gradient_ref, table_ref, hidden_ref, query_ref, key_ref, value_ref,
    key_out, value_out,
    held, weights, partial, other, queries, pairs, staged, upstream,
    grads, peer_grads, made, rounded, send_squares, peer_squares,
    aid_weights, guest, aid_partial, guest_partial, aid_cross, aid_other, gift, gift_pairs,
    rows_recv, rows_send, mate_send, load_sem,
    wide_send, wide_recv, core_send, core_recv, cross_send, cross_recv, hand_send, hand_recv,
    partial_send, partial_recv, share_send, share_recv, pair_send, pair_recv,
    above_keep, above_send, above_recv, grad_send, grad_recv,
    near_send, far_send, final_recv, square_send, square_recv,
    aid_send, aid_recv, aid_core_send, aid_core_recv, guest_send, guest_recv,
    return_send, return_recv, aid_sum_send, aid_sum_recv, gift_send, gift_recv,
):
    me = lax.axis_index("tensor")
    core = lax.axis_index("dp")
    group = lax.axis_index("groups")
    side = lax.rem(me, 2)
    place = lax.div(me, 2)
    mate = me + 1 - 2 * side
    chain = count // 2
    length, half = held.shape
    rows = length // count
    piece_rows = rows // PIECES
    query_cols = query_ref.shape[1]
    head_width = key_ref.shape[1]
    heads = query_cols // head_width
    cut = query_cols + head_width
    sums = core == side
    has_up = place < chain - 1
    has_down = place > 0

    helper = has_up & has_down
    end = jnp.logical_not(helper)
    end_way = 2 - place
    near = 1 + lax.div(place, chain - 1)
    last = PIECES - 1

    def helped(slot, piece):
        return end & (lax.div(slot, 2) == near) & (piece == last)

    barrier = pltpu.get_barrier_semaphore()
    pl.semaphore_signal(barrier, inc=1, device_id={"tensor": mate}, device_id_type=MESH)
    pl.semaphore_signal(barrier, inc=1, device_id={"dp": 1 - core}, device_id_type=MESH)
    pl.semaphore_signal(
        barrier, inc=1, device_id={"tensor": mate, "dp": 1 - core}, device_id_type=MESH)
    pl.semaphore_signal(barrier, inc=1, device_id={"groups": 1 - group}, device_id_type=MESH)

    @pl.when(has_up)
    def _():
        pl.semaphore_signal(barrier, inc=1, device_id={"tensor": me + 2}, device_id_type=MESH)

    @pl.when(has_down)
    def _():
        pl.semaphore_signal(barrier, inc=1, device_id={"tensor": me - 2}, device_id_type=MESH)

    edges = jnp.where(has_up, 1, 0) + jnp.where(has_down, 1, 0)
    pl.semaphore_wait(barrier, 4 + edges)

    def piece_at(slot, piece):
        return pl.ds(pl.multiple_of(slot * rows + piece * piece_rows, piece_rows), piece_rows)

    def rows_copy(way, slot, piece, source):
        return pltpu.make_async_remote_copy(
            src_ref=source, dst_ref=held.at[piece_at(slot, piece)],
            send_sem=rows_send.at[way, slot, piece], recv_sem=rows_recv.at[slot, piece],
            device_id={"tensor": me + 2 - 4 * way}, device_id_type=MESH)

    def pass_on(way, slot, piece):
        rows_copy(way, slot, piece, held.at[piece_at(slot, piece)]).start()

    def wait_rows(slot, piece):
        here = held.at[piece_at(slot, piece)]
        pltpu.make_async_remote_copy(
            src_ref=here, dst_ref=here, send_sem=mate_send.at[piece],
            recv_sem=rows_recv.at[slot, piece], device_id={"tensor": mate},
            device_id_type=MESH).wait_recv()

    own_cols = pl.ds(pl.multiple_of(side * half, half), half)
    mate_half = pl.ds(pl.multiple_of((1 - side) * half, half), half)

    def own_piece(piece):
        return hidden_ref.at[piece * piece_rows:(piece + 1) * piece_rows, own_cols]

    to_mate = [
        pltpu.make_async_remote_copy(
            src_ref=hidden_ref.at[piece * piece_rows:(piece + 1) * piece_rows, mate_half],
            dst_ref=held.at[piece_at(me, piece)], send_sem=mate_send.at[piece],
            recv_sem=rows_recv.at[me, piece], device_id={"tensor": mate}, device_id_type=MESH)
        for piece in range(PIECES)
    ]
    to_mate[0].start()
    for piece in range(PIECES):
        @pl.when(has_up & jnp.logical_not(helper & (end_way == 0) & (piece == last)))
        def _():
            rows_copy(0, me, piece, own_piece(piece)).start()

        @pl.when(has_down & jnp.logical_not(helper & (end_way == 1) & (piece == last)))
        def _():
            rows_copy(1, me, piece, own_piece(piece)).start()

    own_at = pl.ds(pl.multiple_of(side * cut, head_width), query_cols)
    mate_at = pl.ds(pl.multiple_of((1 - side) * cut, head_width), query_cols)
    quarter = half // 4
    strip = quarter // STRIPS
    half_rows = pl.ds(pl.multiple_of(side * half, half), half)
    loads = [
        pltpu.make_async_copy(
            hidden_ref.at[:, own_cols], held.at[pl.ds(pl.multiple_of(me * rows, rows), rows)],
            load_sem.at[0]),
        pltpu.make_async_copy(
            key_ref, weights.at[:, pl.ds(query_cols, head_width)], load_sem.at[1]),
        pltpu.make_async_copy(
            value_ref, weights.at[:, pl.ds(cut + query_cols, head_width)], load_sem.at[2]),
        pltpu.make_async_copy(
            query_ref.at[half_rows], weights.at[:, own_at], load_sem.at[3]),
    ]
    for load in loads:
        load.start()

    def strip_at(quarter_of, index):
        start = quarter_of * quarter + index * strip
        return pl.ds(pl.multiple_of(start, strip), strip)

    here_quarter = group * 2 + core
    cross_quarter = (1 - group) * 2 + core

    def wide_copy(index):
        start = (1 - side) * half + here_quarter * quarter + index * strip
        return pltpu.make_async_remote_copy(
            src_ref=query_ref.at[pl.ds(pl.multiple_of(start, strip), strip)],
            dst_ref=weights.at[strip_at(here_quarter, index), own_at],
            send_sem=wide_send.at[index], recv_sem=wide_recv.at[index],
            device_id={"tensor": mate}, device_id_type=MESH)

    def weight_copy(quarter_of, index, send, recv, device):
        here = weights.at[strip_at(quarter_of, index), mate_at]
        return pltpu.make_async_remote_copy(
            src_ref=here, dst_ref=here, send_sem=send.at[index], recv_sem=recv.at[index],
            device_id=device, device_id_type=MESH)

    def core_copy(index):
        return weight_copy(here_quarter, index, core_send, core_recv, {"dp": 1 - core})

    def cross_copy(index):
        return weight_copy(here_quarter, index, cross_send, cross_recv, {"groups": 1 - group})

    def hand_copy(index):
        return weight_copy(cross_quarter, index, hand_send, hand_recv, {"dp": 1 - core})

    live = lengths_ref[0]

    @pl.loop(0, count)
    def _(slot):
        here = pl.ds(pl.multiple_of(slot * rows, rows), rows)
        position = slot * rows + lax.broadcasted_iota(jnp.int32, (rows, head_width), 0)
        for head in range(heads):
            gradient = gradient_ref[here, head * head_width:(head + 1) * head_width]
            staged[slot, head * rows:(head + 1) * rows, :] = jnp.where(
                position < live, gradient.astype(jnp.float32), 0.0).astype(jnp.bfloat16)

    for piece in range(PIECES):
        if piece < last:
            to_mate[piece].wait_send()
            to_mate[piece + 1].start()
        wait_rows(mate, piece)

        @pl.when(has_up & jnp.logical_not(helper & (end_way == 0) & (piece == last)))
        def _():
            pass_on(0, mate, piece)

        @pl.when(has_down & jnp.logical_not(helper & (end_way == 1) & (piece == last)))
        def _():
            pass_on(1, mate, piece)

    for index in range(STRIPS):
        wide_copy(index).start()
    for load in loads:
        load.wait()

    quarter_cols = 2 * quarter
    near_cols = pl.ds(pl.multiple_of(group * quarter_cols, quarter_cols), quarter_cols)
    cross_cols = pl.ds(pl.multiple_of((1 - group) * quarter_cols, quarter_cols), quarter_cols)
    aided = (2 * place, 2 * place + 1)

    def part_at(part):
        return pl.ds(pl.multiple_of(part * cut, head_width), cut)

    def aid_rows(of_core, index):
        start = of_core * quarter + index * strip
        return pl.ds(pl.multiple_of(start, strip), strip)

    def aid_copy(turn, part, index):
        return pltpu.make_async_remote_copy(
            src_ref=weights.at[strip_at(here_quarter, index), part_at(part)],
            dst_ref=aid_weights.at[aid_rows(core, index), part_at(part)],
            send_sem=aid_send.at[turn, index], recv_sem=aid_recv.at[turn, index],
            device_id={"tensor": 2 * near + side}, device_id_type=MESH)

    def aid_core_copy(turn, part, index):
        here = aid_weights.at[aid_rows(core, index), part_at(part)]
        return pltpu.make_async_remote_copy(
            src_ref=here, dst_ref=here, send_sem=aid_core_send.at[turn, index],
            recv_sem=aid_core_recv.at[turn, index], device_id={"dp": 1 - core},
            device_id_type=MESH)

    def guest_copy(which):
        return pltpu.make_async_remote_copy(
            src_ref=held.at[piece_at(aided[which], last), cross_cols], dst_ref=guest.at[which],
            send_sem=guest_send.at[which], recv_sem=guest_recv.at[which],
            device_id={"groups": 1 - group}, device_id_type=MESH)

    def return_copy(turn, part, which):
        return pltpu.make_async_remote_copy(
            src_ref=guest_partial.at[which, :, part_at(part)],
            dst_ref=aid_cross.at[which, :, part_at(part)],
            send_sem=return_send.at[turn, which], recv_sem=return_recv.at[turn, which],
            device_id={"groups": 1 - group}, device_id_type=MESH)

    def aid_sum_copy(part, which):
        return pltpu.make_async_remote_copy(
            src_ref=aid_partial.at[which, :, part_at(part)],
            dst_ref=aid_other.at[which, :, part_at(part)],
            send_sem=aid_sum_send.at[part, which], recv_sem=aid_sum_recv.at[part, which],
            device_id={"tensor": mate}, device_id_type=MESH)

    def gift_copies(which):
        slot = aided[which]
        to_end = {"tensor": me + 2 - 4 * end_way}
        rows_there = pl.ds(last * piece_rows, piece_rows)
        return [
            pltpu.make_async_remote_copy(
                src_ref=gift.at[which, part], dst_ref=queries.at[part, slot, :, rows_there],
                send_sem=gift_send.at[which, part], recv_sem=gift_recv.at[which, part],
                device_id=to_end, device_id_type=MESH)
            for part in range(2)
        ] + [
            pltpu.make_async_remote_copy(
                src_ref=gift_pairs.at[which], dst_ref=pairs.at[piece_at(slot, last)],
                send_sem=gift_send.at[which, 2], recv_sem=gift_recv.at[which, 2],
                device_id=to_end, device_id_type=MESH),
        ]

    @pl.when(helper)
    def _():
        for which in range(2):
            guest_copy(which).start()

    def slot_of(distance, which, way):
        plane = place - distance + 2 * distance * way
        turned = side + which - 2 * side * which
        return plane, 2 * plane + turned

    def receive(distance, which):
        @pl.loop(0, 2 * PIECES)
        def _(step):
            piece = lax.div(step, 2)
            way = lax.rem(step, 2)
            plane, slot = slot_of(distance, which, way)

            @pl.when((plane >= 0) & (plane < chain) & jnp.logical_not(helped(slot, piece)))
            def _():
                wait_rows(slot, piece)

                @pl.when((place + 1 - 2 * way >= 0) & (place + 1 - 2 * way < chain))
                def _():
                    pass_on(way, slot, piece)

    def partial_copy(slot, piece, part):
        here = piece_at(slot, piece)
        columns = pl.ds(part * cut, cut)
        return pltpu.make_async_remote_copy(
            src_ref=partial.at[here, columns], dst_ref=other.at[here, columns],
            send_sem=partial_send.at[slot, piece, part],
            recv_sem=partial_recv.at[slot, piece, part],
            device_id={"tensor": mate}, device_id_type=MESH)

    def project(slot, piece):
        here = piece_at(slot, piece)
        for part in range(2):
            columns = slice(part * cut, (part + 1) * cut)
            partial[here, columns] = jnp.dot(
                held[here], weights[:, columns], preferred_element_type=jnp.float32)

            @pl.when(jnp.logical_not(sums))
            def _():
                partial_copy(slot, piece, part).start()

    def project_whole(slot):
        here = pl.ds(pl.multiple_of(slot * rows, rows), rows)
        for part in range(2):
            columns = slice(part * cut, (part + 1) * cut)
            partial[here, columns] = jnp.dot(
                held[here], weights[:, columns], preferred_element_type=jnp.float32)

            @pl.when(jnp.logical_not(sums))
            def _():
                for piece in range(PIECES):
                    partial_copy(slot, piece, part).start()

    def project_step(distance, which):
        @pl.loop(0, 2)
        def _(way):
            plane, slot = slot_of(distance, which, way)
            inside = (plane >= 0) & (plane < chain)

            @pl.when(inside & jnp.logical_not(end & (plane == near)))
            def _():
                project_whole(slot)

            @pl.when(inside & end & (plane == near))
            def _():
                for piece in range(last):
                    project(slot, piece)

    def share_copy(slot, piece):
        here = queries.at[
            1 - core, slot, :, pl.ds(pl.multiple_of(piece * piece_rows, piece_rows), piece_rows)]
        return pltpu.make_async_remote_copy(
            src_ref=here, dst_ref=here, send_sem=share_send.at[slot, piece],
            recv_sem=share_recv.at[slot, piece], device_id={"dp": 1 - core}, device_id_type=MESH)

    def pair_copy(slot, piece):
        here = pairs.at[piece_at(slot, piece)]
        return pltpu.make_async_remote_copy(
            src_ref=here, dst_ref=here, send_sem=pair_send.at[slot, piece],
            recv_sem=pair_recv.at[slot, piece], device_id={"dp": 1 - core}, device_id_type=MESH)

    key_at = slice(query_cols, cut)
    value_at = slice(cut + query_cols, 2 * cut)

    def turner(here):
        cosine, sine = cosine_sine(table_ref[here, :])

        def turn(mixed):
            return (mixed * cosine + swap_halves(mixed) * sine).astype(jnp.bfloat16)

        return turn

    def head_at(part, head):
        start = part * cut + head * head_width
        return slice(start, start + head_width)

    def finish(slot, piece):
        for part in range(2):
            partial_copy(slot, piece, part).wait_recv()
        here = piece_at(slot, piece)
        there = pl.ds(pl.multiple_of(piece * piece_rows, piece_rows), piece_rows)
        turn = turner(here)
        for part in range(2):
            for head in range(heads):
                columns = head_at(part, head)
                queries[part, slot, head, there, :] = turn(
                    partial[here, columns] + other[here, columns])
        pairs[here, :head_width] = turn(partial[here, key_at] + other[here, key_at])
        pairs[here, head_width:] = (
            partial[here, value_at] + other[here, value_at]).astype(jnp.bfloat16)
        share_copy(slot, piece).start()
        pair_copy(slot, piece).start()

    def finish_step(distance, which):
        @pl.loop(0, 2 * PIECES)
        def _(step):
            piece = lax.div(step, 2)
            way = lax.rem(step, 2)
            plane, slot = slot_of(distance, which, way)
            inside = (plane >= 0) & (plane < chain)

            @pl.when(sums & inside & jnp.logical_not(helped(slot, piece)))
            def _():
                finish(slot, piece)

    def aid(turn):
        part = side + turn - 2 * side * turn
        for index in range(STRIPS):
            aid_copy(turn, part, index).wait_recv()
            aid_core_copy(turn, part, index).start()
        for index in range(STRIPS):
            aid_core_copy(turn, part, index).wait_recv()
        for which in range(2):
            guest_partial[which, :, part_at(part)] = jnp.dot(
                guest[which], aid_weights[:, part_at(part)], preferred_element_type=jnp.float32)
            return_copy(turn, part, which).start()
        for which in range(2):
            aid_partial[which, :, part_at(part)] = jnp.dot(
                held[piece_at(aided[which], last), near_cols], aid_weights[:, part_at(part)],
                preferred_element_type=jnp.float32)

    def aid_sum(turn):
        part = side + turn - 2 * side * turn
        for which in range(2):
            return_copy(turn, part, which).wait_recv()
            aid_partial[which, :, part_at(part)] += aid_cross[which, :, part_at(part)]

            @pl.when(jnp.logical_not(sums))
            def _():
                aid_sum_copy(part, which).start()

    def aid_finish(which):
        for part in range(2):
            aid_sum_copy(part, which).wait_recv()
        turn = turner(piece_at(aided[which], last))
        for part in range(2):
            for head in range(heads):
                columns = head_at(part, head)
                gift[which, part, head] = turn(
                    aid_partial[which, :, columns] + aid_other[which, :, columns])
        gift_pairs[which, :, :head_width] = turn(
            aid_partial[which, :, key_at] + aid_other[which, :, key_at])
        gift_pairs[which, :, head_width:] = (
            aid_partial[which, :, value_at] + aid_other[which, :, value_at]).astype(jnp.bfloat16)
        for copy in gift_copies(which):
            copy.start()

    receive(1, 0)
    for index in range(STRIPS):
        wide_copy(index).wait_recv()
        core_copy(index).start()
        cross_copy(index).start()
    keep_above = pltpu.make_async_copy(staged, upstream, above_keep)
    send_above = pltpu.make_async_remote_copy(
        src_ref=staged, dst_ref=upstream, send_sem=above_send, recv_sem=above_recv,
        device_id={"tensor": mate, "dp": 1 - core}, device_id_type=MESH)

    @pl.when(sums)
    def _():
        keep_above.start()

    @pl.when(jnp.logical_not(sums))
    def _():
        send_above.start()

    receive(1, 1)

    @pl.when(end)
    def _():
        for turn in range(2):
            part = side + turn - 2 * side * turn
            for index in range(STRIPS):
                aid_copy(turn, part, index).start()

    for index in range(STRIPS):
        cross_copy(index).wait_recv()
        hand_copy(index).start()
    for index in range(STRIPS):
        core_copy(index).wait_recv()
    for index in range(STRIPS):
        hand_copy(index).wait_recv()

    @pl.loop(0, 2)
    def _(which):
        project_whole(2 * place + which)

    receive(2, 0)

    @pl.loop(0, 2)
    def _(which):
        project_step(1, which)

    @pl.when(sums)
    def _():
        @pl.loop(0, 2 * PIECES)
        def _(step):
            finish(2 * place + lax.rem(step, 2), lax.div(step, 2))

    receive(2, 1)
    project_step(2, 0)

    @pl.when(helper)
    def _():
        for which in range(2):
            guest_copy(which).wait_recv()
        aid(0)

    project_step(2, 1)

    @pl.when(helper)
    def _():
        aid_sum(0)
        aid(1)
        aid_sum(1)

    @pl.loop(2, 6)
    def _(step):
        finish_step(lax.div(step, 2), lax.rem(step, 2))

    @pl.when(helper & sums)
    def _():
        for which in range(2):
            aid_finish(which)

    @pl.when(helper)
    def _():
        for slot in aided:
            pass_on(end_way, slot, last)

    @pl.loop(6, 2 * chain)
    def _(step):
        @pl.loop(0, PIECES)
        def _(piece):
            for way in range(2):
                plane, slot = slot_of(lax.div(step, 2), lax.rem(step, 2), way)

                @pl.when((plane >= 0) & (plane < chain))
                def _():
                    wait_rows(slot, piece)
                    project(slot, piece)

        @pl.when(step == 2 * chain - 1)
        def _():
            finish_step(chain - 1, 0)

    finish_step(chain - 1, 1)

    near_slots = (2 * near, 2 * near + 1)

    @pl.when(end & sums)
    def _():
        for which in range(2):
            rows_there = pl.ds(last * piece_rows, piece_rows)
            mine = [queries.at[part, near_slots[which], :, rows_there] for part in range(2)]
            pair = pairs.at[piece_at(near_slots[which], last)]
            for index, here in enumerate(mine + [pair]):
                pltpu.make_async_remote_copy(
                    src_ref=here, dst_ref=here, send_sem=gift_send.at[which, index],
                    recv_sem=gift_recv.at[which, index], device_id={"tensor": mate},
                    device_id_type=MESH).wait_recv()
            share_copy(near_slots[which], last).start()
            pair_copy(near_slots[which], last).start()

    scale = 1.0 / math.sqrt(head_width)
    blocks = count

    def grad_copy(block):
        return pltpu.make_async_remote_copy(
            src_ref=grads.at[block], dst_ref=peer_grads.at[block],
            send_sem=grad_send.at[block], recv_sem=grad_recv.at[block],
            device_id={"dp": 1 - core}, device_id_type=MESH)

    def rows_of(block):
        return slice(block * rows, (block + 1) * rows)

    def near_copy(block):
        here = rows_of(block)
        return pltpu.make_async_remote_copy(
            src_ref=made.at[here], dst_ref=rounded.at[here],
            send_sem=near_send.at[block], recv_sem=final_recv.at[block],
            device_id={"dp": 1 - core}, device_id_type=MESH)

    def far_copy(block):
        here = rows_of(block)
        return pltpu.make_async_remote_copy(
            src_ref=made.at[here], dst_ref=rounded.at[here],
            send_sem=far_send.at[block], recv_sem=final_recv.at[block],
            device_id={"tensor": mate, "dp": side}, device_id_type=MESH)

    def sum_up(block):
        @pl.when(core == block % 2)
        def _():
            grad_copy(block).wait_recv()
            here = rows_of(block)
            cosine, sine = cosine_sine(table_ref[here, :])
            key_grad = grads[block, :, :head_width] + peer_grads[block, :, :head_width]
            key_grad = key_grad * cosine - swap_halves(key_grad) * sine
            key_grad = key_grad.astype(jnp.bfloat16)
            value_grad = (
                grads[block, :, head_width:] + peer_grads[block, :, head_width:]
            ).astype(jnp.bfloat16)
            made[here, :head_width] = key_grad
            made[here, head_width:] = value_grad
            far_copy(block).start()

            @pl.when(sums)
            def _():
                rounded[here, :head_width] = key_grad
                rounded[here, head_width:] = value_grad

            @pl.when(jnp.logical_not(sums))
            def _():
                near_copy(block).start()

    wide = heads * rows
    contract_last = (((1,), (1,)), ((), ()))
    @pl.when(sums)
    def _():
        keep_above.wait()

    @pl.when(jnp.logical_not(sums))
    def _():
        send_above.wait_recv()

        @pl.loop(0, count * PIECES)
        def _(step):
            share_copy(lax.div(step, PIECES), lax.rem(step, PIECES)).wait_recv()
            pair_copy(lax.div(step, PIECES), lax.rem(step, PIECES)).wait_recv()

    for block in reversed(range(blocks)):
        extent = (block + 1) * rows
        query = queries[core, block].reshape(wide, head_width)
        above = upstream[block]
        scores = lax.dot_general(
            pairs[:extent, :head_width], query, contract_last, preferred_element_type=jnp.float32)
        key_at = lax.broadcasted_iota(jnp.int32, (rows, wide), 0)
        query_at = lax.rem(lax.broadcasted_iota(jnp.int32, (rows, wide), 1), rows)
        corner = jnp.where(key_at <= query_at, scores[extent - rows:], far_below)
        if block > 0:
            scores = jnp.concatenate([scores[:extent - rows], corner], axis=0)
        else:
            scores = corner
        peak = jnp.max(scores, axis=0, keepdims=True)
        powers = jnp.exp2((scores - peak) * (scale * math.log2(math.e)))
        prob = powers * (1.0 / jnp.sum(powers, axis=0, keepdims=True))
        dprob = lax.dot_general(
            pairs[:extent, head_width:], above, contract_last, preferred_element_type=jnp.float32)
        row_dot = jnp.sum(prob * dprob, axis=0, keepdims=True)
        dscore = (prob * (dprob - row_dot) * scale).astype(jnp.bfloat16)
        key_part = jnp.dot(dscore, query, preferred_element_type=jnp.float32)
        value_part = jnp.dot(prob.astype(jnp.bfloat16), above, preferred_element_type=jnp.float32)
        key_part = key_part.reshape(block + 1, rows, head_width)
        value_part = value_part.reshape(block + 1, rows, head_width)
        if block == blocks - 1:
            grads[:, :, :head_width] = key_part
            grads[:, :, head_width:] = value_part
        else:
            grads[:block + 1, :, :head_width] += key_part
            grads[:block + 1, :, head_width:] += value_part

        @pl.when(core != block % 2)
        def _():
            grad_copy(block).start()

        if block + 3 < blocks:
            sum_up(block + 3)

    for block in reversed(range(min(3, blocks))):
        sum_up(block)
    for block in reversed(range(blocks)):
        @pl.when(jnp.logical_not(sums & (core == block % 2)))
        def _():
            far_copy(block).wait_recv()

    @pl.when(end)
    def _():
        for slot in near_slots:
            wait_rows(slot, last)

    share = half // 2
    tiles = share // TILE

    def squares_of(start):
        columns = pl.ds(pl.multiple_of(start, TILE), TILE)
        sample = lax.dot_general(
            held[:, columns], rounded[...], (((0,), (0,)), ((), ())),
            preferred_element_type=jnp.float32)
        return sample * sample

    def square_copy(index):
        here = pl.ds(pl.multiple_of(index * TILE, TILE), TILE)
        return pltpu.make_async_remote_copy(
            src_ref=send_squares.at[here], dst_ref=peer_squares.at[here],
            send_sem=square_send.at[index], recv_sem=square_recv.at[index],
            device_id={"dp": 1 - core}, device_id_type=MESH)

    @pl.loop(0, tiles)
    def _(index):
        here = pl.ds(pl.multiple_of(index * TILE, TILE), TILE)
        send_squares[here, :] = squares_of((1 - core) * share + index * TILE)
        square_copy(index).start()

    @pl.loop(0, tiles)
    def _(index):
        here = pl.ds(pl.multiple_of(index * TILE, TILE), TILE)
        squares = squares_of(core * share + index * TILE)
        square_copy(index).wait_recv()
        squares = squares + peer_squares[here, :]
        key_out[here, :] = squares[:, :head_width]
        value_out[here, :] = squares[:, head_width:]

    to_mate[last].wait_send()
    for index in range(STRIPS):
        wide_copy(index).wait_send()
        core_copy(index).wait_send()
        cross_copy(index).wait_send()
        hand_copy(index).wait_send()

    @pl.loop(0, count * PIECES)
    def _(step):
        slot = lax.div(step, PIECES)
        piece = lax.rem(step, PIECES)

        @pl.when(jnp.logical_not(sums) & jnp.logical_not(helped(slot, piece)))
        def _():
            for part in range(2):
                partial_copy(slot, piece, part).wait_send()

        origin = lax.div(slot, 2)

        @pl.when(has_up & (origin <= place))
        def _():
            rows_copy(0, slot, piece, held.at[piece_at(slot, piece)]).wait_send()

        @pl.when(has_down & (origin >= place))
        def _():
            rows_copy(1, slot, piece, held.at[piece_at(slot, piece)]).wait_send()

    @pl.when(sums)
    def _():
        @pl.loop(0, count * PIECES)
        def _(step):
            share_copy(lax.div(step, PIECES), lax.rem(step, PIECES)).wait_send()
            pair_copy(lax.div(step, PIECES), lax.rem(step, PIECES)).wait_send()

        @pl.when(helper)
        def _():
            for which in range(2):
                for copy in gift_copies(which):
                    copy.wait_send()

    @pl.when(jnp.logical_not(sums))
    def _():
        send_above.wait_send()

        @pl.when(helper)
        def _():
            for which in range(2):
                for part in range(2):
                    aid_sum_copy(part, which).wait_send()

    @pl.when(helper)
    def _():
        for which in range(2):
            guest_copy(which).wait_send()
        for turn in range(2):
            part = side + turn - 2 * side * turn
            for which in range(2):
                return_copy(turn, part, which).wait_send()
            for index in range(STRIPS):
                aid_core_copy(turn, part, index).wait_send()

    @pl.when(end)
    def _():
        for turn in range(2):
            part = side + turn - 2 * side * turn
            for index in range(STRIPS):
                aid_copy(turn, part, index).wait_send()

    for block in range(blocks):
        @pl.when(core != block % 2)
        def _():
            grad_copy(block).wait_send()

        @pl.when(core == block % 2)
        def _():
            far_copy(block).wait_send()

            @pl.when(jnp.logical_not(sums))
            def _():
                near_copy(block).wait_send()

    @pl.loop(0, tiles)
    def _(index):
        square_copy(index).wait_send()


PIECES = 2
STRIPS = 4
TILE = 512


def fused(lengths, head_grad, table, hidden, query_weight, key_weight, value_weight):
    count = lax.axis_size("tensor")
    rows, model_width = hidden.shape
    length = rows * count
    half = model_width // 2
    query_cols = query_weight.shape[1]
    head_width = key_weight.shape[1]
    pair_cols = 2 * head_width
    all_cols = 2 * (query_cols + head_width)
    heads = query_cols // head_width
    share = half // 2
    dma = pltpu.SemaphoreType.DMA
    anywhere = pl.BlockSpec(memory_space=pl.ANY)
    here = pl.BlockSpec(memory_space=pltpu.VMEM)
    out = jax.ShapeDtypeStruct((share, head_width), jnp.float32)
    return pl.pallas_call(
        functools.partial(fused_kernel, count),
        out_shape=(out, out),
        in_specs=[pl.BlockSpec(memory_space=pltpu.SMEM)] + [here] * 2 + [anywhere] * 4,
        out_specs=(here, here),
        scratch_shapes=[
            pltpu.VMEM((length, half), jnp.bfloat16),
            pltpu.VMEM((half, all_cols), jnp.bfloat16),
            pltpu.VMEM((length, all_cols), jnp.float32),
            pltpu.VMEM((length, all_cols), jnp.float32),
            pltpu.VMEM((2, count, heads, rows, head_width), jnp.bfloat16),
            pltpu.VMEM((length, pair_cols), jnp.bfloat16),
            pltpu.VMEM((count, heads * rows, head_width), jnp.bfloat16),
            pltpu.VMEM((count, heads * rows, head_width), jnp.bfloat16),
            pltpu.VMEM((count, rows, pair_cols), jnp.float32),
            pltpu.VMEM((count, rows, pair_cols), jnp.float32),
            pltpu.VMEM((length, pair_cols), jnp.bfloat16),
            pltpu.VMEM((length, pair_cols), jnp.bfloat16),
            pltpu.VMEM((share, pair_cols), jnp.float32),
            pltpu.VMEM((share, pair_cols), jnp.float32),
            pltpu.VMEM((half // 2, all_cols), jnp.bfloat16),
            pltpu.VMEM((2, rows // PIECES, half // 2), jnp.bfloat16),
            pltpu.VMEM((2, rows // PIECES, all_cols), jnp.float32),
            pltpu.VMEM((2, rows // PIECES, all_cols), jnp.float32),
            pltpu.VMEM((2, rows // PIECES, all_cols), jnp.float32),
            pltpu.VMEM((2, rows // PIECES, all_cols), jnp.float32),
            pltpu.VMEM((2, 2, heads, rows // PIECES, head_width), jnp.bfloat16),
            pltpu.VMEM((2, rows // PIECES, pair_cols), jnp.bfloat16),
            dma((count, PIECES)), dma((2, count, PIECES)), dma((PIECES,)), dma((4,)),
            dma((STRIPS,)), dma((STRIPS,)), dma((STRIPS,)), dma((STRIPS,)),
            dma((STRIPS,)), dma((STRIPS,)), dma((STRIPS,)), dma((STRIPS,)),
            dma((count, PIECES, 2)), dma((count, PIECES, 2)),
            dma((count, PIECES)), dma((count, PIECES)), dma((count, PIECES)), dma((count, PIECES)),
            dma, dma, dma,
            dma((count,)), dma((count,)), dma((count,)), dma((count,)), dma((count,)),
            dma((share // TILE,)), dma((share // TILE,)),
            dma((2, STRIPS)), dma((2, STRIPS)), dma((2, STRIPS)), dma((2, STRIPS)),
            dma((2,)), dma((2,)), dma((2, 2)), dma((2, 2)), dma((2, 2)), dma((2, 2)),
            dma((2, 3)), dma((2, 3)),
        ],
        compiler_params=pltpu.CompilerParams(
            collective_id=2, has_side_effects=True, vmem_limit_bytes=58 * 2**20),
    )(lengths, head_grad, table, hidden, query_weight, key_weight, value_weight)


def local(hidden, query_weight, key_weight, value_weight, head_grad, lengths):
    head_width = key_weight.shape[2]
    length = head_grad.shape[1]
    table = jnp.asarray(turn_table(length, head_width))
    if lax.axis_size("groups") == 2 and lax.axis_size("dp") == 2 and lax.axis_size("tensor") == 8:
        fisher_key, fisher_value = fused(
            lengths, head_grad[0], table, hidden[0], query_weight, key_weight[0], value_weight[0])
        return (fisher_key[None], fisher_value[None])
    half_rows, queries, pairs, upstream = gather_project(
        lengths, head_grad[0], table, hidden[0], query_weight, key_weight[0], value_weight[0]
    )
    own, peer = attend(
        queries, upstream, pairs.reshape(length, -1), table, half_rows.reshape(length, -1),
        head_width,
    )
    fisher_key = own[:1] + jnp.sum(peer[:, :1], axis=0)
    fisher_value = own[1:] + jnp.sum(peer[:, 1:], axis=0)
    return (fisher_key, fisher_value)


def solution(mesh):
    in_specs = (
        P(("groups", "dp"), "tensor", None),
        P(None, "tensor"),
        P("tensor", None, None),
        P("tensor", None, None),
        P(("groups", "dp"), None, "tensor"),
        P(("groups", "dp")),
    )
    out_specs = (P(("groups", "tensor"), "dp", None), P(("groups", "tensor"), "dp", None))
    return jax.shard_map(local, mesh=mesh, in_specs=in_specs, out_specs=out_specs, check_vma=False)
```
